32 devices in a mesh: dp: 8 (over z, x), shard: 4 (over y, core).
Axes of the slice: x: 2, y: 2, z: 4, core: 2. Of those that a mesh axis runs over, the one named last changes fastest.
Arguments:
- target: bfloat16 [32, 1024, 512], P(('dp', 'shard')), may hold values from -6 to 6
- memory: bfloat16 [32, 1024, 512], P(('dp', 'shard')), may hold values from -6 to 6
- cotangent: bfloat16 [32, 1024, 512], P(('dp', 'shard')), may hold values from -6 to 6
- target_lengths: int32 [32, 24], P(('dp', 'shard')), may hold values from 1 to 512, 1024 in all within a row
- source_lengths: int32 [32, 24], P(('dp', 'shard')), may hold values from 1 to 512, 1024 in all within a row
- inward_master: float32 [1572864], P(('dp', 'shard')), may hold values from -0.25 to 0.25
- inward_mean: float32 [1572864], P(('dp', 'shard')), may hold values from -320 to 320
- inward_square: float32 [1572864], P(('dp', 'shard')), may hold values from 327.68 to 32768
- outward_master: float32 [524288], P(('dp', 'shard')), may hold values from -0.75 to 0.75
- outward_mean: float32 [524288], P(('dp', 'shard')), may hold values from -320 to 320
- outward_square: float32 [524288], P(('dp', 'shard')), may hold values from 327.68 to 32768
- expand_master: float32 [1048576], P(('dp', 'shard')), may hold values from -0.25 to 0.25
- expand_mean: float32 [1048576], P(('dp', 'shard')), may hold values from -320 to 320
- expand_square: float32 [1048576], P(('dp', 'shard')), may hold values from 327.68 to 32768
- shrink_master: float32 [1048576], P(('dp', 'shard')), may hold values from -0.125 to 0.125
- shrink_mean: float32 [1048576], P(('dp', 'shard')), may hold values from -320 to 320
- shrink_square: float32 [1048576], P(('dp', 'shard')), may hold values from 327.68 to 32768
- norms_master: float32 [3072], P(('dp', 'shard')), may hold values from -0.5 to 1.3, as said below
- norms_mean: float32 [3072], P(('dp', 'shard')), may hold values from -320 to 320
- norms_square: float32 [3072], P(('dp', 'shard')), may hold values from 327.68 to 32768
Outputs:
- result: bfloat16 [32, 1024, 512], P(('dp', 'shard'))
- target_grad: float32 [32, 1024, 512], P(('dp', 'shard'))
- memory_grad: float32 [32, 1024, 512], P(('dp', 'shard'))
- change_inward: float32 [1572864], P(('dp', 'shard'))
- mean_inward: float32 [1572864], P(('dp', 'shard'))
- summed_inward: float32 [1572864], P(('dp', 'shard'))
- change_outward: float32 [524288], P(('dp', 'shard'))
- mean_outward: float32 [524288], P(('dp', 'shard'))
- summed_outward: float32 [524288], P(('dp', 'shard'))
- change_expand: float32 [1048576], P(('dp', 'shard'))
- mean_expand: float32 [1048576], P(('dp', 'shard'))
- summed_expand: float32 [1048576], P(('dp', 'shard'))
- change_shrink: float32 [1048576], P(('dp', 'shard'))
- mean_shrink: float32 [1048576], P(('dp', 'shard'))
- summed_shrink: float32 [1048576], P(('dp', 'shard'))
- change_norms: float32 [3072], P(('dp', 'shard'))
- mean_norms: float32 [3072], P(('dp', 'shard'))
- summed_norms: float32 [3072], P(('dp', 'shard'))
The draws below stay inside these ranges and needn't reach their ends.
Inputs may be any that keep to these rules, and one draw needn't show every extreme that they name: `target_lengths`: in each row the 24 lengths sum to 1024; the last entry is padding, the others are sentences; target sentence i is the translation of source sentence i. `source_lengths`: as target_lengths, for the source side. `norms_master`: the first 1536 entries are gains, the others biases.
All inputs are finite; a program needn't handle non-finite values.
Results may differ from the reference program's by a relative error of at most 0.015.
The reference program's roundings to bfloat16 on the way count: a program that leaves them out, or rounds other values in their place, can miss the bound.
Values may be sent and summed in bfloat16 or wider, within the bound.
A program may use at most 192 MiB of HBM per device.

```python
import math
import jax
import jax.numpy as jnp
import numpy as np
from jax import lax

D = 512
HEADS = 8
HD = 64
FF = 2048
ROW = 1024
SEGS = 24
MOST = 512
STEP = 10
ROWS = 32


def draw_norms_master(key, part):
    first_key, second_key = jax.random.split(jax.random.fold_in(key, 7))
    gains = jax.random.uniform(first_key, (3 * D,), jnp.float32, 0.7, 1.3)
    biases = jax.random.uniform(second_key, (3 * D,), jnp.float32, -0.5, 0.5)
    return jnp.concatenate([gains, biases])


def shard_levels(key, dims, pieces, low, largest):
    level = 1.0
    for position, shards_of in pieces:
        heights = jax.random.uniform(jax.random.fold_in(jax.random.fold_in(key, 6), position), (shards_of,), jnp.float32, low / len(pieces), largest / len(pieces))
        level = level * jnp.repeat(jnp.exp(heights), dims[position] // shards_of).reshape((-1,) + (1,) * (len(dims) - 1 - position))
    return level


def length_profile(count, total, reach, skew):
    loads = [(1 << 20) // math.isqrt(grade ** skew) + 1 for grade in range(2, count + 1)]
    rest, counts = total - reach - (count - 1), [1] * (count - 1)
    while rest > 0:
        movable = [i for i in range(count - 1) if counts[i] < reach]
        mass, left = sum([loads[i] for i in movable]), rest
        for i in movable:
            more = min(reach - counts[i], max(1, left * loads[i] // mass), rest)
            counts[i] = counts[i] + more
            rest = rest - more
    return np.array([reach] + counts)


def ragged_sizes(key, number_of, total, limit, skew):
    if number_of == 2:
        one = jax.random.randint(key, (), max(1, total - limit), min(limit, total - 1) + 1)
        return jnp.stack([one, total - one])
    tallies = jnp.asarray(length_profile(number_of, total, limit, skew), jnp.int32)
    pairs = (number_of - 1) // 2
    giver, sink = tallies[1:1 + 2 * pairs:2], tallies[2:2 + 2 * pairs:2]
    margin = jnp.minimum(giver - 1, limit - sink)
    passed = jax.random.randint(jax.random.fold_in(key, 1), (pairs,), 0, 1 << 20) % (margin + 1)
    tallies = tallies.at[1:1 + 2 * pairs:2].set(giver - passed).at[2:2 + 2 * pairs:2].set(sink + passed)
    return tallies[jax.random.permutation(jax.random.fold_in(key, 2), number_of)]


def scatter_about(stream_key, extent, width, most, cuts=(), kind=jnp.bfloat16):
    values = width * jax.random.normal(stream_key, extent, jnp.float32)
    if cuts:
        values = values * shard_levels(stream_key, extent, cuts, -0.22, 0.18)
    return jnp.clip(values, -most, most).astype(kind)


def setup_inputs(seed: int = 0) -> dict:
    arg_keys = jax.random.split(jax.random.key(seed), 21)
    target = scatter_about(arg_keys[0], (ROWS, ROW, D), 1.0, 6.0, ((0, 32),))
    memory = scatter_about(arg_keys[1], (ROWS, ROW, D), 1.0, 6.0, ((0, 32),))
    cotangent = scatter_about(arg_keys[2], (ROWS, ROW, D), 1.0, 6.0, ((0, 32),))
    target_lengths = jax.vmap(lambda own: ragged_sizes(own, SEGS, ROW, MOST, 2))(jax.random.split(arg_keys[3], ROWS)).reshape((ROWS, SEGS)).astype(jnp.int32)
    source_lengths = jax.vmap(lambda own: ragged_sizes(own, SEGS, ROW, MOST, 2))(jax.random.split(arg_keys[4], ROWS)).reshape((ROWS, SEGS)).astype(jnp.int32)
    inward_master = scatter_about(arg_keys[5], (6 * D * D,), D ** -0.5, 0.25, ((0, 32),), jnp.float32)
    inward_mean = scatter_about(arg_keys[6], (6 * D * D,), (0.3 * (ROWS * ROW) ** 0.5), 320.0, ((0, 32),), jnp.float32)
    inward_square = jnp.clip(jnp.exp(math.log(32768.0) - 4.6051702 * jax.random.uniform(arg_keys[7], (6 * D * D,), jnp.float32) ** shard_levels(arg_keys[7], (6 * D * D,), ((0, 32),), -0.2, 0.2)), 327.68, 32768.0)
    outward_master = scatter_about(arg_keys[8], (2 * D * D,), (D // 8) ** -0.5, 0.75, ((0, 32),), jnp.float32)
    outward_mean = scatter_about(arg_keys[9], (2 * D * D,), (0.3 * (ROWS * ROW) ** 0.5), 320.0, ((0, 32),), jnp.float32)
    outward_square = jnp.clip(jnp.exp(math.log(32768.0) - 4.6051702 * jax.random.uniform(arg_keys[10], (2 * D * D,), jnp.float32) ** shard_levels(arg_keys[10], (2 * D * D,), ((0, 32),), -0.2, 0.2)), 327.68, 32768.0)
    expand_master = scatter_about(arg_keys[11], (D * FF,), D ** -0.5, 0.25, ((0, 32),), jnp.float32)
    expand_mean = scatter_about(arg_keys[12], (D * FF,), (0.3 * (ROWS * ROW) ** 0.5), 320.0, ((0, 32),), jnp.float32)
    expand_square = jnp.clip(jnp.exp(math.log(32768.0) - 4.6051702 * jax.random.uniform(arg_keys[13], (D * FF,), jnp.float32) ** shard_levels(arg_keys[13], (D * FF,), ((0, 32),), -0.2, 0.2)), 327.68, 32768.0)
    shrink_master = scatter_about(arg_keys[14], (FF * D,), FF ** -0.5, 0.125, ((0, 32),), jnp.float32)
    shrink_mean = scatter_about(arg_keys[15], (FF * D,), (0.3 * (ROWS * ROW) ** 0.5), 320.0, ((0, 32),), jnp.float32)
    shrink_square = jnp.clip(jnp.exp(math.log(32768.0) - 4.6051702 * jax.random.uniform(arg_keys[16], (FF * D,), jnp.float32) ** shard_levels(arg_keys[16], (FF * D,), ((0, 32),), -0.2, 0.2)), 327.68, 32768.0)
    norms_master = draw_norms_master(jax.random.fold_in(arg_keys[20], 71), 0)
    norms_mean = scatter_about(arg_keys[18], (6 * D,), (0.3 * (ROWS * ROW) ** 0.5), 320.0, ((0, 32),), jnp.float32)
    norms_square = jnp.clip(jnp.exp(math.log(32768.0) - 4.6051702 * jax.random.uniform(arg_keys[19], (6 * D,), jnp.float32) ** shard_levels(arg_keys[19], (6 * D,), ((0, 32),), -0.2, 0.2)), 327.68, 32768.0)
    return {"target": target, "memory": memory, "cotangent": cotangent, "target_lengths": target_lengths, "source_lengths": source_lengths, "inward_master": inward_master, "inward_mean": inward_mean, "inward_square": inward_square, "outward_master": outward_master, "outward_mean": outward_mean, "outward_square": outward_square, "expand_master": expand_master, "expand_mean": expand_mean, "expand_square": expand_square, "shrink_master": shrink_master, "shrink_mean": shrink_mean, "shrink_square": shrink_square, "norms_master": norms_master, "norms_mean": norms_mean, "norms_square": norms_square}


learn_rate = 0.001
beta_one = 0.9
beta_two = 0.999

@jax.custom_vjp
def low(v):
    return lax.optimization_barrier(v.astype(jnp.bfloat16)).astype(jnp.float32)

@jax.custom_vjp
def low_back(v):
    return v

def low_keep(v):
    return (low(v), None)

def low_pass(kept, grad):
    return (grad,)

def back_keep(v):
    return (v, None)

def back_low(kept, grad):
    return (low(grad),)
low.defvjp(low_keep, low_pass)
low_back.defvjp(back_keep, back_low)

def matmul_high(left_mat, right_mat):
    return jnp.dot(left_mat, right_mat, precision=lax.Precision.HIGHEST)

def layer_norm(residual, norm_gain, norm_bias):
    centered = residual - lax.optimization_barrier(jnp.mean(residual, -1, keepdims=True))
    spread = lax.optimization_barrier(jnp.mean(centered * centered, -1, keepdims=True))
    return centered * lax.rsqrt(spread + 1e-05) * norm_gain + norm_bias

def segments(lengths):
    ends = jnp.cumsum(lengths).astype(jnp.int32)
    places = jnp.arange(ROW, dtype=jnp.int32)
    return lax.optimization_barrier(jnp.sum((places[:, None] >= ends[None, :]).astype(jnp.int32), -1))

def attention(queries, keys, values, query_seg, key_seg, causal):
    length = queries.shape[0]
    block_rows = min(512, length)
    q_heads = queries.reshape(length, HEADS, HD)
    k_heads = keys.reshape(length, HEADS, HD)
    v_heads = values.reshape(length, HEADS, HD)
    key_pos = jnp.arange(length, dtype=jnp.int32)

    def one_block(block_index):
        row_start = block_index * block_rows
        q_block = lax.dynamic_slice_in_dim(q_heads, row_start, block_rows, 0)
        seg_block = lax.dynamic_slice_in_dim(query_seg, row_start, block_rows, 0)
        query_pos = row_start + jnp.arange(block_rows, dtype=jnp.int32)
        raw = jnp.einsum('qhd,khd->hqk', q_block, k_heads, precision=lax.Precision.HIGHEST)
        scores = low_back(raw) * HD ** (-0.5)
        allowed = seg_block[:, None] == key_seg[None, :]
        if causal:
            allowed = allowed & (key_pos[None, :] <= query_pos[:, None])
        scores = jnp.where(allowed[None], scores, -1000000000.0)
        probs = jax.nn.softmax(scores, -1)
        context = jnp.einsum('hqk,khd->qhd', low(probs), v_heads, precision=lax.Precision.HIGHEST)
        return context.reshape(block_rows, HEADS * HD)
    blocks = lax.map(jax.checkpoint(one_block), jnp.arange(length // block_rows, dtype=jnp.int32))
    return blocks.reshape(length, HEADS * HD)

def project(inputs, weight):
    return low_back(low(matmul_high(inputs, weight)))

def layer(tokens, source, inward, outward, expand, shrink, norms, target_seg, source_seg):
    w_in = inward.reshape(6, D, D)
    w_out = outward.reshape(2, D, D)
    w_up = expand.reshape(D, FF)
    w_down = shrink.reshape(FF, D)
    norm_par = norms.reshape(2, 3, D)
    query_one = project(tokens, w_in[0])
    key_one = project(tokens, w_in[1])
    value_one = project(tokens, w_in[2])
    ctx_one = low_back(low(attention(query_one, key_one, value_one, target_seg, target_seg, True)))
    resid_one = tokens + low_back(matmul_high(ctx_one, w_out[0]))
    hidden_one = layer_norm(resid_one, norm_par[0, 0], norm_par[1, 0])
    hidden_low = low(hidden_one)
    query_two = project(hidden_low, w_in[3])
    key_two = project(source, w_in[4])
    value_two = project(source, w_in[5])
    ctx_two = low_back(low(attention(query_two, key_two, value_two, target_seg, source_seg, False)))
    resid_two = hidden_one + low_back(matmul_high(ctx_two, w_out[1]))
    hidden_two = layer_norm(resid_two, norm_par[0, 1], norm_par[1, 1])
    second_low = low(hidden_two)
    activated = low(jax.nn.silu(low_back(matmul_high(second_low, w_up))))
    resid_three = hidden_two + low_back(matmul_high(activated, w_down))
    return layer_norm(resid_three, norm_par[0, 2], norm_par[1, 2])

def adam_step(mean_old, square_old, grad_sum):
    mean_new = beta_one * mean_old + (1.0 - beta_one) * grad_sum
    square_new = beta_two * square_old + (1.0 - beta_two) * grad_sum * grad_sum
    steps_float = float(STEP)
    mean_hat = mean_new / (1.0 - beta_one ** steps_float)
    square_hat = square_new / (1.0 - beta_two ** steps_float)
    change = -learn_rate * mean_hat / (jnp.sqrt(square_hat) + 1e-08)
    return (change, mean_new, grad_sum)

def reference(target, memory, cotangent, target_lengths, source_lengths, inward_master, inward_mean, inward_square, outward_master, outward_mean, outward_square, expand_master, expand_mean, expand_square, shrink_master, shrink_mean, shrink_square, norms_master, norms_mean, norms_square):
    masters = (inward_master, outward_master, expand_master, shrink_master, norms_master)
    lowered = tuple((lax.optimization_barrier(weight.astype(jnp.bfloat16)).astype(jnp.float32) for weight in masters))

    def row_step(totals, row_items):
        tokens_row, source_row, seed_row, target_len, source_len = row_items
        target_seg = segments(target_len)
        source_seg = segments(source_len)

        def run(tokens, source, inward, outward, expand, shrink, norms):
            return layer(tokens, source, inward, outward, expand, shrink, norms, target_seg, source_seg)
        output, pull = jax.vjp(run, tokens_row.astype(jnp.float32), source_row.astype(jnp.float32), *lowered)
        live_rows = (target_seg < SEGS - 1).astype(jnp.float32)
        grads = pull(seed_row.astype(jnp.float32) * live_rows[:, None])
        totals = tuple((total + grad for total, grad in zip(totals, grads[2:])))
        return (totals, (output.astype(jnp.bfloat16), grads[0], grads[1]))
    zeros = tuple((jnp.zeros_like(weight) for weight in lowered))
    totals, outputs = lax.scan(row_step, zeros, (target, memory, cotangent, target_lengths, source_lengths))
    result, target_grad, memory_grad = outputs
    in_c, in_m, in_g = adam_step(inward_mean, inward_square, totals[0])
    out_c, out_m, out_g = adam_step(outward_mean, outward_square, totals[1])
    up_c, up_m, up_g = adam_step(expand_mean, expand_square, totals[2])
    down_c, down_m, down_g = adam_step(shrink_mean, shrink_square, totals[3])
    norm_c, norm_m, norm_g = adam_step(norms_mean, norms_square, totals[4])
    return (result, target_grad, memory_grad, in_c, in_m, in_g, out_c, out_m, out_g, up_c, up_m, up_g, down_c, down_m, down_g, norm_c, norm_m, norm_g)
```

```python
import functools
import jax
import jax.numpy as jnp
from jax import lax
from jax.experimental import pallas as pl
from jax.experimental.pallas import tpu as pltpu
from jax.sharding import PartitionSpec as P

MESH = pl.DeviceIdType.MESH
BF = jnp.bfloat16
F32 = jnp.float32
learn_rate = 0.001
beta_one = 0.9
beta_two = 0.999
STEP = 10


class Place:
    def __init__(self, sizes):
        self.sizes = sizes
        dp, sh = lax.axis_index("dp"), lax.axis_index("shard")
        self.at = (dp // sizes[1], dp % sizes[1], sh // sizes[3], sh % sizes[3])

    def device(self, axis, coord):
        a, b, c, e = [coord if i == axis else v for i, v in enumerate(self.at)]
        return (a * self.sizes[1] + b, c * self.sizes[3] + e)

    def greet(self):
        barrier = pltpu.get_barrier_semaphore()
        count = 0
        for axis in range(4):
            n, me = self.sizes[axis], self.at[axis]
            if n == 2:
                pl.semaphore_signal(barrier, inc=1, device_id=self.device(axis, 1 - me), device_id_type=MESH)
                count = count + 1
            else:
                for step in (-1, 1):
                    there = me + step
                    ok = (there >= 0) & (there < n)

                    @pl.when(ok)
                    def _():
                        pl.semaphore_signal(barrier, inc=1, device_id=self.device(axis, there), device_id_type=MESH)

                    count = count + ok.astype(jnp.int32)
        pl.semaphore_wait(barrier, count)


class Sems:
    def __init__(self, send, recv):
        self.send, self.recv, self.used = send, recv, 0

    def take(self):
        k = self.used
        self.used += 1
        return self.send.at[k], self.recv.at[k]


def gather_sems(order, sizes):
    return 1 + sum(2 if sizes[x] == 2 else 4 * (sizes[x] - 1) for x in order)


def gather_rounds(place, ref, order, sems):
    sizes = place.sizes
    after = []
    held = []

    def group(axis=None, coord=None):
        idx = [slice(None) if i in held else place.at[i] for i in range(4)]
        if axis is not None:
            idx[axis] = coord
        return ref.at[tuple(idx)]

    def copy(block, axis, coord, pair):
        return pltpu.make_async_remote_copy(
            src_ref=block, dst_ref=block, send_sem=pair[0], recv_sem=pair[1],
            device_id=place.device(axis, coord), device_id_type=MESH)

    def to_sibling(axis, coord, cond):
        pair = sems.take()
        idx = [slice(None) if i in held else place.at[i] for i in range(4)]
        if axis is not None:
            idx[axis] = coord
        mine = ref.at[tuple(idx)]
        idx[3] = 1 - place.at[3]
        theirs = ref.at[tuple(idx)]
        e = place.at[3]
        go = copy(mine, 3, 1 - e, pair)
        come = copy(theirs, 3, 1 - e, pair)

        def run(f):
            if cond is None:
                f()
            else:
                pl.when(cond)(f)

        run(go.start)

        def finish():
            go.wait_send()
            come.wait_recv()

        after.append(lambda: run(finish))

    to_sibling(None, None, None)
    for axis in order:
        n, me = sizes[axis], place.at[axis]
        if n == 2:
            pair = sems.take()
            go = copy(group(), axis, 1 - me, pair)
            come = copy(group(axis, 1 - me), axis, 1 - me, pair)
            go.start()
            after.append(go.wait_send)
            yield
            come.wait_recv()
            to_sibling(axis, 1 - me, None)
        else:
            for t in range(1, n):
                pending = []
                for step in (1, -1):
                    pair = sems.take()
                    out_c, in_c, to = me - step * (t - 1), me - step * t, me + step
                    can = (out_c >= 0) & (out_c < n) & (to >= 0) & (to < n)
                    gets = (in_c >= 0) & (in_c < n)
                    go = copy(group(axis, out_c), axis, to, pair)
                    come = copy(group(axis, in_c), axis, to, pair)
                    pl.when(can)(go.start)
                    after.append(lambda go=go, can=can: pl.when(can)(go.wait_send))
                    pending.append((come, gets, in_c))
                yield
                for come, gets, in_c in pending:
                    pl.when(gets)(come.wait_recv)
                    to_sibling(axis, in_c, gets)
        held.append(axis)
    yield
    for f in after:
        f()


def interleave(rounds):
    live = list(rounds)
    while live:
        still = []
        for r in live:
            try:
                next(r)
                still.append(r)
            except StopIteration:
                pass
        live = still


def flat_to_rows(src, dst, rows, cols):
    w = cols // 128
    for j in range(w):
        dst[:, j * 128:(j + 1) * 128] = src[pl.ds(j, rows, stride=w), :].astype(dst.dtype)


def rows_to_flat(value, dst, rows, cols):
    w = cols // 128
    for j in range(w):
        dst[pl.ds(j, rows, stride=w), :] = value[:, j * 128:(j + 1) * 128]


ORDERS = ((0, 2, 1), (0, 1, 2), (1, 2, 0), (0, 1, 2), (0, 1, 2))


def gather_kernel(sizes, shapes, *refs):
    n = len(shapes)
    masters, outs = refs[:n], refs[n:2 * n]
    stage, local, send, recv = refs[2 * n:3 * n], refs[3 * n], refs[3 * n + 1], refs[3 * n + 2]
    place = Place(sizes)
    copies = []
    for k, (rows, cols) in enumerate(shapes):
        if rows == 1:
            stage[k][...] = masters[k][...].astype(BF).astype(stage[k].dtype)
        else:
            flat_to_rows(masters[k], stage[k], rows, cols)
        cp = pltpu.make_async_copy(stage[k], outs[k].at[place.at], local.at[k])
        cp.start()
        copies.append(cp)
    place.greet()
    for cp in copies:
        cp.wait()
    sems = Sems(send, recv)
    interleave([gather_rounds(place, outs[k], ORDERS[k], sems) for k in range(n)])


def gather_all(mesh_sizes, masters, shapes, dtypes):
    n = len(shapes)
    total = sum(gather_sems(ORDERS[k], mesh_sizes) for k in range(n))
    vm = pl.BlockSpec(memory_space=pltpu.VMEM)
    return pl.pallas_call(
        functools.partial(gather_kernel, mesh_sizes, shapes),
        out_shape=[jax.ShapeDtypeStruct((*mesh_sizes, *s), d) for s, d in zip(shapes, dtypes)],
        in_specs=[vm] * n,
        out_specs=[pl.BlockSpec(memory_space=pl.ANY)] * n,
        scratch_shapes=[pltpu.VMEM(s, d) for s, d in zip(shapes, dtypes)]
        + [pltpu.SemaphoreType.DMA((n,)), pltpu.SemaphoreType.DMA((total,)), pltpu.SemaphoreType.DMA((total,))],
        compiler_params=pltpu.CompilerParams(collective_id=0, has_side_effects=True, vmem_limit_bytes=48 << 20),
        name="gather_weights",
    )(*masters)


def reduce_sems(order, sizes):
    return 1 + sum(1 if sizes[x] == 2 else 2 * (sizes[x] - 1) for x in order)


def reduce_rounds(place, grad, order, got, bufs, total, sems):
    sizes = place.sizes
    after = []
    e = place.at[3]

    def rdma(src, dst, axis, coord, pair):
        return pltpu.make_async_remote_copy(
            src_ref=src, dst_ref=dst, send_sem=pair[0], recv_sem=pair[1],
            device_id=place.device(axis, coord), device_id_type=MESH)

    def add_into(dst, src):
        dst[...] = (dst[...].astype(F32) + src[...].astype(F32)).astype(dst.dtype)

    def each(dims, f):
        count = 1
        for d in dims:
            count *= d
        if count == 1:
            f(tuple(0 for _ in dims))
            return

        def step(i, _):
            idx = []
            for d in reversed(dims):
                idx.append(i % d)
                i = i // d
            f(tuple(reversed(idx)))
            return 0

        lax.fori_loop(0, count, step, 0)

    cp = rdma(grad.at[:, :, :, 1 - e], got, 3, 1 - e, sems.take())
    cp.start()
    yield
    cp.wait()
    each(sizes[:3], lambda i: add_into(got.at[i], grad.at[(*i, e)]))
    cur, left = got, [0, 1, 2]
    for axis, buf in zip(order, bufs):
        n, me = sizes[axis], place.at[axis]
        pos = left.index(axis)
        rest = [x for x in left if x != axis]
        dims = [sizes[x] for x in rest]

        def part(ref, coord):
            return ref.at[tuple(coord if i == pos else slice(None) for i in range(len(left)))]

        def one(ref, coord, i):
            i = list(i)
            i.insert(pos, coord)
            return ref.at[tuple(i)]

        last = not rest
        if n == 2:
            cp = rdma(part(cur, 1 - me), buf, axis, 1 - me, sems.take())
            cp.start()
            yield
            cp.wait()
            if last:
                total[...] = buf[...].astype(F32) + cur[me].astype(F32)
            else:
                each(dims, lambda i: add_into(buf.at[i], one(cur, me, i)))
        else:
            for t in range(n - 1):
                for way, step in enumerate((1, -1)):
                    j = n - 1 - t if step == 1 else t
                    to, back = me + step, me - step
                    ahead = (j > me) if step == 1 else (j < me)
                    gets = ahead & (back >= 0) & (back < n)
                    pair = sems.take()
                    come = rdma(part(cur, j), buf.at[way, j], axis, to, pair)

                    @pl.when(gets)
                    def _():
                        come.wait_recv()
                        each(dims, lambda i: add_into(one(cur, j, i), buf.at[(way, j, *i)]))

                    pl.when(ahead)(come.start)
                    after.append(lambda come=come, ahead=ahead: pl.when(ahead)(come.wait_send))
                    ends = (j == me) & (back >= 0) & (back < n)
                    after.append(lambda come=come, ends=ends: pl.when(ends)(come.wait_recv))
                yield
            for f in after:
                f()
            after = []
            keep = buf.at[0, me]

            def close(i):
                mine = one(cur, me, i)[...].astype(F32)
                v = mine + jnp.where(me > 0, buf[(0, me, *i)].astype(F32), 0.0)
                v = v + jnp.where(me < n - 1, buf[(1, me, *i)].astype(F32), 0.0)
                if last:
                    total[...] = v
                else:
                    buf[(0, me, *i)] = v.astype(buf.dtype)

            each(dims, close)
            buf = keep
        cur, left = buf, rest
    for f in after:
        f()


def reduce_bufs(order, sizes, shape):
    left, out = [0, 1, 2], [(*sizes[:3], *shape)]
    for axis in order:
        rest = [x for x in left if x != axis]
        dims = tuple(sizes[x] for x in rest)
        out.append((*dims, *shape) if sizes[axis] == 2 else (2, sizes[axis], *dims, *shape))
        left = rest
    return out


BACK = tuple(tuple(reversed(o)) for o in ORDERS)


def adam(mean_old, square_old, grad):
    mean_new = beta_one * mean_old + (1.0 - beta_one) * grad
    square_new = beta_two * square_old + (1.0 - beta_two) * grad * grad
    steps = float(STEP)
    mean_hat = mean_new / (1.0 - beta_one**steps)
    square_hat = square_new / (1.0 - beta_two**steps)
    return -learn_rate * mean_hat / (jnp.sqrt(square_hat) + 1e-08), mean_new


def reduce_kernel(sizes, shapes, counts, *refs):
    n = len(shapes)
    refs = list(refs)

    def take(k):
        out = refs[:k]
        del refs[:k]
        return out

    grads, means, squares = take(n), take(n), take(n)
    outs = take(3 * n)
    totals = take(n)
    bufs = [take(c) for c in counts]
    send, recv = take(2)
    place = Place(sizes)
    place.greet()
    sems = Sems(send, recv)
    interleave([reduce_rounds(place, grads[k], BACK[k], bufs[k][0], bufs[k][1:], totals[k], sems) for k in range(n)])
    for k, (rows, cols) in enumerate(shapes):
        change, mean, summed = outs[3 * k:3 * k + 3]
        if rows == 1:
            summed[...] = totals[k][...]
        else:
            rows_to_flat(totals[k], summed, rows, cols)
        change[...], mean[...] = adam(means[k][...], squares[k][...], summed[...])


def reduce_all(mesh_sizes, grads, means, squares, shapes):
    n = len(shapes)
    flat = [((s[0] * s[1]) // 128, 128) for s in shapes]
    lists = [reduce_bufs(BACK[k], mesh_sizes, shapes[k]) for k in range(n)]
    total = sum(reduce_sems(BACK[k], mesh_sizes) for k in range(n))
    vm = pl.BlockSpec(memory_space=pltpu.VMEM)
    scratch = [pltpu.VMEM(s, F32) for s in shapes]
    for k in range(n):
        scratch += [pltpu.VMEM(s, grads[k].dtype) for s in lists[k]]
    scratch += [pltpu.SemaphoreType.DMA((total,)), pltpu.SemaphoreType.DMA((total,))]
    return pl.pallas_call(
        functools.partial(reduce_kernel, mesh_sizes, shapes, [len(x) for x in lists]),
        out_shape=[jax.ShapeDtypeStruct(f, F32) for f in flat for _ in range(3)],
        in_specs=[vm] * (3 * n),
        out_specs=[vm] * (3 * n),
        scratch_shapes=scratch,
        compiler_params=pltpu.CompilerParams(collective_id=1, has_side_effects=True, vmem_limit_bytes=60 << 20),
        name="reduce_gradients",
    )(*grads, *means, *squares)


D = 512
HEADS = 8
HD = 64
FF = 2048
ROW = 1024
SEGS = 24
STEP = 10


def matmul(left_mat, right_mat):
    return jnp.dot(left_mat, right_mat, preferred_element_type=jnp.float32)


def left_dot(left_mat, right_mat):
    return lax.dot_general(
        left_mat, right_mat, (((0,), (0,)), ((), ())), preferred_element_type=jnp.float32
    )


def right_dot(left_mat, right_mat):
    return lax.dot_general(
        left_mat, right_mat, (((1,), (1,)), ((), ())), preferred_element_type=jnp.float32
    )


def layer_norm(residual, norm_gain, norm_bias):
    centered = residual - jnp.mean(residual, -1, keepdims=True)
    spread = jnp.mean(centered * centered, -1, keepdims=True)
    return centered * lax.rsqrt(spread + 1e-05) * norm_gain + norm_bias


def segments(lengths):
    upto = jnp.arange(SEGS)[:, None] <= jnp.arange(SEGS)[None, :]
    ends = jnp.sum(jnp.where(upto[None], lengths[:, :, None], 0), 1)
    places = jnp.arange(ROW, dtype=jnp.int32)
    return jnp.sum((places[None, :, None] >= ends[:, None, :]).astype(jnp.int32), -1)


def pair_mask(query_seg, key_seg, row_start, causal):
    allowed = query_seg[:, None] == key_seg[None, :]
    if causal:
        query_pos = row_start + jnp.arange(query_seg.shape[0], dtype=jnp.int32)
        key_pos = jnp.arange(key_seg.shape[0], dtype=jnp.int32)
        allowed = allowed & (key_pos[None, :] <= query_pos[:, None])
    return allowed


def attend(queries, keys, values, query_seg, key_seg, causal):
    block_rows = min(512, queries.shape[1])
    block_count = queries.shape[1] // block_rows
    score_scale = queries.shape[3] ** (-0.5)

    def one_row(row_items):
        q_row, k_row, v_row, qs_row, ks_row = row_items

        def one_block(block_index):
            row_start = block_index * block_rows
            q_block = lax.dynamic_slice_in_dim(q_row, row_start, block_rows, 0)
            seg_block = lax.dynamic_slice_in_dim(qs_row, row_start, block_rows, 0)
            scores = (
                jnp.einsum("qhd,khd->hqk", q_block, k_row, preferred_element_type=jnp.float32)
                * score_scale
            )
            allowed = pair_mask(seg_block, ks_row, row_start, causal)
            scores = jnp.where(allowed[None], scores, -1000000000.0)
            row_peak = jnp.max(scores, -1, keepdims=True)
            raised = jnp.exp(scores - row_peak)
            row_total = jnp.sum(raised, -1, keepdims=True)
            probs = (raised / row_total).astype(jnp.bfloat16)
            context = jnp.einsum("hqk,khd->qhd", probs, v_row, preferred_element_type=jnp.float32)
            return (context, row_peak[..., 0] + jnp.log(row_total[..., 0]))

        context, logsum = lax.map(one_block, jnp.arange(block_count, dtype=jnp.int32))
        return (context.reshape(-1, q_row.shape[1] * q_row.shape[2]), logsum)

    return lax.map(one_row, (queries, keys, values, query_seg, key_seg))


def attend_back(queries, keys, values, logsum, grad_ctx, query_seg, key_seg, causal):
    block_rows = min(512, queries.shape[1])
    block_count = queries.shape[1] // block_rows
    score_scale = queries.shape[3] ** (-0.5)

    def one_row(row_items):
        q_row, k_row, v_row, ls_row, g_row, qs_row, ks_row = row_items

        def one_block(carry, block_index):
            grad_keys, grad_values = carry
            row_start = block_index * block_rows
            q_block = lax.dynamic_slice_in_dim(q_row, row_start, block_rows, 0)
            g_block = lax.dynamic_slice_in_dim(g_row, row_start, block_rows, 0)
            seg_block = lax.dynamic_slice_in_dim(qs_row, row_start, block_rows, 0)
            ls_block = lax.dynamic_index_in_dim(ls_row, block_index, 0, keepdims=False)
            scores = (
                jnp.einsum("qhd,khd->hqk", q_block, k_row, preferred_element_type=jnp.float32)
                * score_scale
            )
            allowed = pair_mask(seg_block, ks_row, row_start, causal)
            probs = jnp.where(allowed[None], jnp.exp(scores - ls_block[..., None]), 0.0)
            grad_probs = jnp.einsum(
                "qhd,khd->hqk", g_block, v_row, preferred_element_type=jnp.float32
            )
            inner = jnp.sum(probs * grad_probs, -1, keepdims=True)
            grad_scores = (probs * (grad_probs - inner) * score_scale).astype(jnp.bfloat16)
            grad_query = jnp.einsum(
                "hqk,khd->qhd", grad_scores, k_row, preferred_element_type=jnp.float32
            )
            grad_keys = grad_keys + jnp.einsum(
                "hqk,qhd->khd", grad_scores, q_block, preferred_element_type=jnp.float32
            )
            grad_values = grad_values + jnp.einsum(
                "hqk,qhd->khd",
                probs.astype(jnp.bfloat16),
                g_block,
                preferred_element_type=jnp.float32,
            )
            return ((grad_keys, grad_values), grad_query)

        empty = jnp.zeros(k_row.shape, jnp.float32)
        (grad_keys, grad_values), grad_query = lax.scan(
            one_block, (empty, empty), jnp.arange(block_count, dtype=jnp.int32)
        )
        return (grad_query.reshape(q_row.shape), grad_keys, grad_values)

    return lax.map(one_row, (queries, keys, values, logsum, grad_ctx, query_seg, key_seg))


def unpack(inward_all, outward_all, norms_all, expand_all, shrink_all):
    norm_par = norms_all.reshape(2, 3, D).astype(jnp.float32)
    return (
        inward_all.reshape(6, D, D),
        outward_all.reshape(2, D, D),
        expand_all.reshape(D, FF),
        shrink_all.reshape(FF, D),
        norm_par[0],
        norm_par[1],
    )


def shard_views(inward, outward, expand, shrink, norms):
    arrays, shapes = [], []
    for x, wide in ((inward, D), (outward, D), (expand, FF), (shrink, D)):
        cols = wide if x.shape[0] >= 16 * wide else D
        arrays.append(x.reshape(-1, 128))
        shapes.append((x.shape[0] // cols, cols))
    width = -(-norms.shape[0] // 128) * 128
    arrays.append(jnp.pad(norms, (0, width - norms.shape[0])).reshape(1, width))
    shapes.append((1, width))
    return arrays, tuple(shapes)


def body(
    sizes,
    target,
    memory,
    cotangent,
    target_lengths,
    source_lengths,
    inward_master,
    inward_mean,
    inward_square,
    outward_master,
    outward_mean,
    outward_square,
    expand_master,
    expand_mean,
    expand_square,
    shrink_master,
    shrink_mean,
    shrink_square,
    norms_master,
    norms_mean,
    norms_square,
):
    row_count = target.shape[0]
    flat, shapes = shard_views(
        inward_master, outward_master, expand_master, shrink_master, norms_master
    )
    inward_all, outward_all, expand_all, shrink_all, norms_all = gather_all(
        sizes, flat, shapes, [BF, BF, BF, BF, F32]
    )
    norm_count = norms_master.shape[0]
    norms_all = norms_all.reshape(-1, norms_all.shape[-1])[:, :norm_count]
    w_in, w_out, w_up, w_down, gains, biases = unpack(
        inward_all, outward_all, norms_all, expand_all, shrink_all
    )
    target_seg = segments(target_lengths)
    source_seg = segments(source_lengths)
    live_rows = (target_seg < SEGS - 1).astype(jnp.float32).reshape(-1, 1)

    def heads(values_flat):
        return values_flat.reshape(row_count, ROW, HEADS, HD)

    tokens = target.reshape(-1, D)
    source = memory.reshape(-1, D)
    query_one = matmul(tokens, w_in[0]).astype(jnp.bfloat16)
    key_one = matmul(tokens, w_in[1]).astype(jnp.bfloat16)
    value_one = matmul(tokens, w_in[2]).astype(jnp.bfloat16)
    ctx_raw, logsum_one = attend(
        heads(query_one), heads(key_one), heads(value_one), target_seg, target_seg, True
    )
    ctx_one = ctx_raw.reshape(-1, D).astype(jnp.bfloat16)
    resid_one = tokens.astype(jnp.float32) + matmul(ctx_one, w_out[0])
    hidden_one = layer_norm(resid_one, gains[0], biases[0])
    hidden_low = hidden_one.astype(jnp.bfloat16)
    query_two = matmul(hidden_low, w_in[3]).astype(jnp.bfloat16)
    key_two = matmul(source, w_in[4]).astype(jnp.bfloat16)
    value_two = matmul(source, w_in[5]).astype(jnp.bfloat16)
    ctx_raw, logsum_two = attend(
        heads(query_two), heads(key_two), heads(value_two), target_seg, source_seg, False
    )
    ctx_two = ctx_raw.reshape(-1, D).astype(jnp.bfloat16)
    resid_two = hidden_one + matmul(ctx_two, w_out[1])
    hidden_two = layer_norm(resid_two, gains[1], biases[1])
    second_low = hidden_two.astype(jnp.bfloat16)
    pre_act = matmul(second_low, w_up)
    activated = jax.nn.silu(pre_act).astype(jnp.bfloat16)
    resid_three = hidden_two + matmul(activated, w_down)
    output = layer_norm(resid_three, gains[2], biases[2])
    seed = cotangent.reshape(-1, D).astype(jnp.float32) * live_rows
    _, pull_three = jax.vjp(layer_norm, resid_three, gains[2], biases[2])
    grad_three, gain_three, bias_three = pull_three(seed)
    grad_out = grad_three.astype(jnp.bfloat16)
    grad_shrink = left_dot(activated, grad_out)
    grad_act = right_dot(grad_out, w_down)
    _, pull_act = jax.vjp(jax.nn.silu, pre_act)
    grad_pre = pull_act(grad_act)[0].astype(jnp.bfloat16)
    grad_expand = left_dot(second_low, grad_pre)
    grad_hidden_two = grad_three + right_dot(grad_pre, w_up)
    _, pull_two = jax.vjp(layer_norm, resid_two, gains[1], biases[1])
    grad_two, gain_two, bias_two = pull_two(grad_hidden_two)
    branch_two = grad_two.astype(jnp.bfloat16)
    grad_wo_two = left_dot(ctx_two, branch_two)
    grad_ctx_two = right_dot(branch_two, w_out[1]).astype(jnp.bfloat16)
    dq_two, dk_two, dv_two = attend_back(
        heads(query_two),
        heads(key_two),
        heads(value_two),
        logsum_two,
        heads(grad_ctx_two),
        target_seg,
        source_seg,
        False,
    )
    dq_two = dq_two.reshape(-1, D).astype(jnp.bfloat16)
    dk_two = dk_two.reshape(-1, D).astype(jnp.bfloat16)
    dv_two = dv_two.reshape(-1, D).astype(jnp.bfloat16)
    grad_wq_two = left_dot(hidden_low, dq_two)
    grad_wk_two = left_dot(source, dk_two)
    grad_wv_two = left_dot(source, dv_two)
    memory_grad = right_dot(dk_two, w_in[4]) + right_dot(dv_two, w_in[5])
    grad_hidden_one = grad_two + right_dot(dq_two, w_in[3])
    _, pull_one = jax.vjp(layer_norm, resid_one, gains[0], biases[0])
    grad_one, gain_one, bias_one = pull_one(grad_hidden_one)
    branch_one = grad_one.astype(jnp.bfloat16)
    grad_wo_one = left_dot(ctx_one, branch_one)
    grad_ctx_one = right_dot(branch_one, w_out[0]).astype(jnp.bfloat16)
    dq_one, dk_one, dv_one = attend_back(
        heads(query_one),
        heads(key_one),
        heads(value_one),
        logsum_one,
        heads(grad_ctx_one),
        target_seg,
        target_seg,
        True,
    )
    dq_one = dq_one.reshape(-1, D).astype(jnp.bfloat16)
    dk_one = dk_one.reshape(-1, D).astype(jnp.bfloat16)
    dv_one = dv_one.reshape(-1, D).astype(jnp.bfloat16)
    grad_wq_one = left_dot(tokens, dq_one)
    grad_wk_one = left_dot(tokens, dk_one)
    grad_wv_one = left_dot(tokens, dv_one)
    target_grad = (
        grad_one
        + right_dot(dq_one, w_in[0])
        + right_dot(dk_one, w_in[1])
        + right_dot(dv_one, w_in[2])
    )
    grad_inward = jnp.stack(
        [grad_wq_one, grad_wk_one, grad_wv_one, grad_wq_two, grad_wk_two, grad_wv_two]
    ).reshape(-1)
    grad_outward = jnp.stack([grad_wo_one, grad_wo_two]).reshape(-1)
    grad_norms = jnp.stack(
        [jnp.stack([gain_one, gain_two, gain_three]), jnp.stack([bias_one, bias_two, bias_three])]
    ).reshape(-1)
    norm_pad = shapes[4][1] - norm_count
    grad_norms = jnp.pad(grad_norms.reshape(-1, norm_count), ((0, 0), (0, norm_pad)))
    grads = [
        g.astype(d).reshape(*sizes, *s)
        for g, s, d in zip(
            (grad_inward, grad_outward, grad_expand, grad_shrink, grad_norms),
            shapes,
            (BF, BF, BF, BF, F32),
        )
    ]
    means, _ = shard_views(inward_mean, outward_mean, expand_mean, shrink_mean, norms_mean)
    squares, _ = shard_views(
        inward_square, outward_square, expand_square, shrink_square, norms_square
    )
    outs = [x.reshape(-1) for x in reduce_all(sizes, grads, means, squares, shapes)]
    in_c, in_m, in_g, out_c, out_m, out_g, up_c, up_m, up_g, down_c, down_m, down_g = outs[:12]
    norm_c, norm_m, norm_g = [x[:norm_count] for x in outs[12:]]
    shape_rows = (row_count, ROW, D)
    return (
        output.astype(jnp.bfloat16).reshape(shape_rows),
        target_grad.reshape(shape_rows),
        memory_grad.reshape(shape_rows),
        in_c,
        in_m,
        in_g,
        out_c,
        out_m,
        out_g,
        up_c,
        up_m,
        up_g,
        down_c,
        down_m,
        down_g,
        norm_c,
        norm_m,
        norm_g,
    )


def solution(mesh):
    rows, cols = mesh.shape["dp"], mesh.shape["shard"]
    return jax.shard_map(
        functools.partial(body, (rows // 2, 2, cols // 2, 2)),
        mesh=mesh,
        in_specs=(
            P(("dp", "shard"), None, None),
            P(("dp", "shard"), None, None),
            P(("dp", "shard"), None, None),
            P(("dp", "shard"), None),
            P(("dp", "shard"), None),
            P(("dp", "shard")),
            P(("dp", "shard")),
            P(("dp", "shard")),
            P(("dp", "shard")),
            P(("dp", "shard")),
            P(("dp", "shard")),
            P(("dp", "shard")),
            P(("dp", "shard")),
            P(("dp", "shard")),
            P(("dp", "shard")),
            P(("dp", "shard")),
            P(("dp", "shard")),
            P(("dp", "shard")),
            P(("dp", "shard")),
            P(("dp", "shard")),
        ),
        out_specs=(
            P(("dp", "shard"), None, None),
            P(("dp", "shard"), None, None),
            P(("dp", "shard"), None, None),
            P(("dp", "shard")),
            P(("dp", "shard")),
            P(("dp", "shard")),
            P(("dp", "shard")),
            P(("dp", "shard")),
            P(("dp", "shard")),
            P(("dp", "shard")),
            P(("dp", "shard")),
            P(("dp", "shard")),
            P(("dp", "shard")),
            P(("dp", "shard")),
            P(("dp", "shard")),
            P(("dp", "shard")),
            P(("dp", "shard")),
            P(("dp", "shard")),
        ),
        check_vma=False,
    )
```

```python
import functools
import jax
import jax.numpy as jnp
from jax import lax
from jax.experimental import pallas as pl
from jax.experimental.pallas import tpu as pltpu
from jax.sharding import PartitionSpec as P

MESH = pl.DeviceIdType.MESH
BF = jnp.bfloat16
F32 = jnp.float32
learn_rate = 0.001
beta_one = 0.9
beta_two = 0.999
STEP = 10


class Place:
    def __init__(self, sizes):
        self.sizes = sizes
        dp, sh = lax.axis_index("dp"), lax.axis_index("shard")
        self.at = (dp // sizes[1], dp % sizes[1], sh // sizes[3], sh % sizes[3])

    def device(self, axis, coord):
        a, b, c, e = [coord if i == axis else v for i, v in enumerate(self.at)]
        return (a * self.sizes[1] + b, c * self.sizes[3] + e)

    def greet(self):
        barrier = pltpu.get_barrier_semaphore()
        count = 0
        for axis in range(4):
            n, me = self.sizes[axis], self.at[axis]
            if n == 2:
                pl.semaphore_signal(barrier, inc=1, device_id=self.device(axis, 1 - me), device_id_type=MESH)
                count = count + 1
            else:
                for step in (-1, 1):
                    there = me + step
                    ok = (there >= 0) & (there < n)

                    @pl.when(ok)
                    def _():
                        pl.semaphore_signal(barrier, inc=1, device_id=self.device(axis, there), device_id_type=MESH)

                    count = count + ok.astype(jnp.int32)
        pl.semaphore_wait(barrier, count)


class Sems:
    def __init__(self, send, recv):
        self.send, self.recv, self.used = send, recv, 0

    def take(self):
        k = self.used
        self.used += 1
        return self.send.at[k], self.recv.at[k]


def gather_sems(order, sizes):
    return 1 + sum(2 if sizes[x] == 2 else 4 * (sizes[x] - 1) for x in order)


def gather_rounds(place, ref, order, sems):
    sizes = place.sizes
    after = []
    held = []

    def group(axis=None, coord=None):
        idx = [slice(None) if i in held else place.at[i] for i in range(4)]
        if axis is not None:
            idx[axis] = coord
        return ref.at[tuple(idx)]

    def copy(block, axis, coord, pair):
        return pltpu.make_async_remote_copy(
            src_ref=block, dst_ref=block, send_sem=pair[0], recv_sem=pair[1],
            device_id=place.device(axis, coord), device_id_type=MESH)

    def to_sibling(axis, coord, cond):
        pair = sems.take()
        idx = [slice(None) if i in held else place.at[i] for i in range(4)]
        if axis is not None:
            idx[axis] = coord
        mine = ref.at[tuple(idx)]
        idx[3] = 1 - place.at[3]
        theirs = ref.at[tuple(idx)]
        e = place.at[3]
        go = copy(mine, 3, 1 - e, pair)
        come = copy(theirs, 3, 1 - e, pair)

        def run(f):
            if cond is None:
                f()
            else:
                pl.when(cond)(f)

        run(go.start)

        def finish():
            go.wait_send()
            come.wait_recv()

        after.append(lambda: run(finish))

    to_sibling(None, None, None)
    for axis in order:
        n, me = sizes[axis], place.at[axis]
        if n == 2:
            pair = sems.take()
            go = copy(group(), axis, 1 - me, pair)
            come = copy(group(axis, 1 - me), axis, 1 - me, pair)
            go.start()
            after.append(go.wait_send)
            yield
            come.wait_recv()
            to_sibling(axis, 1 - me, None)
        else:
            for t in range(1, n):
                pending = []
                for step in (1, -1):
                    pair = sems.take()
                    out_c, in_c, to = me - step * (t - 1), me - step * t, me + step
                    can = (out_c >= 0) & (out_c < n) & (to >= 0) & (to < n)
                    gets = (in_c >= 0) & (in_c < n)
                    go = copy(group(axis, out_c), axis, to, pair)
                    come = copy(group(axis, in_c), axis, to, pair)
                    pl.when(can)(go.start)
                    after.append(lambda go=go, can=can: pl.when(can)(go.wait_send))
                    pending.append((come, gets, in_c))
                yield
                for come, gets, in_c in pending:
                    pl.when(gets)(come.wait_recv)
                    to_sibling(axis, in_c, gets)
        held.append(axis)
    yield
    for f in after:
        f()


def interleave(rounds):
    live = list(rounds)
    while live:
        still = []
        for r in live:
            try:
                next(r)
                still.append(r)
            except StopIteration:
                pass
        live = still


def flat_to_rows(src, dst, rows, cols):
    w = cols // 128
    for j in range(w):
        dst[:, j * 128:(j + 1) * 128] = src[pl.ds(j, rows, stride=w), :].astype(dst.dtype)


def rows_to_flat(value, dst, rows, cols):
    w = cols // 128
    for j in range(w):
        dst[pl.ds(j, rows, stride=w), :] = value[:, j * 128:(j + 1) * 128]


ORDERS = ((0, 2, 1), (0, 1, 2), (1, 2, 0), (0, 1, 2), (0, 1, 2))


def gather_kernel(sizes, shapes, *refs):
    n = len(shapes)
    masters, outs = refs[:n], refs[n:2 * n]
    stage, local, send, recv = refs[2 * n:3 * n], refs[3 * n], refs[3 * n + 1], refs[3 * n + 2]
    place = Place(sizes)
    copies = []
    for k, (rows, cols) in enumerate(shapes):
        if rows == 1:
            stage[k][...] = masters[k][...].astype(BF).astype(stage[k].dtype)
        else:
            flat_to_rows(masters[k], stage[k], rows, cols)
        cp = pltpu.make_async_copy(stage[k], outs[k].at[place.at], local.at[k])
        cp.start()
        copies.append(cp)
    place.greet()
    for cp in copies:
        cp.wait()
    sems = Sems(send, recv)
    interleave([gather_rounds(place, outs[k], ORDERS[k], sems) for k in range(n)])


def gather_all(mesh_sizes, masters, shapes, dtypes):
    n = len(shapes)
    total = sum(gather_sems(ORDERS[k], mesh_sizes) for k in range(n))
    vm = pl.BlockSpec(memory_space=pltpu.VMEM)
    return pl.pallas_call(
        functools.partial(gather_kernel, mesh_sizes, shapes),
        out_shape=[jax.ShapeDtypeStruct((*mesh_sizes, *s), d) for s, d in zip(shapes, dtypes)],
        in_specs=[vm] * n,
        out_specs=[pl.BlockSpec(memory_space=pl.ANY)] * n,
        scratch_shapes=[pltpu.VMEM(s, d) for s, d in zip(shapes, dtypes)]
        + [pltpu.SemaphoreType.DMA((n,)), pltpu.SemaphoreType.DMA((total,)), pltpu.SemaphoreType.DMA((total,))],
        compiler_params=pltpu.CompilerParams(collective_id=0, has_side_effects=True, vmem_limit_bytes=48 << 20),
        name="gather_weights",
    )(*masters)


def reduce_sems(order, sizes):
    return 1 + sum(1 if sizes[x] == 2 else 2 * (sizes[x] - 1) for x in order)


def reduce_rounds(place, grad, order, got, bufs, total, sems):
    sizes = place.sizes
    after = []
    e = place.at[3]

    def rdma(src, dst, axis, coord, pair):
        return pltpu.make_async_remote_copy(
            src_ref=src, dst_ref=dst, send_sem=pair[0], recv_sem=pair[1],
            device_id=place.device(axis, coord), device_id_type=MESH)

    def add_into(dst, src):
        dst[...] = (dst[...].astype(F32) + src[...].astype(F32)).astype(dst.dtype)

    def each(dims, f):
        count = 1
        for d in dims:
            count *= d
        if count == 1:
            f(tuple(0 for _ in dims))
            return

        def step(i, _):
            idx = []
            for d in reversed(dims):
                idx.append(i % d)
                i = i // d
            f(tuple(reversed(idx)))
            return 0

        lax.fori_loop(0, count, step, 0)

    cp = rdma(grad.at[:, :, :, 1 - e], got, 3, 1 - e, sems.take())
    cp.start()
    yield
    cp.wait()
    each(sizes[:3], lambda i: add_into(got.at[i], grad.at[(*i, e)]))
    cur, left = got, [0, 1, 2]
    for axis, buf in zip(order, bufs):
        n, me = sizes[axis], place.at[axis]
        pos = left.index(axis)
        rest = [x for x in left if x != axis]
        dims = [sizes[x] for x in rest]

        def part(ref, coord):
            return ref.at[tuple(coord if i == pos else slice(None) for i in range(len(left)))]

        def one(ref, coord, i):
            i = list(i)
            i.insert(pos, coord)
            return ref.at[tuple(i)]

        last = not rest
        if n == 2:
            cp = rdma(part(cur, 1 - me), buf, axis, 1 - me, sems.take())
            cp.start()
            yield
            cp.wait()
            if last:
                total[...] = buf[...].astype(F32) + cur[me].astype(F32)
            else:
                each(dims, lambda i: add_into(buf.at[i], one(cur, me, i)))
        else:
            for t in range(n - 1):
                for way, step in enumerate((1, -1)):
                    j = n - 1 - t if step == 1 else t
                    to, back = me + step, me - step
                    ahead = (j > me) if step == 1 else (j < me)
                    gets = ahead & (back >= 0) & (back < n)
                    pair = sems.take()
                    come = rdma(part(cur, j), buf.at[way, j], axis, to, pair)

                    @pl.when(gets)
                    def _():
                        come.wait_recv()
                        each(dims, lambda i: add_into(one(cur, j, i), buf.at[(way, j, *i)]))

                    pl.when(ahead)(come.start)
                    after.append(lambda come=come, ahead=ahead: pl.when(ahead)(come.wait_send))
                    ends = (j == me) & (back >= 0) & (back < n)
                    after.append(lambda come=come, ends=ends: pl.when(ends)(come.wait_recv))
                yield
            for f in after:
                f()
            after = []
            keep = buf.at[0, me]

            def close(i):
                mine = one(cur, me, i)[...].astype(F32)
                v = mine + jnp.where(me > 0, buf[(0, me, *i)].astype(F32), 0.0)
                v = v + jnp.where(me < n - 1, buf[(1, me, *i)].astype(F32), 0.0)
                if last:
                    total[...] = v
                else:
                    buf[(0, me, *i)] = v.astype(buf.dtype)

            each(dims, close)
            buf = keep
        cur, left = buf, rest
    for f in after:
        f()


def reduce_bufs(order, sizes, shape):
    left, out = [0, 1, 2], [(*sizes[:3], *shape)]
    for axis in order:
        rest = [x for x in left if x != axis]
        dims = tuple(sizes[x] for x in rest)
        out.append((*dims, *shape) if sizes[axis] == 2 else (2, sizes[axis], *dims, *shape))
        left = rest
    return out


BACK = tuple(tuple(reversed(o)) for o in ORDERS)


def adam(mean_old, square_old, grad):
    mean_new = beta_one * mean_old + (1.0 - beta_one) * grad
    square_new = beta_two * square_old + (1.0 - beta_two) * grad * grad
    steps = float(STEP)
    mean_hat = mean_new / (1.0 - beta_one**steps)
    square_hat = square_new / (1.0 - beta_two**steps)
    return -learn_rate * mean_hat / (jnp.sqrt(square_hat) + 1e-08), mean_new


def reduce_kernel(sizes, shapes, counts, *refs):
    n = len(shapes)
    refs = list(refs)

    def take(k):
        out = refs[:k]
        del refs[:k]
        return out

    grads, means, squares = take(n), take(n), take(n)
    outs = take(3 * n)
    totals = take(n)
    bufs = [take(c) for c in counts]
    send, recv = take(2)
    place = Place(sizes)
    place.greet()
    sems = Sems(send, recv)
    interleave([reduce_rounds(place, grads[k], BACK[k], bufs[k][0], bufs[k][1:], totals[k], sems) for k in range(n)])
    for k, (rows, cols) in enumerate(shapes):
        change, mean, summed = outs[3 * k:3 * k + 3]
        if rows == 1:
            summed[...] = totals[k][...]
        else:
            rows_to_flat(totals[k], summed, rows, cols)
        change[...], mean[...] = adam(means[k][...], squares[k][...], summed[...])


def reduce_all(mesh_sizes, grads, means, squares, shapes):
    n = len(shapes)
    flat = [((s[0] * s[1]) // 128, 128) for s in shapes]
    lists = [reduce_bufs(BACK[k], mesh_sizes, shapes[k]) for k in range(n)]
    total = sum(reduce_sems(BACK[k], mesh_sizes) for k in range(n))
    vm = pl.BlockSpec(memory_space=pltpu.VMEM)
    scratch = [pltpu.VMEM(s, F32) for s in shapes]
    for k in range(n):
        scratch += [pltpu.VMEM(s, grads[k].dtype) for s in lists[k]]
    scratch += [pltpu.SemaphoreType.DMA((total,)), pltpu.SemaphoreType.DMA((total,))]
    return pl.pallas_call(
        functools.partial(reduce_kernel, mesh_sizes, shapes, [len(x) for x in lists]),
        out_shape=[jax.ShapeDtypeStruct(f, F32) for f in flat for _ in range(3)],
        in_specs=[vm] * (3 * n),
        out_specs=[vm] * (3 * n),
        scratch_shapes=scratch,
        compiler_params=pltpu.CompilerParams(collective_id=1, has_side_effects=True, vmem_limit_bytes=60 << 20),
        name="reduce_gradients",
    )(*grads, *means, *squares)


D = 512
HEADS = 8
HD = 64
FF = 2048
ROW = 1024
SEGS = 24
QT = 256
KT = 128
PAIR = 128
NEG = -1000000000.0


def dot(a, b):
    return jnp.dot(a, b, preferred_element_type=F32)


def dot_t(a, b):
    return lax.dot_general(a, b, (((1,), (1,)), ((), ())), preferred_element_type=F32)


def t_dot(a, b):
    return lax.dot_general(a, b, (((0,), (0,)), ((), ())), preferred_element_type=F32)


def for_rows(block, f, rows=ROW):
    def step(i, _):
        f(pl.ds(pl.multiple_of(i * block, block), block))
        return 0

    lax.fori_loop(0, rows // block, step, 0)


def ends_of(lengths):
    out, total = [], jnp.int32(0)
    for i in range(SEGS):
        total = total + lengths[0, i]
        out.append(total)
    return out


def seg_at(ends, place):
    count = jnp.int32(0)
    for e in ends:
        count = count + (e <= place).astype(jnp.int32)
    return count


def pick(values, index):
    out = values[-1]
    for i in range(len(values) - 2, -1, -1):
        out = jnp.where(index <= i, values[i], out)
    return out


def seg_row(ends):
    place = lax.broadcasted_iota(jnp.int32, (1, ROW), 1)
    out = jnp.zeros((1, ROW), jnp.int32)
    for e in ends:
        out = out + (place >= e).astype(jnp.int32)
    return out.astype(F32)


def store_seg(ends, row_ref, col_ref):
    row_ref[...] = jnp.broadcast_to(seg_row(ends), (8, ROW))
    for i in range(ROW // 128):
        block = jnp.broadcast_to(row_ref[0:1, i * 128:(i + 1) * 128], (128, 128))
        col_ref[i * 128:(i + 1) * 128, :] = jnp.transpose(block)


def ranges(query_ends, key_ends, causal, tile, other, by_query):
    out = []
    here, there = (query_ends, key_ends) if by_query else (key_ends, query_ends)
    starts = [jnp.int32(0)] + there[:-1]
    for i in range(ROW // tile):
        first, last = i * tile, (i + 1) * tile - 1
        low = pick(starts, seg_at(here, first)) // other
        high = (pick(there, seg_at(here, last)) + other - 1) // other
        if causal and by_query:
            high = jnp.int32((i + 1) * tile // other)
        if causal and not by_query:
            low = jnp.int32(i * tile // other)
        out.append((low, high))
    return out


def store_ranges(ref, base, pairs):
    for i, (low, high) in enumerate(pairs):
        ref[base + 2 * i] = low
        ref[base + 2 * i + 1] = high


def head_masks():
    lane = lax.broadcasted_iota(jnp.int32, (1, PAIR), 1)
    left = (lane < HD).astype(F32).astype(BF)
    return left, (1.0 - left.astype(F32)).astype(BF)


def stack_heads(block, masks):
    return jnp.concatenate([block * masks[0], block * masks[1]], 0)


def block_diag(pair_t):
    zero = jnp.zeros((HD, pair_t.shape[1]), pair_t.dtype)
    top = jnp.concatenate([pair_t[:HD], zero], 1)
    low = jnp.concatenate([zero, pair_t[HD:]], 1)
    return jnp.concatenate([top, low], 0)


def bias_tile(key_col, query_row, k0, q0, causal):
    keys = key_col[pl.ds(k0, KT), :]
    keys = jnp.concatenate([keys] * (QT // 128), 1)
    ok = keys == query_row[0:1, pl.ds(q0, QT)]
    if causal:
        kpos = k0 + lax.broadcasted_iota(jnp.int32, (KT, QT), 0)
        qpos = q0 + lax.broadcasted_iota(jnp.int32, (KT, QT), 1)
        ok = ok & (kpos <= qpos)
    return jnp.where(ok, 0.0, NEG)


def attend(q, k, vt, key_col, query_row, table, base, causal, out, lse, acc, peak, tally):
    masks = head_masks()

    def q_tile(i, _):
        q0 = pl.multiple_of(i * QT, QT)
        acc[...] = jnp.zeros_like(acc)
        peak[...] = jnp.full_like(peak, -3e38)
        tally[...] = jnp.zeros_like(tally)

        def k_tile(j, _):
            k0 = pl.multiple_of(j * KT, KT)
            bias = bias_tile(key_col, query_row, k0, q0, causal)
            peaks, tallies = [], []
            for hp in range(HEADS // 2):
                cols = slice(hp * PAIR, (hp + 1) * PAIR)
                s = dot_t(stack_heads(k[pl.ds(k0, KT), cols], masks), q[pl.ds(q0, QT), cols])
                probs, scales = [], []
                for side in range(2):
                    h = 2 * hp + side
                    sh = s[side * KT:(side + 1) * KT] + bias
                    old = peak[h:h + 1, :]
                    new = jnp.maximum(old, jnp.max(sh, 0, keepdims=True))
                    p = jnp.exp(sh - new)
                    scale = jnp.exp(old - new)
                    tallies.append(scale * tally[h:h + 1, :] + jnp.sum(p, 0, keepdims=True))
                    peaks.append(new)
                    probs.append(p.astype(BF))
                    scales.append(scale)
                o = dot(block_diag(vt[cols, pl.ds(k0, KT)]), jnp.concatenate(probs, 0))
                for side in range(2):
                    rows = slice(hp * PAIR + side * HD, hp * PAIR + (side + 1) * HD)
                    acc[rows, :] = acc[rows, :] * scales[side] + o[side * HD:(side + 1) * HD]
            peak[...] = jnp.concatenate(peaks, 0)
            tally[...] = jnp.concatenate(tallies, 0)
            return 0

        lax.fori_loop(table[base + 2 * i], table[base + 2 * i + 1], k_tile, 0)
        total = tally[...]
        lse[:, pl.ds(q0, QT)] = peak[...] + jnp.log(total)
        inverse = 1.0 / total
        for hp in range(HEADS // 2):
            rows = [acc[hp * PAIR + s * HD:hp * PAIR + (s + 1) * HD, :] * inverse[2 * hp + s:2 * hp + s + 1, :] for s in range(2)]
            out[pl.ds(q0, QT), hp * PAIR:(hp + 1) * PAIR] = jnp.transpose(jnp.concatenate(rows, 0)).astype(BF)
        return 0

    lax.fori_loop(0, ROW // QT, q_tile, 0)


def attend_back(q, k, v, kt, grad, lse, inner, key_col, query_row, table, base, causal, dqt, dk, dv, dk_acc, dv_acc):
    masks = head_masks()
    left = lax.broadcasted_iota(jnp.int32, (KT, PAIR), 1) < HD
    dqt[...] = jnp.zeros_like(dqt)

    def k_tile(j, _):
        k0 = pl.multiple_of(j * KT, KT)
        dk_acc[...] = jnp.zeros_like(dk_acc)
        dv_acc[...] = jnp.zeros_like(dv_acc)

        def q_tile(i, _):
            q0 = pl.multiple_of(i * QT, QT)
            bias = bias_tile(key_col, query_row, k0, q0, causal)
            for hp in range(HEADS // 2):
                cols = slice(hp * PAIR, (hp + 1) * PAIR)
                qp, gp = q[pl.ds(q0, QT), cols], grad[pl.ds(q0, QT), cols]
                s = dot_t(stack_heads(k[pl.ds(k0, KT), cols], masks), qp)
                dp = dot_t(stack_heads(v[pl.ds(k0, KT), cols], masks), gp)
                probs, slopes = [], []
                for side in range(2):
                    h = 2 * hp + side
                    rows = slice(side * KT, (side + 1) * KT)
                    p = jnp.exp(s[rows] + bias - lse[h:h + 1, pl.ds(q0, QT)])
                    slopes.append((p * (dp[rows] - inner[h:h + 1, pl.ds(q0, QT)])).astype(BF))
                    probs.append(p.astype(BF))
                probs, slopes = jnp.concatenate(probs, 0), jnp.concatenate(slopes, 0)
                to_v, to_k = dot(probs, gp), dot(slopes, qp)
                dv_acc[:, cols] += jnp.where(left, to_v[:KT], to_v[KT:])
                dk_acc[:, cols] += jnp.where(left, to_k[:KT], to_k[KT:])
                dqt[cols, pl.ds(q0, QT)] += dot(block_diag(kt[cols, pl.ds(k0, KT)]), slopes)
            return 0

        lax.fori_loop(table[base + 2 * j], table[base + 2 * j + 1], q_tile, 0)
        dk[pl.ds(k0, KT), :] = dk_acc[...].astype(BF)
        dv[pl.ds(k0, KT), :] = dv_acc[...].astype(BF)
        return 0

    lax.fori_loop(0, ROW // KT, k_tile, 0)


def normalize(r, xhat, rstd, at):
    centered = r - jnp.mean(r, -1, keepdims=True)
    spread = jnp.mean(centered * centered, -1, keepdims=True)
    scale = lax.rsqrt(spread + 1e-05)
    out = centered * scale
    xhat[at, :] = out
    rstd[at, :] = jnp.broadcast_to(scale, (out.shape[0], 128))
    return out


def norm_back(dh, xhat, rstd, gain):
    dx = dh * gain
    mean_dx = jnp.mean(dx, -1, keepdims=True)
    mean_xx = jnp.mean(dx * xhat, -1, keepdims=True)
    return rstd[:, 0:1] * (dx - mean_dx - xhat * mean_xx)


def fold(x):
    return jnp.sum(x.reshape(-1, 8, x.shape[-1]), 0)


def forward_kernel(
    tlen, slen, x, mem, win, wout, norms,
    q1, k1, v1, q2, k2, v2, c1, c2, lse1, lse2, xh1, rs1, xh2, rs2,
    trow, tcol, scol, table, vt, acc, peak, tally,
):
    tends, sends = ends_of(tlen), ends_of(slen)
    store_seg(tends, trow, tcol)
    store_seg(sends, trow, scol)
    trow[...] = jnp.broadcast_to(seg_row(tends), (8, ROW))
    store_ranges(table, 0, ranges(tends, tends, True, QT, KT, True))
    store_ranges(table, 8, ranges(tends, sends, False, QT, KT, True))

    def project(at):
        for out, src, w in ((q1, x, 0), (k1, x, 1), (v1, x, 2), (k2, mem, 4), (v2, mem, 5)):
            y = dot(src[at, :], win[w * D:(w + 1) * D, :]).astype(BF)
            out[at, :] = y * BF(0.125) if w == 0 else y

    for_rows(256, project)

    def flip(v):
        for i in range(ROW // 128):
            vt[:, i * 128:(i + 1) * 128] = jnp.transpose(v[i * 128:(i + 1) * 128, :])

    flip(v1)
    attend(q1, k1, vt, tcol, trow, table, 0, True, c1, lse1, acc, peak, tally)

    def middle(at):
        r = x[at, :].astype(F32) + dot(c1[at, :], wout[0:D, :])
        h = normalize(r, xh1, rs1, at) * norms[0:1, :] + norms[3:4, :]
        q2[at, :] = dot(h.astype(BF), win[3 * D:4 * D, :]).astype(BF) * BF(0.125)

    for_rows(256, middle)
    flip(v2)
    attend(q2, k2, vt, scol, trow, table, 8, False, c2, lse2, acc, peak, tally)

    def end(at):
        h = xh1[at, :] * norms[0:1, :] + norms[3:4, :]
        normalize(h + dot(c2[at, :], wout[D:2 * D, :]), xh2, rs2, at)

    for_rows(256, end)


def ffn_kernel(tlen, xh2, cot, up, down, norms, result, dh2, gup, gdown, gnorm, h2b, act, du, dy, pre):
    live_end = ends_of(tlen)[SEGS - 2]
    gnorm[...] = jnp.zeros_like(gnorm)
    block = 256

    def rows(i, _):
        at = pl.ds(pl.multiple_of(i * block, block), block)
        h = xh2[at, :] * norms[1:2, :] + norms[4:5, :]
        hb = h.astype(BF)
        h2b[at, :] = hb
        r3 = h
        for j in range(FF // D):
            cols = slice(j * D, (j + 1) * D)
            u = dot(hb, up[:, cols])
            pre[:, cols] = u
            a = (u / (1.0 + jnp.exp(-u))).astype(BF)
            act[at, cols] = a
            r3 = r3 + dot(a, down[cols, :])
        centered = r3 - jnp.mean(r3, -1, keepdims=True)
        spread = jnp.mean(centered * centered, -1, keepdims=True)
        rstd = lax.rsqrt(spread + 1e-05)
        xhat = centered * rstd
        result[at, :] = (xhat * norms[2:3, :] + norms[5:6, :]).astype(BF)
        place = i * block + lax.broadcasted_iota(jnp.int32, (block, D), 0)
        seed = jnp.where(place < live_end, cot[at, :].astype(F32), 0.0)
        gnorm[0:8, :] += fold(seed * xhat)
        gnorm[8:16, :] += fold(seed)
        dr3 = norm_back(seed, xhat, rstd, norms[2:3, :])
        dyb = dr3.astype(BF)
        dy[at, :] = dyb
        dh = dr3
        for j in range(FF // D):
            cols = slice(j * D, (j + 1) * D)
            da = dot_t(dyb, down[cols, :])
            u = pre[:, cols]
            sig = 1.0 / (1.0 + jnp.exp(-u))
            d = (da * (sig * (1.0 + u * (1.0 - sig)))).astype(BF)
            du[at, cols] = d
            dh = dh + dot_t(d, up[:, cols])
        dh2[at, :] = dh
        return 0

    lax.fori_loop(0, ROW // block, rows, 0)
    for j in range(FF // D):
        cols = slice(j * D, (j + 1) * D)
        gdown[cols, :] = t_dot(act[:, cols], dy[...]).astype(BF)
        gup[:, cols] = t_dot(h2b[...], du[:, cols]).astype(BF)


def backward_kernel(
    tlen, slen, x, mem, win, wout, norms, q1, k1, v1, q2, k2, v2, c1, c2, lse1, lse2, xh1, rs1, xh2, rs2, dh2,
    tgrad, mgrad, gin, gout, gnorm,
    trow, tcol, scol, table, kt, dc, h1b, inner, dqt, dq, dk, dv, dk_acc, dv_acc, dr,
):
    tends, sends = ends_of(tlen), ends_of(slen)
    store_seg(tends, trow, tcol)
    store_seg(sends, trow, scol)
    trow[...] = jnp.broadcast_to(seg_row(tends), (8, ROW))
    store_ranges(table, 0, ranges(tends, tends, True, KT, QT, False))
    store_ranges(table, 16, ranges(tends, sends, False, KT, QT, False))
    gnorm[...] = jnp.zeros_like(gnorm)
    heads = (lax.broadcasted_iota(jnp.int32, (HEADS, D), 1) // HD == lax.broadcasted_iota(jnp.int32, (HEADS, D), 0))
    heads = heads.astype(F32).astype(BF)

    def into_attention(at, r, w, c):
        g = dot_t(r.astype(BF), wout[w * D:(w + 1) * D, :]).astype(BF)
        dc[at, :] = g
        both = g.astype(F32) * c[at, :].astype(F32)
        high = both.astype(BF)
        low = (both - high.astype(F32)).astype(BF)
        inner[:, at] = dot_t(heads, high) + dot_t(heads, low)

    def flip(k):
        for i in range(ROW // 128):
            kt[:, i * 128:(i + 1) * 128] = jnp.transpose(k[i * 128:(i + 1) * 128, :])

    def queries_back(at):
        dq[at, :] = jnp.transpose(dqt[:, at] * 0.125).astype(BF)

    def first(at):
        dh, xhat = dh2[at, :], xh2[at, :]
        gnorm[0:8, :] += fold(dh * xhat)
        gnorm[8:16, :] += fold(dh)
        r = norm_back(dh, xhat, rs2[at, :], norms[1:2, :])
        dr[at, :] = r
        h1b[at, :] = (xh1[at, :] * norms[0:1, :] + norms[3:4, :]).astype(BF)
        into_attention(at, r, 1, c2)

    for_rows(256, first)
    gout[D:2 * D, :] = t_dot(c2[...], dr[...].astype(BF)).astype(BF)
    flip(k2)
    attend_back(q2, k2, v2, kt, dc, lse2, inner, scol, trow, table, 16, False, dqt, dk, dv, dk_acc, dv_acc)
    for_rows(256, queries_back)
    gin[3 * D:4 * D, :] = t_dot(h1b[...], dq[...]).astype(BF)
    gin[4 * D:5 * D, :] = t_dot(mem[...], dk[...]).astype(BF)
    gin[5 * D:6 * D, :] = t_dot(mem[...], dv[...]).astype(BF)

    def second(at):
        mgrad[at, :] = dot_t(dk[at, :], win[4 * D:5 * D, :]) + dot_t(dv[at, :], win[5 * D:6 * D, :])
        dh = dr[at, :] + dot_t(dq[at, :], win[3 * D:4 * D, :])
        xhat = xh1[at, :]
        gnorm[16:24, :] += fold(dh * xhat)
        gnorm[24:32, :] += fold(dh)
        r = norm_back(dh, xhat, rs1[at, :], norms[0:1, :])
        dr[at, :] = r
        into_attention(at, r, 0, c1)

    for_rows(256, second)
    gout[0:D, :] = t_dot(c1[...], dr[...].astype(BF)).astype(BF)
    flip(k1)
    attend_back(q1, k1, v1, kt, dc, lse1, inner, tcol, trow, table, 0, True, dqt, dk, dv, dk_acc, dv_acc)
    for_rows(256, queries_back)
    for i, g in enumerate((dq, dk, dv)):
        gin[i * D:(i + 1) * D, :] = t_dot(x[...], g[...]).astype(BF)

    def third(at):
        t = dr[at, :]
        for i, g in enumerate((dq, dk, dv)):
            t = t + dot_t(g[at, :], win[i * D:(i + 1) * D, :])
        tgrad[at, :] = t

    for_rows(256, third)


VM = pl.BlockSpec(memory_space=pltpu.VMEM)
SM = pl.BlockSpec(memory_space=pltpu.SMEM)


def call(kernel, name, ins, outs, scratch, scalars):
    return pl.pallas_call(
        kernel,
        out_shape=[jax.ShapeDtypeStruct(s, d) for s, d in outs],
        in_specs=[SM] * scalars + [VM] * (len(ins) - scalars),
        out_specs=[VM] * len(outs),
        scratch_shapes=scratch,
        compiler_params=pltpu.CompilerParams(vmem_limit_bytes=62 << 20),
        name=name,
    )(*ins)


def layer(tlen, slen, x, mem, cot, win, wout, up, down, norms):
    tok, tokf, stat, rep = ((ROW, D), BF), ((ROW, D), F32), ((HEADS, ROW), F32), ((ROW, 128), F32)
    segs = [pltpu.VMEM((8, ROW), F32), pltpu.VMEM((ROW, 128), F32), pltpu.VMEM((ROW, 128), F32), pltpu.SMEM((32,), jnp.int32)]
    kept = call(
        forward_kernel, "forward", [tlen, slen, x, mem, win, wout, norms],
        [tok] * 8 + [stat] * 2 + [tokf, rep] * 2,
        segs + [pltpu.VMEM((D, ROW), BF), pltpu.VMEM((D, QT), F32), pltpu.VMEM((HEADS, QT), F32), pltpu.VMEM((HEADS, QT), F32)],
        2,
    )
    xh2 = kept[12]
    result, dh2, gup, gdown, gnorm_three = call(
        ffn_kernel, "feed_forward", [tlen, xh2, cot, up, down, norms],
        [tok, tokf, ((D, FF), BF), ((FF, D), BF), ((16, D), F32)],
        [pltpu.VMEM((ROW, D), BF), pltpu.VMEM((ROW, FF), BF), pltpu.VMEM((ROW, FF), BF), pltpu.VMEM((ROW, D), BF), pltpu.VMEM((256, FF), F32)],
        1,
    )
    tgrad, mgrad, gin, gout, gnorm_rest = call(
        backward_kernel, "backward", [tlen, slen, x, mem, win, wout, norms, *kept, dh2],
        [tokf, tokf, ((6 * D, D), BF), ((2 * D, D), BF), ((32, D), F32)],
        segs + [pltpu.VMEM((D, ROW), BF), pltpu.VMEM((ROW, D), BF), pltpu.VMEM((ROW, D), BF), pltpu.VMEM((HEADS, ROW), F32),
                pltpu.VMEM((D, ROW), F32)] + [pltpu.VMEM((ROW, D), BF)] * 3 + [pltpu.VMEM((KT, D), F32)] * 2 + [pltpu.VMEM((ROW, D), F32)],
        2,
    )
    three = jnp.sum(gnorm_three.reshape(2, 8, D), 1)
    rest = jnp.sum(gnorm_rest.reshape(4, 8, D), 1)
    gnorm = jnp.stack([rest[2], rest[0], three[0], rest[3], rest[1], three[1]])
    return result, tgrad, mgrad, gin, gout, gup, gdown, gnorm


def shard_views(inward, outward, expand, shrink, norms):
    arrays, shapes = [], []
    for x, wide in ((inward, D), (outward, D), (expand, FF), (shrink, D)):
        cols = wide if x.shape[0] >= 16 * wide else D
        arrays.append(x.reshape(-1, 128))
        shapes.append((x.shape[0] // cols, cols))
    width = -(-norms.shape[0] // 128) * 128
    arrays.append(jnp.pad(norms, (0, width - norms.shape[0])).reshape(1, width))
    shapes.append((1, width))
    return arrays, tuple(shapes)


def body(
    sizes, target, memory, cotangent, target_lengths, source_lengths,
    inward_master, inward_mean, inward_square, outward_master, outward_mean, outward_square,
    expand_master, expand_mean, expand_square, shrink_master, shrink_mean, shrink_square,
    norms_master, norms_mean, norms_square,
):
    flat, shapes = shard_views(inward_master, outward_master, expand_master, shrink_master, norms_master)
    win, wout, up, down, norms = gather_all(sizes, flat, shapes, [BF, BF, BF, BF, F32])
    norm_count = norms_master.shape[0]
    norms = norms.reshape(-1, norms.shape[-1])[:, :norm_count].reshape(6, D)
    result, tgrad, mgrad, gin, gout, gup, gdown, gnorm = layer(
        target_lengths, source_lengths, target[0], memory[0], cotangent[0],
        win.reshape(6 * D, D), wout.reshape(2 * D, D), up.reshape(D, FF), down.reshape(FF, D), norms,
    )
    gnorm = jnp.pad(gnorm.reshape(-1, norm_count), ((0, 0), (0, shapes[4][1] - norm_count)))
    grads = [g.reshape(*sizes, *s) for g, s in zip((gin, gout, gup, gdown, gnorm), shapes)]
    means, _ = shard_views(inward_mean, outward_mean, expand_mean, shrink_mean, norms_mean)
    squares, _ = shard_views(inward_square, outward_square, expand_square, shrink_square, norms_square)
    outs = [x.reshape(-1) for x in reduce_all(sizes, grads, means, squares, shapes)]
    return (result[None], tgrad[None], mgrad[None], *outs[:12], *[x[:norm_count] for x in outs[12:]])


def solution(mesh):
    rows, cols = mesh.shape["dp"], mesh.shape["shard"]
    both = ("dp", "shard")
    row, flat = P(both, None, None), P(both)
    return jax.shard_map(
        functools.partial(body, (rows // 2, 2, cols // 2, 2)),
        mesh=mesh,
        in_specs=(row, row, row, P(both, None), P(both, None), *[flat] * 15),
        out_specs=(row, row, row, *[flat] * 15),
        check_vma=False,
    )
```

```python
import functools
import jax
import jax.numpy as jnp
from jax import lax
from jax.experimental import pallas as pl
from jax.experimental.pallas import tpu as pltpu
from jax.sharding import PartitionSpec as P

MESH = pl.DeviceIdType.MESH
BF = jnp.bfloat16
F32 = jnp.float32
learn_rate = 0.001
beta_one = 0.9
beta_two = 0.999
STEP = 10


class Place:
    def __init__(self, sizes):
        self.sizes = sizes
        dp, sh = lax.axis_index("dp"), lax.axis_index("shard")
        self.at = (dp // sizes[1], dp % sizes[1], sh // sizes[3], sh % sizes[3])

    def device(self, axis, coord):
        a, b, c, e = [coord if i == axis else v for i, v in enumerate(self.at)]
        return (a * self.sizes[1] + b, c * self.sizes[3] + e)

    def greet(self):
        barrier = pltpu.get_barrier_semaphore()
        count = 0
        for axis in range(4):
            n, me = self.sizes[axis], self.at[axis]
            if n == 2:
                pl.semaphore_signal(barrier, inc=1, device_id=self.device(axis, 1 - me), device_id_type=MESH)
                count = count + 1
            else:
                for step in (-1, 1):
                    there = me + step
                    ok = (there >= 0) & (there < n)

                    @pl.when(ok)
                    def _():
                        pl.semaphore_signal(barrier, inc=1, device_id=self.device(axis, there), device_id_type=MESH)

                    count = count + ok.astype(jnp.int32)
        pl.semaphore_wait(barrier, count)


class Sems:
    def __init__(self, send, recv):
        self.send, self.recv, self.used = send, recv, 0

    def take(self):
        k = self.used
        self.used += 1
        return self.send.at[k], self.recv.at[k]


def gather_sems(order, sizes):
    return 1 + sum(2 if sizes[x] == 2 else 4 * (sizes[x] - 1) for x in order)


def gather_rounds(place, ref, order, sems):
    sizes = place.sizes
    after = []
    held = []

    def group(axis=None, coord=None):
        idx = [slice(None) if i in held else place.at[i] for i in range(4)]
        if axis is not None:
            idx[axis] = coord
        return ref.at[tuple(idx)]

    def copy(block, axis, coord, pair):
        return pltpu.make_async_remote_copy(
            src_ref=block, dst_ref=block, send_sem=pair[0], recv_sem=pair[1],
            device_id=place.device(axis, coord), device_id_type=MESH)

    def to_sibling(axis, coord, cond):
        pair = sems.take()
        idx = [slice(None) if i in held else place.at[i] for i in range(4)]
        if axis is not None:
            idx[axis] = coord
        mine = ref.at[tuple(idx)]
        idx[3] = 1 - place.at[3]
        theirs = ref.at[tuple(idx)]
        e = place.at[3]
        go = copy(mine, 3, 1 - e, pair)
        come = copy(theirs, 3, 1 - e, pair)

        def run(f):
            if cond is None:
                f()
            else:
                pl.when(cond)(f)

        run(go.start)

        def finish():
            go.wait_send()
            come.wait_recv()

        after.append(lambda: run(finish))

    to_sibling(None, None, None)
    for axis in order:
        n, me = sizes[axis], place.at[axis]
        if n == 2:
            pair = sems.take()
            go = copy(group(), axis, 1 - me, pair)
            come = copy(group(axis, 1 - me), axis, 1 - me, pair)
            go.start()
            after.append(go.wait_send)
            yield
            come.wait_recv()
            to_sibling(axis, 1 - me, None)
        else:
            for t in range(1, n):
                pending = []
                for step in (1, -1):
                    pair = sems.take()
                    out_c, in_c, to = me - step * (t - 1), me - step * t, me + step
                    can = (out_c >= 0) & (out_c < n) & (to >= 0) & (to < n)
                    gets = (in_c >= 0) & (in_c < n)
                    go = copy(group(axis, out_c), axis, to, pair)
                    come = copy(group(axis, in_c), axis, to, pair)
                    pl.when(can)(go.start)
                    after.append(lambda go=go, can=can: pl.when(can)(go.wait_send))
                    pending.append((come, gets, in_c))
                yield
                for come, gets, in_c in pending:
                    pl.when(gets)(come.wait_recv)
                    to_sibling(axis, in_c, gets)
        held.append(axis)
    yield
    for f in after:
        f()


def interleave(rounds):
    live = list(rounds)
    while live:
        still = []
        for r in live:
            try:
                next(r)
                still.append(r)
            except StopIteration:
                pass
        live = still


def flat_to_rows(src, dst, rows, cols):
    w = cols // 128
    for j in range(w):
        dst[:, j * 128:(j + 1) * 128] = src[pl.ds(j, rows, stride=w), :].astype(dst.dtype)


def rows_to_flat(value, dst, rows, cols):
    w = cols // 128
    for j in range(w):
        dst[pl.ds(j, rows, stride=w), :] = value[:, j * 128:(j + 1) * 128]


MOST_PATHS = 40


def both(a, b):
    return b if a is None else a if b is None else a & b


def when(cond, f):
    if cond is None:
        f()
    else:
        pl.when(cond)(f)


def paths(order, sizes):
    found = [()]
    for axis in order:
        n = sizes[axis]
        moves = [(axis, 0, 1)] if n == 2 else [(axis, way, d) for d in range(1, n) for way in (1, -1)]
        found = found + [p + (m,) for p in found for m in moves]
    return sorted(found, key=lambda p: sum(m[2] for m in p))


def parent(path):
    axis, way, dist = path[-1]
    return path[:-1] + (((axis, way, dist - 1),) if dist > 1 else ())


class Block:
    def __init__(self, place, path):
        self.coords, self.exists = list(place.at), None
        for axis, way, dist in path:
            me, n = place.at[axis], place.sizes[axis]
            self.coords[axis] = 1 - me if way == 0 else me - way * dist
            if way:
                self.exists = both(self.exists, (self.coords[axis] >= 0) & (self.coords[axis] < n))

    def next_hop(self, place, child):
        axis, way, _ = child[-1]
        me, n = place.at[axis], place.sizes[axis]
        to = 1 - me if way == 0 else me + way
        ok = None if way == 0 else (to >= 0) & (to < n)
        return place.device(axis, to), both(self.exists, ok)


def remote(src, dst, pair, device):
    return pltpu.make_async_remote_copy(
        src_ref=src, dst_ref=dst, send_sem=pair[0], recv_sem=pair[1], device_id=device, device_id_type=MESH)


def gather_flow(place, ref, order, sems):
    e, sibling = place.at[3], place.device(3, 1 - place.at[3])
    ways = paths(order, place.sizes)
    blocks = {p: Block(place, p) for p in ways}
    pairs = {p: sems.take() for p in ways if p}
    after = []
    for p in ways:
        b = blocks[p]
        mine = ref.at[tuple(b.coords)]
        if p:
            yield
            when(b.exists, remote(mine, mine, pairs[p], sibling).wait_recv)
        for child in ways:
            if child and parent(child) == p:
                device, ok = b.next_hop(place, child)
                go = remote(mine, mine, pairs[child], device)
                when(ok, go.start)
                after.append((ok, go.wait_send))
        pair = sems.take()
        go = remote(mine, mine, pair, sibling)
        theirs = ref.at[(*b.coords[:3], 1 - e)]
        come = remote(theirs, theirs, pair, sibling)
        when(b.exists, go.start)
        after.append((b.exists, go.wait_send))
        after.append((b.exists, come.wait_recv))
    yield
    for ok, f in after:
        when(ok, f)


def reduce_flow(place, grad, order, half, arrived, total, sems):
    e, sibling = place.at[3], place.device(3, 1 - place.at[3])
    ways = paths(order, place.sizes)[::-1]
    blocks = {p: Block(place, p) for p in ways}
    slot = {p: i for i, p in enumerate(p for p in ways if p)}
    pairs = {p: sems.take() for p in ways if p}
    cores = {p: sems.take() for p in ways}
    rows = total.shape[0]
    chunk = 32 if rows % 32 == 0 else 16 if rows % 16 == 0 else rows
    after = []
    for p in ways:
        b = blocks[p]
        go = remote(grad.at[(*b.coords[:3], 1 - e)], half.at[tuple(b.coords[:3])], cores[p], sibling)
        when(b.exists, go.start)
        after.append((b.exists, go.wait_send))
    for p in ways:
        yield
        b = blocks[p]
        own, sums = grad.at[tuple(b.coords)], half.at[tuple(b.coords[:3])]
        kids = []
        for child in ways:
            if child and parent(child) == p:
                device, ok = b.next_hop(place, child)
                here = arrived.at[slot[child]]
                when(ok, remote(here, here, pairs[child], device).wait_recv)
                kids.append((here, ok))
        when(b.exists, remote(own, sums, cores[p], sibling).wait_recv)

        def add():
            def step(i, _):
                at = pl.ds(pl.multiple_of(i * chunk, chunk), chunk)
                v = own[at, :].astype(F32) + sums[at, :].astype(F32)
                for here, ok in kids:
                    term = here[at, :].astype(F32)
                    v = v + (term if ok is None else jnp.where(ok, term, 0.0))
                if p:
                    sums[at, :] = v.astype(sums.dtype)
                else:
                    total[at, :] = v
                return 0

            if rows == chunk:
                v = own[...].astype(F32) + sums[...].astype(F32)
                for here, ok in kids:
                    term = here[...].astype(F32)
                    v = v + (term if ok is None else jnp.where(ok, term, 0.0))
                if p:
                    sums[...] = v.astype(sums.dtype)
                else:
                    total[...] = v
            else:
                lax.fori_loop(0, rows // chunk, step, 0)

        when(b.exists, add)
        if p:
            axis, way, _ = p[-1]
            me = place.at[axis]
            device = place.device(axis, 1 - me if way == 0 else me - way)
            go = remote(sums, arrived.at[slot[p]], pairs[p], device)
            when(b.exists, go.start)
            after.append((b.exists, go.wait_send))
    yield
    for ok, f in after:
        when(ok, f)


ORDERS = ((0, 2, 1), (0, 1, 2), (1, 2, 0), (0, 1, 2), (0, 1, 2))


def flows(sizes):
    return len(paths((0, 1, 2), sizes)) <= MOST_PATHS


def gather_kernel(sizes, shapes, *refs):
    n = len(shapes)
    masters, outs = refs[:n], refs[n:2 * n]
    stage, local, send, recv = refs[2 * n:3 * n], refs[3 * n], refs[3 * n + 1], refs[3 * n + 2]
    place = Place(sizes)
    copies = []
    for k, (rows, cols) in enumerate(shapes):
        if rows == 1:
            stage[k][...] = masters[k][...].astype(BF).astype(stage[k].dtype)
        else:
            flat_to_rows(masters[k], stage[k], rows, cols)
        cp = pltpu.make_async_copy(stage[k], outs[k].at[place.at], local.at[k])
        cp.start()
        copies.append(cp)
    place.greet()
    for cp in copies:
        cp.wait()
    sems = Sems(send, recv)
    rounds = gather_flow if flows(sizes) else gather_rounds
    interleave([rounds(place, outs[k], ORDERS[k], sems) for k in range(n)])


def gather_all(mesh_sizes, masters, shapes, dtypes):
    n = len(shapes)
    if flows(mesh_sizes):
        total = n * 2 * len(paths((0, 1, 2), mesh_sizes))
    else:
        total = sum(gather_sems(ORDERS[k], mesh_sizes) for k in range(n))
    vm = pl.BlockSpec(memory_space=pltpu.VMEM)
    return pl.pallas_call(
        functools.partial(gather_kernel, mesh_sizes, shapes),
        out_shape=[jax.ShapeDtypeStruct((*mesh_sizes, *s), d) for s, d in zip(shapes, dtypes)],
        in_specs=[vm] * n,
        out_specs=[pl.BlockSpec(memory_space=pl.ANY)] * n,
        scratch_shapes=[pltpu.VMEM(s, d) for s, d in zip(shapes, dtypes)]
        + [pltpu.SemaphoreType.DMA((n,)), pltpu.SemaphoreType.DMA((total,)), pltpu.SemaphoreType.DMA((total,))],
        compiler_params=pltpu.CompilerParams(collective_id=0, has_side_effects=True, vmem_limit_bytes=48 << 20),
        name="gather_weights",
    )(*masters)


def reduce_sems(order, sizes):
    return 1 + sum(1 if sizes[x] == 2 else 2 * (sizes[x] - 1) for x in order)


def reduce_rounds(place, grad, order, got, bufs, total, sems):
    sizes = place.sizes
    after = []
    e = place.at[3]

    def rdma(src, dst, axis, coord, pair):
        return pltpu.make_async_remote_copy(
            src_ref=src, dst_ref=dst, send_sem=pair[0], recv_sem=pair[1],
            device_id=place.device(axis, coord), device_id_type=MESH)

    def add_into(dst, src):
        dst[...] = (dst[...].astype(F32) + src[...].astype(F32)).astype(dst.dtype)

    def each(dims, f):
        count = 1
        for d in dims:
            count *= d
        if count == 1:
            f(tuple(0 for _ in dims))
            return

        def step(i, _):
            idx = []
            for d in reversed(dims):
                idx.append(i % d)
                i = i // d
            f(tuple(reversed(idx)))
            return 0

        lax.fori_loop(0, count, step, 0)

    cp = rdma(grad.at[:, :, :, 1 - e], got, 3, 1 - e, sems.take())
    cp.start()
    yield
    cp.wait()
    each(sizes[:3], lambda i: add_into(got.at[i], grad.at[(*i, e)]))
    cur, left = got, [0, 1, 2]
    for axis, buf in zip(order, bufs):
        n, me = sizes[axis], place.at[axis]
        pos = left.index(axis)
        rest = [x for x in left if x != axis]
        dims = [sizes[x] for x in rest]

        def part(ref, coord):
            return ref.at[tuple(coord if i == pos else slice(None) for i in range(len(left)))]

        def one(ref, coord, i):
            i = list(i)
            i.insert(pos, coord)
            return ref.at[tuple(i)]

        last = not rest
        if n == 2:
            cp = rdma(part(cur, 1 - me), buf, axis, 1 - me, sems.take())
            cp.start()
            yield
            cp.wait()
            if last:
                total[...] = buf[...].astype(F32) + cur[me].astype(F32)
            else:
                each(dims, lambda i: add_into(buf.at[i], one(cur, me, i)))
        else:
            for t in range(n - 1):
                for way, step in enumerate((1, -1)):
                    j = n - 1 - t if step == 1 else t
                    to, back = me + step, me - step
                    ahead = (j > me) if step == 1 else (j < me)
                    gets = ahead & (back >= 0) & (back < n)
                    pair = sems.take()
                    come = rdma(part(cur, j), buf.at[way, j], axis, to, pair)

                    @pl.when(gets)
                    def _():
                        come.wait_recv()
                        each(dims, lambda i: add_into(one(cur, j, i), buf.at[(way, j, *i)]))

                    pl.when(ahead)(come.start)
                    after.append(lambda come=come, ahead=ahead: pl.when(ahead)(come.wait_send))
                    ends = (j == me) & (back >= 0) & (back < n)
                    after.append(lambda come=come, ends=ends: pl.when(ends)(come.wait_recv))
                yield
            for f in after:
                f()
            after = []
            keep = buf.at[0, me]

            def close(i):
                mine = one(cur, me, i)[...].astype(F32)
                v = mine + jnp.where(me > 0, buf[(0, me, *i)].astype(F32), 0.0)
                v = v + jnp.where(me < n - 1, buf[(1, me, *i)].astype(F32), 0.0)
                if last:
                    total[...] = v
                else:
                    buf[(0, me, *i)] = v.astype(buf.dtype)

            each(dims, close)
            buf = keep
        cur, left = buf, rest
    for f in after:
        f()


def reduce_bufs(order, sizes, shape):
    left, out = [0, 1, 2], [(*sizes[:3], *shape)]
    for axis in order:
        rest = [x for x in left if x != axis]
        dims = tuple(sizes[x] for x in rest)
        out.append((*dims, *shape) if sizes[axis] == 2 else (2, sizes[axis], *dims, *shape))
        left = rest
    return out


BACK = tuple(tuple(reversed(o)) for o in ORDERS)


def adam(mean_old, square_old, grad):
    mean_new = beta_one * mean_old + (1.0 - beta_one) * grad
    square_new = beta_two * square_old + (1.0 - beta_two) * grad * grad
    steps = float(STEP)
    mean_hat = mean_new / (1.0 - beta_one**steps)
    square_hat = square_new / (1.0 - beta_two**steps)
    return -learn_rate * mean_hat / (jnp.sqrt(square_hat) + 1e-08), mean_new


def reduce_kernel(sizes, shapes, counts, *refs):
    n = len(shapes)
    refs = list(refs)

    def take(k):
        out = refs[:k]
        del refs[:k]
        return out

    grads, totals = take(n), take(n)
    bufs = [take(c) for c in counts]
    send, recv = take(2)
    place = Place(sizes)
    place.greet()
    sems = Sems(send, recv)
    if flows(sizes):
        interleave([reduce_flow(place, grads[k], ORDERS[k], *bufs[k], totals[k], sems) for k in range(n)])
    else:
        interleave([reduce_rounds(place, grads[k], BACK[k], bufs[k][0], bufs[k][1:], totals[k], sems) for k in range(n)])


def reduce_all(mesh_sizes, grads, shapes):
    n = len(shapes)
    ways = len(paths((0, 1, 2), mesh_sizes))
    if flows(mesh_sizes):
        lists = [[(*mesh_sizes[:3], *s), (ways - 1, *s)] for s in shapes]
        total = n * 2 * ways
    else:
        lists = [reduce_bufs(BACK[k], mesh_sizes, shapes[k]) for k in range(n)]
        total = sum(reduce_sems(BACK[k], mesh_sizes) for k in range(n))
    vm = pl.BlockSpec(memory_space=pltpu.VMEM)
    scratch = []
    for k in range(n):
        scratch += [pltpu.VMEM(s, grads[k].dtype) for s in lists[k]]
    scratch += [pltpu.SemaphoreType.DMA((total,)), pltpu.SemaphoreType.DMA((total,))]
    return pl.pallas_call(
        functools.partial(reduce_kernel, mesh_sizes, shapes, [len(x) for x in lists]),
        out_shape=[jax.ShapeDtypeStruct(s, F32) for s in shapes],
        in_specs=[vm] * n,
        out_specs=[vm] * n,
        scratch_shapes=scratch,
        compiler_params=pltpu.CompilerParams(collective_id=1, has_side_effects=True, vmem_limit_bytes=60 << 20),
        name="reduce_gradients",
    )(*grads)


def adam_kernel(shapes, *refs):
    n = len(shapes)
    grads, means, squares, outs = refs[:n], refs[n:2 * n], refs[2 * n:3 * n], refs[3 * n:]
    for k, (rows, cols) in enumerate(shapes):
        change, mean, summed = outs[3 * k:3 * k + 3]
        if rows == 1:
            summed[...] = grads[k][...]
        else:
            rows_to_flat(grads[k], summed, rows, cols)
        change[...], mean[...] = adam(means[k][...], squares[k][...], summed[...])


def adam_all(grads, means, squares, shapes):
    vm = pl.BlockSpec(memory_space=pltpu.VMEM)
    return pl.pallas_call(
        functools.partial(adam_kernel, shapes),
        out_shape=[jax.ShapeDtypeStruct(((r * c) // 128, 128), F32) for r, c in shapes for _ in range(3)],
        in_specs=[vm] * (3 * len(shapes)),
        out_specs=[vm] * (3 * len(shapes)),
        name="adam",
    )(*grads, *means, *squares)


D = 512
HEADS = 8
HD = 64
FF = 2048
ROW = 1024
SEGS = 24
QT = 256
KT = 128
PAIR = 128
NEG = -1000000000.0


def dot(a, b):
    return jnp.dot(a, b, preferred_element_type=F32)


def dot_t(a, b):
    return lax.dot_general(a, b, (((1,), (1,)), ((), ())), preferred_element_type=F32)


def t_dot(a, b):
    return lax.dot_general(a, b, (((0,), (0,)), ((), ())), preferred_element_type=F32)


def for_rows(block, f, rows=ROW):
    def step(i, _):
        f(pl.ds(pl.multiple_of(i * block, block), block))
        return 0

    lax.fori_loop(0, rows // block, step, 0)


def ends_of(lengths):
    out, total = [], jnp.int32(0)
    for i in range(SEGS):
        total = total + lengths[0, i]
        out.append(total)
    return out


def seg_at(ends, place):
    count = jnp.int32(0)
    for e in ends:
        count = count + (e <= place).astype(jnp.int32)
    return count


def pick(values, index):
    out = values[-1]
    for i in range(len(values) - 2, -1, -1):
        out = jnp.where(index <= i, values[i], out)
    return out


def seg_row(ends):
    place = lax.broadcasted_iota(jnp.int32, (1, ROW), 1)
    out = jnp.zeros((1, ROW), jnp.int32)
    for e in ends:
        out = out + (place >= e).astype(jnp.int32)
    return out.astype(F32)


def store_seg(ends, row_ref, col_ref):
    row_ref[...] = jnp.broadcast_to(seg_row(ends), (8, ROW))
    for i in range(ROW // 128):
        block = jnp.broadcast_to(row_ref[0:1, i * 128:(i + 1) * 128], (128, 128))
        col_ref[i * 128:(i + 1) * 128, :] = jnp.transpose(block)


def ranges(query_ends, key_ends, causal, tile, other, by_query):
    out = []
    here, there = (query_ends, key_ends) if by_query else (key_ends, query_ends)
    starts = [jnp.int32(0)] + there[:-1]
    for i in range(ROW // tile):
        first, last = i * tile, (i + 1) * tile - 1
        low = pick(starts, seg_at(here, first)) // other
        high = (pick(there, seg_at(here, last)) + other - 1) // other
        if causal and by_query:
            high = jnp.int32((i + 1) * tile // other)
        if causal and not by_query:
            low = jnp.int32(i * tile // other)
        out.append((low, high))
    return out


def store_ranges(ref, base, pairs):
    for i, (low, high) in enumerate(pairs):
        ref[base + 2 * i] = low
        ref[base + 2 * i + 1] = high


def head_masks():
    lane = lax.broadcasted_iota(jnp.int32, (1, PAIR), 1)
    left = (lane < HD).astype(F32).astype(BF)
    return left, (1.0 - left.astype(F32)).astype(BF)


def stack_heads(block, masks):
    return jnp.concatenate([block * masks[0], block * masks[1]], 0)


def block_diag(pair_t):
    zero = jnp.zeros((HD, pair_t.shape[1]), pair_t.dtype)
    top = jnp.concatenate([pair_t[:HD], zero], 1)
    low = jnp.concatenate([zero, pair_t[HD:]], 1)
    return jnp.concatenate([top, low], 0)


def bias_tile(key_col, query_row, k0, q0, causal):
    keys = key_col[pl.ds(k0, KT), :]
    keys = jnp.concatenate([keys] * (QT // 128), 1)
    ok = keys == query_row[0:1, pl.ds(q0, QT)]
    if causal:
        kpos = k0 + lax.broadcasted_iota(jnp.int32, (KT, QT), 0)
        qpos = q0 + lax.broadcasted_iota(jnp.int32, (KT, QT), 1)
        ok = ok & (kpos <= qpos)
    return jnp.where(ok, 0.0, NEG)


def attend(q, k, vt, key_col, query_row, table, base, causal, out, lse, acc, peak, tally):
    masks = head_masks()

    def q_tile(i, _):
        q0 = pl.multiple_of(i * QT, QT)
        acc[...] = jnp.zeros_like(acc)
        peak[...] = jnp.full_like(peak, -3e38)
        tally[...] = jnp.zeros_like(tally)

        def k_tile(j, _):
            k0 = pl.multiple_of(j * KT, KT)
            bias = bias_tile(key_col, query_row, k0, q0, causal)
            peaks, tallies = [], []
            for hp in range(HEADS // 2):
                cols = slice(hp * PAIR, (hp + 1) * PAIR)
                s = dot_t(stack_heads(k[pl.ds(k0, KT), cols], masks), q[pl.ds(q0, QT), cols])
                probs, scales = [], []
                for side in range(2):
                    h = 2 * hp + side
                    sh = s[side * KT:(side + 1) * KT] + bias
                    old = peak[h:h + 1, :]
                    new = jnp.maximum(old, jnp.max(sh, 0, keepdims=True))
                    p = jnp.exp(sh - new)
                    scale = jnp.exp(old - new)
                    tallies.append(scale * tally[h:h + 1, :] + jnp.sum(p, 0, keepdims=True))
                    peaks.append(new)
                    probs.append(p.astype(BF))
                    scales.append(scale)
                o = dot(block_diag(vt[cols, pl.ds(k0, KT)]), jnp.concatenate(probs, 0))
                for side in range(2):
                    rows = slice(hp * PAIR + side * HD, hp * PAIR + (side + 1) * HD)
                    acc[rows, :] = acc[rows, :] * scales[side] + o[side * HD:(side + 1) * HD]
            peak[...] = jnp.concatenate(peaks, 0)
            tally[...] = jnp.concatenate(tallies, 0)
            return 0

        lax.fori_loop(table[base + 2 * i], table[base + 2 * i + 1], k_tile, 0)
        total = tally[...]
        lse[:, pl.ds(q0, QT)] = peak[...] + jnp.log(total)
        inverse = 1.0 / total
        for hp in range(HEADS // 2):
            rows = [acc[hp * PAIR + s * HD:hp * PAIR + (s + 1) * HD, :] * inverse[2 * hp + s:2 * hp + s + 1, :] for s in range(2)]
            out[pl.ds(q0, QT), hp * PAIR:(hp + 1) * PAIR] = jnp.transpose(jnp.concatenate(rows, 0)).astype(BF)
        return 0

    lax.fori_loop(0, ROW // QT, q_tile, 0)


def attend_back(q, k, v, kt, grad, lse, inner, key_col, query_row, table, base, causal, dqt, dk, dv, dk_acc, dv_acc):
    masks = head_masks()
    left = lax.broadcasted_iota(jnp.int32, (KT, PAIR), 1) < HD
    dqt[...] = jnp.zeros_like(dqt)

    def k_tile(j, _):
        k0 = pl.multiple_of(j * KT, KT)
        dk_acc[...] = jnp.zeros_like(dk_acc)
        dv_acc[...] = jnp.zeros_like(dv_acc)

        def q_tile(i, _):
            q0 = pl.multiple_of(i * QT, QT)
            bias = bias_tile(key_col, query_row, k0, q0, causal)
            for hp in range(HEADS // 2):
                cols = slice(hp * PAIR, (hp + 1) * PAIR)
                qp, gp = q[pl.ds(q0, QT), cols], grad[pl.ds(q0, QT), cols]
                s = dot_t(stack_heads(k[pl.ds(k0, KT), cols], masks), qp)
                dp = dot_t(stack_heads(v[pl.ds(k0, KT), cols], masks), gp)
                probs, slopes = [], []
                for side in range(2):
                    h = 2 * hp + side
                    rows = slice(side * KT, (side + 1) * KT)
                    p = jnp.exp(s[rows] + bias - lse[h:h + 1, pl.ds(q0, QT)])
                    slopes.append((p * (dp[rows] - inner[h:h + 1, pl.ds(q0, QT)])).astype(BF))
                    probs.append(p.astype(BF))
                probs, slopes = jnp.concatenate(probs, 0), jnp.concatenate(slopes, 0)
                to_v, to_k = dot(probs, gp), dot(slopes, qp)
                dv_acc[:, cols] += jnp.where(left, to_v[:KT], to_v[KT:])
                dk_acc[:, cols] += jnp.where(left, to_k[:KT], to_k[KT:])
                dqt[cols, pl.ds(q0, QT)] += dot(block_diag(kt[cols, pl.ds(k0, KT)]), slopes)
            return 0

        lax.fori_loop(table[base + 2 * j], table[base + 2 * j + 1], q_tile, 0)
        dk[pl.ds(k0, KT), :] = dk_acc[...].astype(BF)
        dv[pl.ds(k0, KT), :] = dv_acc[...].astype(BF)
        return 0

    lax.fori_loop(0, ROW // KT, k_tile, 0)


def normalize(r, xhat, rstd, at):
    centered = r - jnp.mean(r, -1, keepdims=True)
    spread = jnp.mean(centered * centered, -1, keepdims=True)
    scale = lax.rsqrt(spread + 1e-05)
    out = centered * scale
    xhat[at, :] = out
    rstd[at, :] = jnp.broadcast_to(scale, (out.shape[0], 128))
    return out


def norm_back(dh, xhat, rstd, gain):
    dx = dh * gain
    mean_dx = jnp.mean(dx, -1, keepdims=True)
    mean_xx = jnp.mean(dx * xhat, -1, keepdims=True)
    return rstd[:, 0:1] * (dx - mean_dx - xhat * mean_xx)


def fold(x):
    return jnp.sum(x.reshape(-1, 8, x.shape[-1]), 0)


def forward_kernel(
    tlen, slen, x, mem, win, wout, norms,
    q1, k1, v1, q2, k2, v2, c1, c2, lse1, lse2, xh1, rs1, xh2, rs2,
    trow, tcol, scol, table, vt, acc, peak, tally,
):
    tends, sends = ends_of(tlen), ends_of(slen)
    store_seg(tends, trow, tcol)
    store_seg(sends, trow, scol)
    trow[...] = jnp.broadcast_to(seg_row(tends), (8, ROW))
    store_ranges(table, 0, ranges(tends, tends, True, QT, KT, True))
    store_ranges(table, 8, ranges(tends, sends, False, QT, KT, True))

    def project(at):
        for out, src, w in ((q1, x, 0), (k1, x, 1), (v1, x, 2), (k2, mem, 4), (v2, mem, 5)):
            y = dot(src[at, :], win[w * D:(w + 1) * D, :]).astype(BF)
            out[at, :] = y * BF(0.125) if w == 0 else y

    for_rows(256, project)

    def flip(v):
        for i in range(ROW // 128):
            vt[:, i * 128:(i + 1) * 128] = jnp.transpose(v[i * 128:(i + 1) * 128, :])

    flip(v1)
    attend(q1, k1, vt, tcol, trow, table, 0, True, c1, lse1, acc, peak, tally)

    def middle(at):
        r = x[at, :].astype(F32) + dot(c1[at, :], wout[0:D, :])
        h = normalize(r, xh1, rs1, at) * norms[0:1, :] + norms[3:4, :]
        q2[at, :] = dot(h.astype(BF), win[3 * D:4 * D, :]).astype(BF) * BF(0.125)

    for_rows(256, middle)
    flip(v2)
    attend(q2, k2, vt, scol, trow, table, 8, False, c2, lse2, acc, peak, tally)

    def end(at):
        h = xh1[at, :] * norms[0:1, :] + norms[3:4, :]
        normalize(h + dot(c2[at, :], wout[D:2 * D, :]), xh2, rs2, at)

    for_rows(256, end)


def ffn_kernel(tlen, xh2, cot, up, down, norms, result, dh2, gup, gdown, gnorm, h2b, act, du, dy, pre):
    live_end = ends_of(tlen)[SEGS - 2]
    gnorm[...] = jnp.zeros_like(gnorm)
    block = 256

    def rows(i, _):
        at = pl.ds(pl.multiple_of(i * block, block), block)
        h = xh2[at, :] * norms[1:2, :] + norms[4:5, :]
        hb = h.astype(BF)
        h2b[at, :] = hb
        r3 = h
        for j in range(FF // D):
            cols = slice(j * D, (j + 1) * D)
            u = dot(hb, up[:, cols])
            pre[:, cols] = u
            a = (u / (1.0 + jnp.exp(-u))).astype(BF)
            act[at, cols] = a
            r3 = r3 + dot(a, down[cols, :])
        centered = r3 - jnp.mean(r3, -1, keepdims=True)
        spread = jnp.mean(centered * centered, -1, keepdims=True)
        rstd = lax.rsqrt(spread + 1e-05)
        xhat = centered * rstd
        result[at, :] = (xhat * norms[2:3, :] + norms[5:6, :]).astype(BF)
        place = i * block + lax.broadcasted_iota(jnp.int32, (block, D), 0)
        seed = jnp.where(place < live_end, cot[at, :].astype(F32), 0.0)
        gnorm[0:8, :] += fold(seed * xhat)
        gnorm[8:16, :] += fold(seed)
        dr3 = norm_back(seed, xhat, rstd, norms[2:3, :])
        dyb = dr3.astype(BF)
        dy[at, :] = dyb
        dh = dr3
        for j in range(FF // D):
            cols = slice(j * D, (j + 1) * D)
            da = dot_t(dyb, down[cols, :])
            u = pre[:, cols]
            sig = 1.0 / (1.0 + jnp.exp(-u))
            d = (da * (sig * (1.0 + u * (1.0 - sig)))).astype(BF)
            du[at, cols] = d
            dh = dh + dot_t(d, up[:, cols])
        dh2[at, :] = dh
        return 0

    lax.fori_loop(0, ROW // block, rows, 0)
    for j in range(FF // D):
        cols = slice(j * D, (j + 1) * D)
        gdown[cols, :] = t_dot(act[:, cols], dy[...]).astype(BF)
        gup[:, cols] = t_dot(h2b[...], du[:, cols]).astype(BF)


def backward_kernel(
    tlen, slen, x, mem, win, wout, norms, q1, k1, v1, q2, k2, v2, c1, c2, lse1, lse2, xh1, rs1, xh2, rs2, dh2,
    tgrad, mgrad, gin, gout, gnorm,
    trow, tcol, scol, table, kt, dc, h1b, inner, dqt, dq, dk, dv, dk_acc, dv_acc, dr,
):
    tends, sends = ends_of(tlen), ends_of(slen)
    store_seg(tends, trow, tcol)
    store_seg(sends, trow, scol)
    trow[...] = jnp.broadcast_to(seg_row(tends), (8, ROW))
    store_ranges(table, 0, ranges(tends, tends, True, KT, QT, False))
    store_ranges(table, 16, ranges(tends, sends, False, KT, QT, False))
    gnorm[...] = jnp.zeros_like(gnorm)
    heads = (lax.broadcasted_iota(jnp.int32, (HEADS, D), 1) // HD == lax.broadcasted_iota(jnp.int32, (HEADS, D), 0))
    heads = heads.astype(F32).astype(BF)

    def into_attention(at, r, w, c):
        g = dot_t(r.astype(BF), wout[w * D:(w + 1) * D, :]).astype(BF)
        dc[at, :] = g
        both = g.astype(F32) * c[at, :].astype(F32)
        high = both.astype(BF)
        low = (both - high.astype(F32)).astype(BF)
        inner[:, at] = dot_t(heads, high) + dot_t(heads, low)

    def flip(k):
        for i in range(ROW // 128):
            kt[:, i * 128:(i + 1) * 128] = jnp.transpose(k[i * 128:(i + 1) * 128, :])

    def queries_back(at):
        dq[at, :] = jnp.transpose(dqt[:, at] * 0.125).astype(BF)

    def first(at):
        dh, xhat = dh2[at, :], xh2[at, :]
        gnorm[0:8, :] += fold(dh * xhat)
        gnorm[8:16, :] += fold(dh)
        r = norm_back(dh, xhat, rs2[at, :], norms[1:2, :])
        dr[at, :] = r
        h1b[at, :] = (xh1[at, :] * norms[0:1, :] + norms[3:4, :]).astype(BF)
        into_attention(at, r, 1, c2)

    for_rows(256, first)
    gout[D:2 * D, :] = t_dot(c2[...], dr[...].astype(BF)).astype(BF)
    flip(k2)
    attend_back(q2, k2, v2, kt, dc, lse2, inner, scol, trow, table, 16, False, dqt, dk, dv, dk_acc, dv_acc)
    for_rows(256, queries_back)
    gin[3 * D:4 * D, :] = t_dot(h1b[...], dq[...]).astype(BF)
    gin[4 * D:5 * D, :] = t_dot(mem[...], dk[...]).astype(BF)
    gin[5 * D:6 * D, :] = t_dot(mem[...], dv[...]).astype(BF)

    def second(at):
        mgrad[at, :] = dot_t(dk[at, :], win[4 * D:5 * D, :]) + dot_t(dv[at, :], win[5 * D:6 * D, :])
        dh = dr[at, :] + dot_t(dq[at, :], win[3 * D:4 * D, :])
        xhat = xh1[at, :]
        gnorm[16:24, :] += fold(dh * xhat)
        gnorm[24:32, :] += fold(dh)
        r = norm_back(dh, xhat, rs1[at, :], norms[0:1, :])
        dr[at, :] = r
        into_attention(at, r, 0, c1)

    for_rows(256, second)
    gout[0:D, :] = t_dot(c1[...], dr[...].astype(BF)).astype(BF)
    flip(k1)
    attend_back(q1, k1, v1, kt, dc, lse1, inner, tcol, trow, table, 0, True, dqt, dk, dv, dk_acc, dv_acc)
    for_rows(256, queries_back)
    for i, g in enumerate((dq, dk, dv)):
        gin[i * D:(i + 1) * D, :] = t_dot(x[...], g[...]).astype(BF)

    def third(at):
        t = dr[at, :]
        for i, g in enumerate((dq, dk, dv)):
            t = t + dot_t(g[at, :], win[i * D:(i + 1) * D, :])
        tgrad[at, :] = t

    for_rows(256, third)


VM = pl.BlockSpec(memory_space=pltpu.VMEM)
SM = pl.BlockSpec(memory_space=pltpu.SMEM)


def call(kernel, name, ins, outs, scratch, scalars):
    return pl.pallas_call(
        kernel,
        out_shape=[jax.ShapeDtypeStruct(s, d) for s, d in outs],
        in_specs=[SM] * scalars + [VM] * (len(ins) - scalars),
        out_specs=[VM] * len(outs),
        scratch_shapes=scratch,
        compiler_params=pltpu.CompilerParams(vmem_limit_bytes=62 << 20),
        name=name,
    )(*ins)


def layer(tlen, slen, x, mem, cot, win, wout, up, down, norms):
    tok, tokf, stat, rep = ((ROW, D), BF), ((ROW, D), F32), ((HEADS, ROW), F32), ((ROW, 128), F32)
    segs = [pltpu.VMEM((8, ROW), F32), pltpu.VMEM((ROW, 128), F32), pltpu.VMEM((ROW, 128), F32), pltpu.SMEM((32,), jnp.int32)]
    kept = call(
        forward_kernel, "forward", [tlen, slen, x, mem, win, wout, norms],
        [tok] * 8 + [stat] * 2 + [tokf, rep] * 2,
        segs + [pltpu.VMEM((D, ROW), BF), pltpu.VMEM((D, QT), F32), pltpu.VMEM((HEADS, QT), F32), pltpu.VMEM((HEADS, QT), F32)],
        2,
    )
    xh2 = kept[12]
    result, dh2, gup, gdown, gnorm_three = call(
        ffn_kernel, "feed_forward", [tlen, xh2, cot, up, down, norms],
        [tok, tokf, ((D, FF), BF), ((FF, D), BF), ((16, D), F32)],
        [pltpu.VMEM((ROW, D), BF), pltpu.VMEM((ROW, FF), BF), pltpu.VMEM((ROW, FF), BF), pltpu.VMEM((ROW, D), BF), pltpu.VMEM((256, FF), F32)],
        1,
    )
    tgrad, mgrad, gin, gout, gnorm_rest = call(
        backward_kernel, "backward", [tlen, slen, x, mem, win, wout, norms, *kept, dh2],
        [tokf, tokf, ((6 * D, D), BF), ((2 * D, D), BF), ((32, D), F32)],
        segs + [pltpu.VMEM((D, ROW), BF), pltpu.VMEM((ROW, D), BF), pltpu.VMEM((ROW, D), BF), pltpu.VMEM((HEADS, ROW), F32),
                pltpu.VMEM((D, ROW), F32)] + [pltpu.VMEM((ROW, D), BF)] * 3 + [pltpu.VMEM((KT, D), F32)] * 2 + [pltpu.VMEM((ROW, D), F32)],
        2,
    )
    three = jnp.sum(gnorm_three.reshape(2, 8, D), 1)
    rest = jnp.sum(gnorm_rest.reshape(4, 8, D), 1)
    gnorm = jnp.stack([rest[2], rest[0], three[0], rest[3], rest[1], three[1]])
    return result, tgrad, mgrad, gin, gout, gup, gdown, gnorm


def shard_views(inward, outward, expand, shrink, norms):
    arrays, shapes = [], []
    for x, wide in ((inward, D), (outward, D), (expand, FF), (shrink, D)):
        cols = wide if x.shape[0] >= 16 * wide else D
        arrays.append(x.reshape(-1, 128))
        shapes.append((x.shape[0] // cols, cols))
    width = -(-norms.shape[0] // 128) * 128
    arrays.append(jnp.pad(norms, (0, width - norms.shape[0])).reshape(1, width))
    shapes.append((1, width))
    return arrays, tuple(shapes)


def body(
    sizes, target, memory, cotangent, target_lengths, source_lengths,
    inward_master, inward_mean, inward_square, outward_master, outward_mean, outward_square,
    expand_master, expand_mean, expand_square, shrink_master, shrink_mean, shrink_square,
    norms_master, norms_mean, norms_square,
):
    flat, shapes = shard_views(inward_master, outward_master, expand_master, shrink_master, norms_master)
    win, wout, up, down, norms = gather_all(sizes, flat, shapes, [BF, BF, BF, BF, F32])
    norm_count = norms_master.shape[0]
    norms = norms.reshape(-1, norms.shape[-1])[:, :norm_count].reshape(6, D)
    result, tgrad, mgrad, gin, gout, gup, gdown, gnorm = layer(
        target_lengths, source_lengths, target[0], memory[0], cotangent[0],
        win.reshape(6 * D, D), wout.reshape(2 * D, D), up.reshape(D, FF), down.reshape(FF, D), norms,
    )
    gnorm = jnp.pad(gnorm.reshape(-1, norm_count), ((0, 0), (0, shapes[4][1] - norm_count)))
    grads = [g.reshape(*sizes, *s) for g, s in zip((gin, gout, gup, gdown, gnorm), shapes)]
    means, _ = shard_views(inward_mean, outward_mean, expand_mean, shrink_mean, norms_mean)
    squares, _ = shard_views(inward_square, outward_square, expand_square, shrink_square, norms_square)
    sums = reduce_all(sizes, grads, shapes)
    outs = [x.reshape(-1) for x in adam_all(sums, means, squares, shapes)]
    return (result[None], tgrad[None], mgrad[None], *outs[:12], *[x[:norm_count] for x in outs[12:]])


def solution(mesh):
    rows, cols = mesh.shape["dp"], mesh.shape["shard"]
    both = ("dp", "shard")
    row, flat = P(both, None, None), P(both)
    return jax.shard_map(
        functools.partial(body, (rows // 2, 2, cols // 2, 2)),
        mesh=mesh,
        in_specs=(row, row, row, P(both, None), P(both, None), *[flat] * 15),
        out_specs=(row, row, row, *[flat] * 15),
        check_vma=False,
    )
```

```python
import functools
import jax
import jax.numpy as jnp
from jax import lax
from jax.experimental import pallas as pl
from jax.experimental.pallas import tpu as pltpu
from jax.sharding import PartitionSpec as P

MESH = pl.DeviceIdType.MESH
BF = jnp.bfloat16
F32 = jnp.float32
learn_rate = 0.001
beta_one = 0.9
beta_two = 0.999
STEP = 10


class Place:
    def __init__(self, sizes):
        self.sizes = sizes
        dp, sh = lax.axis_index("dp"), lax.axis_index("shard")
        self.at = (dp // sizes[1], dp % sizes[1], sh // sizes[3], sh % sizes[3])

    def device(self, axis, coord):
        a, b, c, e = [coord if i == axis else v for i, v in enumerate(self.at)]
        return (a * self.sizes[1] + b, c * self.sizes[3] + e)

    def greet(self, far=False):
        barrier = pltpu.get_barrier_semaphore()
        count = 0
        for axis in range(4):
            n, me = self.sizes[axis], self.at[axis]
            if n == 2:
                pl.semaphore_signal(barrier, inc=1, device_id=self.device(axis, 1 - me), device_id_type=MESH)
                count = count + 1
            else:
                for step in [s for d in range(1, n if far else 2) for s in (-d, d)]:
                    there = me + step
                    ok = (there >= 0) & (there < n)

                    @pl.when(ok)
                    def _():
                        pl.semaphore_signal(barrier, inc=1, device_id=self.device(axis, there), device_id_type=MESH)

                    count = count + ok.astype(jnp.int32)
        pl.semaphore_wait(barrier, count)


class Sems:
    def __init__(self, send, recv):
        self.send, self.recv, self.used = send, recv, 0

    def take(self):
        k = self.used
        self.used += 1
        return self.send.at[k], self.recv.at[k]


def gather_sems(order, sizes):
    return 1 + sum(2 if sizes[x] == 2 else 4 * (sizes[x] - 1) for x in order)


def gather_rounds(place, ref, order, sems):
    sizes = place.sizes
    after = []
    held = []

    def group(axis=None, coord=None):
        idx = [slice(None) if i in held else place.at[i] for i in range(4)]
        if axis is not None:
            idx[axis] = coord
        return ref.at[tuple(idx)]

    def copy(block, axis, coord, pair):
        return pltpu.make_async_remote_copy(
            src_ref=block, dst_ref=block, send_sem=pair[0], recv_sem=pair[1],
            device_id=place.device(axis, coord), device_id_type=MESH)

    def to_sibling(axis, coord, cond):
        pair = sems.take()
        idx = [slice(None) if i in held else place.at[i] for i in range(4)]
        if axis is not None:
            idx[axis] = coord
        mine = ref.at[tuple(idx)]
        idx[3] = 1 - place.at[3]
        theirs = ref.at[tuple(idx)]
        e = place.at[3]
        go = copy(mine, 3, 1 - e, pair)
        come = copy(theirs, 3, 1 - e, pair)

        def run(f):
            if cond is None:
                f()
            else:
                pl.when(cond)(f)

        run(go.start)

        def finish():
            go.wait_send()
            come.wait_recv()

        after.append(lambda: run(finish))

    to_sibling(None, None, None)
    for axis in order:
        n, me = sizes[axis], place.at[axis]
        if n == 2:
            pair = sems.take()
            go = copy(group(), axis, 1 - me, pair)
            come = copy(group(axis, 1 - me), axis, 1 - me, pair)
            go.start()
            after.append(go.wait_send)
            yield
            come.wait_recv()
            to_sibling(axis, 1 - me, None)
        else:
            for t in range(1, n):
                pending = []
                for step in (1, -1):
                    pair = sems.take()
                    out_c, in_c, to = me - step * (t - 1), me - step * t, me + step
                    can = (out_c >= 0) & (out_c < n) & (to >= 0) & (to < n)
                    gets = (in_c >= 0) & (in_c < n)
                    go = copy(group(axis, out_c), axis, to, pair)
                    come = copy(group(axis, in_c), axis, to, pair)
                    pl.when(can)(go.start)
                    after.append(lambda go=go, can=can: pl.when(can)(go.wait_send))
                    pending.append((come, gets, in_c))
                yield
                for come, gets, in_c in pending:
                    pl.when(gets)(come.wait_recv)
                    to_sibling(axis, in_c, gets)
        held.append(axis)
    yield
    for f in after:
        f()


def interleave(rounds):
    live = list(rounds)
    while live:
        still = []
        for r in live:
            try:
                next(r)
                still.append(r)
            except StopIteration:
                pass
        live = still


def flat_to_rows(src, dst, rows, cols):
    w = cols // 128
    for j in range(w):
        dst[:, j * 128:(j + 1) * 128] = src[pl.ds(j, rows, stride=w), :].astype(dst.dtype)


def rows_to_flat(value, dst, rows, cols):
    w = cols // 128
    for j in range(w):
        dst[pl.ds(j, rows, stride=w), :] = value[:, j * 128:(j + 1) * 128]


def both(a, b):
    return b if a is None else a if b is None else a & b


def when(cond, f):
    if cond is None:
        f()
    else:
        pl.when(cond)(f)


def remote(src, dst, pair, device):
    return pltpu.make_async_remote_copy(
        src_ref=src, dst_ref=dst, send_sem=pair[0], recv_sem=pair[1], device_id=device, device_id_type=MESH)


ORDERS = ((0, 2, 1), (0, 1, 2), (1, 2, 0), (0, 1, 2), (0, 1, 2))


def gather_kernel(sizes, shapes, *refs):
    n = len(shapes)
    masters, outs = refs[:n], refs[n:2 * n]
    stage, local, send, recv = refs[2 * n:3 * n], refs[3 * n], refs[3 * n + 1], refs[3 * n + 2]
    place = Place(sizes)
    copies = []
    for k, (rows, cols) in enumerate(shapes):
        if rows == 1:
            stage[k][...] = masters[k][...].astype(BF).astype(stage[k].dtype)
        else:
            flat_to_rows(masters[k], stage[k], rows, cols)
        cp = pltpu.make_async_copy(stage[k], outs[k].at[place.at], local.at[k])
        cp.start()
        copies.append(cp)
    place.greet()
    for cp in copies:
        cp.wait()
    sems = Sems(send, recv)
    interleave([gather_rounds(place, outs[k], ORDERS[k], sems) for k in range(n)])


def gather_all(mesh_sizes, masters, shapes, dtypes):
    n = len(shapes)
    total = sum(gather_sems(ORDERS[k], mesh_sizes) for k in range(n))
    vm = pl.BlockSpec(memory_space=pltpu.VMEM)
    return pl.pallas_call(
        functools.partial(gather_kernel, mesh_sizes, shapes),
        out_shape=[jax.ShapeDtypeStruct((*mesh_sizes, *s), d) for s, d in zip(shapes, dtypes)],
        in_specs=[vm] * n,
        out_specs=[pl.BlockSpec(memory_space=pl.ANY)] * n,
        scratch_shapes=[pltpu.VMEM(s, d) for s, d in zip(shapes, dtypes)]
        + [pltpu.SemaphoreType.DMA((n,)), pltpu.SemaphoreType.DMA((total,)), pltpu.SemaphoreType.DMA((total,))],
        compiler_params=pltpu.CompilerParams(collective_id=0, has_side_effects=True, vmem_limit_bytes=48 << 20),
        name="gather_weights",
    )(*masters)


def reduce_sems(order, sizes):
    return 1 + sum(1 if sizes[x] == 2 else 2 * (sizes[x] - 1) for x in order)


def reduce_rounds(place, grad, order, got, bufs, total, sems):
    sizes = place.sizes
    after = []
    e = place.at[3]

    def rdma(src, dst, axis, coord, pair):
        return pltpu.make_async_remote_copy(
            src_ref=src, dst_ref=dst, send_sem=pair[0], recv_sem=pair[1],
            device_id=place.device(axis, coord), device_id_type=MESH)

    def add_into(dst, src):
        dst[...] = (dst[...].astype(F32) + src[...].astype(F32)).astype(dst.dtype)

    def each(dims, f):
        count = 1
        for d in dims:
            count *= d
        if count == 1:
            f(tuple(0 for _ in dims))
            return

        def step(i, _):
            idx = []
            for d in reversed(dims):
                idx.append(i % d)
                i = i // d
            f(tuple(reversed(idx)))
            return 0

        lax.fori_loop(0, count, step, 0)

    cp = rdma(grad.at[:, :, :, 1 - e], got, 3, 1 - e, sems.take())
    cp.start()
    yield
    cp.wait()
    each(sizes[:3], lambda i: add_into(got.at[i], grad.at[(*i, e)]))
    cur, left = got, [0, 1, 2]
    for axis, buf in zip(order, bufs):
        n, me = sizes[axis], place.at[axis]
        pos = left.index(axis)
        rest = [x for x in left if x != axis]
        dims = [sizes[x] for x in rest]

        def part(ref, coord):
            return ref.at[tuple(coord if i == pos else slice(None) for i in range(len(left)))]

        def one(ref, coord, i):
            i = list(i)
            i.insert(pos, coord)
            return ref.at[tuple(i)]

        last = not rest
        if n == 2:
            cp = rdma(part(cur, 1 - me), buf, axis, 1 - me, sems.take())
            cp.start()
            yield
            cp.wait()
            if last:
                total[...] = buf[...].astype(F32) + cur[me].astype(F32)
            else:
                each(dims, lambda i: add_into(buf.at[i], one(cur, me, i)))
        else:
            for t in range(n - 1):
                for way, step in enumerate((1, -1)):
                    j = n - 1 - t if step == 1 else t
                    to, back = me + step, me - step
                    ahead = (j > me) if step == 1 else (j < me)
                    gets = ahead & (back >= 0) & (back < n)
                    pair = sems.take()
                    come = rdma(part(cur, j), buf.at[way, j], axis, to, pair)

                    @pl.when(gets)
                    def _():
                        come.wait_recv()
                        each(dims, lambda i: add_into(one(cur, j, i), buf.at[(way, j, *i)]))

                    pl.when(ahead)(come.start)
                    after.append(lambda come=come, ahead=ahead: pl.when(ahead)(come.wait_send))
                    ends = (j == me) & (back >= 0) & (back < n)
                    after.append(lambda come=come, ends=ends: pl.when(ends)(come.wait_recv))
                yield
            for f in after:
                f()
            after = []
            keep = buf.at[0, me]

            def close(i):
                mine = one(cur, me, i)[...].astype(F32)
                v = mine + jnp.where(me > 0, buf[(0, me, *i)].astype(F32), 0.0)
                v = v + jnp.where(me < n - 1, buf[(1, me, *i)].astype(F32), 0.0)
                if last:
                    total[...] = v
                else:
                    buf[(0, me, *i)] = v.astype(buf.dtype)

            each(dims, close)
            buf = keep
        cur, left = buf, rest
    for f in after:
        f()


def reduce_bufs(order, sizes, shape):
    left, out = [0, 1, 2], [(*sizes[:3], *shape)]
    for axis in order:
        rest = [x for x in left if x != axis]
        dims = tuple(sizes[x] for x in rest)
        out.append((*dims, *shape) if sizes[axis] == 2 else (2, sizes[axis], *dims, *shape))
        left = rest
    return out


BACK = tuple(tuple(reversed(o)) for o in ORDERS)


def adam(mean_old, square_old, grad):
    mean_new = beta_one * mean_old + (1.0 - beta_one) * grad
    square_new = beta_two * square_old + (1.0 - beta_two) * grad * grad
    steps = float(STEP)
    mean_hat = mean_new / (1.0 - beta_one**steps)
    square_hat = square_new / (1.0 - beta_two**steps)
    return -learn_rate * mean_hat / (jnp.sqrt(square_hat) + 1e-08), mean_new


def reduce_kernel(sizes, shapes, counts, *refs):
    n = len(shapes)
    refs = list(refs)

    def take(k):
        out = refs[:k]
        del refs[:k]
        return out

    grads, totals = take(n), take(n)
    bufs = [take(c) for c in counts]
    send, recv = take(2)
    place = Place(sizes)
    place.greet()
    sems = Sems(send, recv)
    interleave([reduce_rounds(place, grads[k], BACK[k], bufs[k][0], bufs[k][1:], totals[k], sems) for k in range(n)])


def reduce_all(mesh_sizes, grads, shapes):
    n = len(shapes)
    lists = [reduce_bufs(BACK[k], mesh_sizes, shapes[k]) for k in range(n)]
    total = sum(reduce_sems(BACK[k], mesh_sizes) for k in range(n))
    vm = pl.BlockSpec(memory_space=pltpu.VMEM)
    scratch = []
    for k in range(n):
        scratch += [pltpu.VMEM(s, grads[k].dtype) for s in lists[k]]
    scratch += [pltpu.SemaphoreType.DMA((total,)), pltpu.SemaphoreType.DMA((total,))]
    return pl.pallas_call(
        functools.partial(reduce_kernel, mesh_sizes, shapes, [len(x) for x in lists]),
        out_shape=[jax.ShapeDtypeStruct(s, F32) for s in shapes],
        in_specs=[vm] * n,
        out_specs=[vm] * n,
        scratch_shapes=scratch,
        compiler_params=pltpu.CompilerParams(collective_id=1, has_side_effects=True, vmem_limit_bytes=60 << 20),
        name="reduce_gradients",
    )(*grads)


def adam_kernel(shapes, rows_in, *refs):
    n = len(shapes)
    grads, means, squares = refs[:n], refs[n:2 * n], refs[2 * n:3 * n]
    rows_out, outs, (held, sem) = refs[3 * n], refs[3 * n + 1:-2], refs[-2:]
    cp = pltpu.make_async_copy(rows_in, held, sem.at[0])
    cp.start()
    for k, (rows, cols) in enumerate(shapes):
        change, mean, summed = outs[3 * k:3 * k + 3]
        if rows == 1:
            summed[...] = grads[k][:, 0:cols]
        else:
            rows_to_flat(grads[k], summed, rows, cols)
        change[...], mean[...] = adam(means[k][...], squares[k][...], summed[...])
        if k == 0:
            cp.wait()
            cp = pltpu.make_async_copy(held, rows_out, sem.at[1])
            cp.start()
    cp.wait()


def adam_all(rows, grads, means, squares, shapes):
    vm, hb = pl.BlockSpec(memory_space=pltpu.VMEM), pl.BlockSpec(memory_space=pltpu.HBM)
    flat = [((r * c) // 128, 128) if r > 1 else (1, c) for r, c in shapes]
    return pl.pallas_call(
        functools.partial(adam_kernel, shapes),
        out_shape=[jax.ShapeDtypeStruct(rows.shape, F32)] + [jax.ShapeDtypeStruct(f, F32) for f in flat for _ in range(3)],
        in_specs=[hb] + [vm] * (3 * len(shapes)),
        out_specs=[hb] + [vm] * (3 * len(shapes)),
        scratch_shapes=[pltpu.VMEM(rows.shape, F32), pltpu.SemaphoreType.DMA((2,))],
        name="adam",
    )(rows, *grads, *means, *squares)

D = 512
HEADS = 8
HD = 64
FF = 2048
ROW = 1024
SEGS = 24
MOST = 512
QT = 256
KT = 128
PAIR = 128
NEG = -1000000000.0


def dot(a, b):
    return jnp.dot(a, b, preferred_element_type=F32)


def dot_t(a, b):
    return lax.dot_general(a, b, (((1,), (1,)), ((), ())), preferred_element_type=F32)


def t_dot(a, b):
    return lax.dot_general(a, b, (((0,), (0,)), ((), ())), preferred_element_type=F32)


def for_rows(block, f, rows=ROW):
    def step(i, _):
        f(pl.ds(pl.multiple_of(i * block, block), block))
        return 0

    lax.fori_loop(0, rows // block, step, 0)


def ends_of(lengths):
    out, total = [], jnp.int32(0)
    for i in range(SEGS):
        total = total + lengths[0, i]
        out.append(total)
    return out


def seg_at(ends, place):
    count = jnp.int32(0)
    for e in ends:
        count = count + (e <= place).astype(jnp.int32)
    return count


def pick(values, index):
    out = values[-1]
    for i in range(len(values) - 2, -1, -1):
        out = jnp.where(index <= i, values[i], out)
    return out


def seg_row(ends):
    place = lax.broadcasted_iota(jnp.int32, (1, ROW), 1)
    out = jnp.zeros((1, ROW), jnp.int32)
    for e in ends:
        out = out + (place >= e).astype(jnp.int32)
    return out.astype(F32)


def store_seg(ends, row_ref, col_ref):
    row_ref[...] = jnp.broadcast_to(seg_row(ends), (8, ROW))
    for i in range(ROW // 128):
        block = jnp.broadcast_to(row_ref[0:1, i * 128:(i + 1) * 128], (128, 128))
        col_ref[i * 128:(i + 1) * 128, :] = jnp.transpose(block)


def ranges(query_ends, key_ends, causal, tile, other, by_query):
    out = []
    here, there = (query_ends, key_ends) if by_query else (key_ends, query_ends)
    starts = [jnp.int32(0)] + there[:-1]
    for i in range(ROW // tile):
        first, last = i * tile, (i + 1) * tile - 1
        low = pick(starts, seg_at(here, first)) // other
        high = (pick(there, seg_at(here, last)) + other - 1) // other
        if causal and by_query:
            high = jnp.int32((i + 1) * tile // other)
        if causal and not by_query:
            low = jnp.int32(i * tile // other)
        out.append((low, high))
    return out


def store_ranges(ref, base, pairs):
    for i, (low, high) in enumerate(pairs):
        ref[base + 2 * i] = low
        ref[base + 2 * i + 1] = high


def head_masks():
    lane = lax.broadcasted_iota(jnp.int32, (1, PAIR), 1)
    left = (lane < HD).astype(F32).astype(BF)
    return left, (1.0 - left.astype(F32)).astype(BF)


def stack_heads(block, masks):
    return jnp.concatenate([block * masks[0], block * masks[1]], 0)


def block_diag(pair_t):
    zero = jnp.zeros((HD, pair_t.shape[1]), pair_t.dtype)
    top = jnp.concatenate([pair_t[:HD], zero], 1)
    low = jnp.concatenate([zero, pair_t[HD:]], 1)
    return jnp.concatenate([top, low], 0)


def bias_tile(key_col, query_row, k0, q0, causal):
    keys = key_col[pl.ds(k0, KT), :]
    keys = jnp.concatenate([keys] * (QT // 128), 1)
    ok = keys == query_row[0:1, pl.ds(q0, QT)]
    if causal:
        kpos = k0 + lax.broadcasted_iota(jnp.int32, (KT, QT), 0)
        qpos = q0 + lax.broadcasted_iota(jnp.int32, (KT, QT), 1)
        ok = ok & (kpos <= qpos)
    return jnp.where(ok, 0.0, NEG)


def norm_back(dh, xhat, rstd, gain):
    dx = dh * gain
    mean_dx = jnp.mean(dx, -1, keepdims=True)
    mean_xx = jnp.mean(dx * xhat, -1, keepdims=True)
    return rstd[:, 0:1] * (dx - mean_dx - xhat * mean_xx)


def fold(x):
    return jnp.sum(x.reshape(-1, 8, x.shape[-1]), 0)


def pipeline(count, *stages):
    values = {}
    last = len(stages) - 1
    for tick in range(count + last):
        for i in reversed(range(count)):
            st = tick - i
            if 0 <= st <= last:
                values[i] = stages[st](i) if st == 0 else stages[st](i, values[i])


def columns(hp):
    return slice(hp * PAIR, (hp + 1) * PAIR)


def score_tile(k0, q0, q, k, key_col, query_row, causal, scores, peak, masks):
    bias = bias_tile(key_col, query_row, k0, q0, causal)

    def meet(hp):
        return dot_t(stack_heads(k[pl.ds(k0, KT), columns(hp)], masks), q[pl.ds(q0, QT), columns(hp)])

    def keep(hp, s):
        for side in range(2):
            h = 2 * hp + side
            sh = s[side * KT:(side + 1) * KT] + bias
            scores[hp][pl.ds(k0, KT), side * QT:(side + 1) * QT] = sh
            peak[h] = jnp.maximum(peak[h], jnp.max(sh.reshape(KT // 8, 8, QT), 0))

    pipeline(HEADS // 2, meet, keep)


def weigh_tile(k0, vt, scores, acc, peak, tally):
    def weigh(hp):
        probs = []
        for side in range(2):
            h = 2 * hp + side
            sh = scores[hp][pl.ds(k0, KT), side * QT:(side + 1) * QT]
            p = jnp.exp(sh.reshape(KT // 8, 8, QT) - peak[h][None])
            tally[h] += jnp.sum(p, 0)
            probs.append(p.reshape(KT, QT).astype(BF))
        return jnp.concatenate(probs, 0)

    def spread(hp, probs):
        return dot(block_diag(vt[columns(hp), pl.ds(k0, KT)]), probs)

    def add(hp, o):
        acc[columns(hp), :] += o

    pipeline(HEADS // 2, weigh, spread, add)


def attend(tile, span, q, k, vt, key_col, query_row, causal, out, lse, scores, acc, peak, tally, pump=None):
    masks = head_masks()
    q0 = pl.multiple_of(tile * QT, QT) if not isinstance(tile, int) else tile * QT
    first, end = span
    peak[...] = jnp.full_like(peak, -3e38)

    def score(j, _):
        score_tile(pl.multiple_of(j * KT, KT), q0, q, k, key_col, query_row, causal, scores, peak, masks)
        return 0

    lax.fori_loop(first, end, score, 0)
    if pump:
        pump()
    for h in range(HEADS):
        peak[h] = jnp.broadcast_to(jnp.max(peak[h], 0, keepdims=True), (8, QT))
    acc[...] = jnp.zeros_like(acc)
    tally[...] = jnp.zeros_like(tally)

    def weigh(j, _):
        weigh_tile(pl.multiple_of(j * KT, KT), vt, scores, acc, peak, tally)
        return 0

    lax.fori_loop(first, end, weigh, 0)
    if pump:
        pump()
    for hp in range(HEADS // 2):
        rows = []
        for side in range(2):
            h = 2 * hp + side
            total = jnp.sum(tally[h], 0, keepdims=True)
            lse[h:h + 1, pl.ds(q0, QT)] = peak[h, 0:1, :] + jnp.log(total)
            rows.append(acc[hp * PAIR + side * HD:hp * PAIR + (side + 1) * HD, :] * (1.0 / total))
        out[pl.ds(q0, QT), hp * PAIR:(hp + 1) * PAIR] = jnp.transpose(jnp.concatenate(rows, 0)).astype(BF)


def attend_back(tile, span, k, v, kt, qt, gt, lse, inner, key_col, query_row, causal, dqt, dk, dv, dk_acc, dv_acc):
    masks = head_masks()
    k0 = pl.multiple_of(tile * KT, KT) if not isinstance(tile, int) else tile * KT
    dk_acc[...] = jnp.zeros_like(dk_acc)
    dv_acc[...] = jnp.zeros_like(dv_acc)

    def step(i, _):
        q0 = pl.multiple_of(i * QT, QT)
        bias = bias_tile(key_col, query_row, k0, q0, causal)
        at = pl.ds(q0, QT)

        def meet(hp):
            cols = columns(hp)
            s = dot(stack_heads(k[pl.ds(k0, KT), cols], masks), qt[cols, at])
            return s, dot(stack_heads(v[pl.ds(k0, KT), cols], masks), gt[cols, at])

        def weigh(hp, both):
            s, dp = both
            probs, slopes = [], []
            for side in range(2):
                h = 2 * hp + side
                rows = slice(side * KT, (side + 1) * KT)
                p = jnp.exp(s[rows] + bias - lse[h:h + 1, at])
                slopes.append((p * (dp[rows] - inner[h:h + 1, at])).astype(BF))
                probs.append(p.astype(BF))
            return jnp.concatenate(probs, 0), jnp.concatenate(slopes, 0)

        def spread(hp, both):
            cols = columns(hp)
            probs, slopes = both
            to_q = dot(block_diag(kt[cols, pl.ds(k0, KT)]), slopes)
            return dot_t(gt[cols, at], probs), dot_t(qt[cols, at], slopes), to_q

        def add(hp, terms):
            to_v, to_k, to_q = terms
            for acc, to in ((dv_acc, to_v), (dk_acc, to_k)):
                acc[hp * PAIR:hp * PAIR + HD, :] += to[:HD, :KT]
                acc[hp * PAIR + HD:(hp + 1) * PAIR, :] += to[HD:, KT:]
            dqt[columns(hp), at] += to_q

        pipeline(HEADS // 2, meet, weigh, spread, add)
        return 0

    lax.fori_loop(span[0], span[1], step, 0)
    dk[pl.ds(k0, KT), :] = jnp.transpose(dk_acc[...]).astype(BF)
    dv[pl.ds(k0, KT), :] = jnp.transpose(dv_acc[...]).astype(BF)


def flip(src, dst):
    for i in range(ROW // 128):
        dst[:, i * 128:(i + 1) * 128] = jnp.transpose(src[i * 128:(i + 1) * 128, :])


def standard(r):
    centered = r - jnp.mean(r, -1, keepdims=True)
    spread = jnp.mean(centered * centered, -1, keepdims=True)
    scale = lax.rsqrt(spread + 1e-05)
    return centered * scale, scale


def into_attention(g, c, inner, at, heads):
    both = g.astype(F32) * c.astype(F32)
    high = both.astype(BF)
    low = (both - high.astype(F32)).astype(BF)
    inner[:, at] = dot_t(heads, high) + dot_t(heads, low)


def head_rows():
    at = lax.broadcasted_iota(jnp.int32, (HEADS, D), 1) // HD == lax.broadcasted_iota(jnp.int32, (HEADS, D), 0)
    return at.astype(F32).astype(BF)


class Mover:
    def __init__(self, sems):
        self.sems, self.used, self.out = sems, 0, []

    def start(self, src, dst):
        cp = pltpu.make_async_copy(src, dst, self.sems.at[self.used])
        self.used += 1
        cp.start()
        return cp

    def store(self, src, dst):
        self.out.append(self.start(src, dst))

    def finish(self):
        for cp in self.out:
            cp.wait()


def own_spans():
    return [(max(0, (i * QT - MOST + 1) // KT), (i + 1) * QT // KT) for i in range(ROW // QT)]


def own_spans_back():
    return [(j * KT // QT, min(ROW // QT, ((j + 1) * KT - 1 + MOST - 1) // QT + 1)) for j in range(ROW // KT)]


def front_compute(x, mem, win, wout, norms, q1, k1, v1, c1, lse1, xh1, rs1, q2, k2, v2, trow, tcol, vt, scores, acc, peak, tally, ready, pump):
    ready("first")
    for i in range(ROW // 256):
        at = slice(i * 256, (i + 1) * 256)
        for out, w in ((q1, 0), (k1, 1), (v1, 2)):
            y = dot(x[at, :], win[w * D:(w + 1) * D, :]).astype(BF)
            out[at, :] = y * BF(0.125) if w == 0 else y
        pump()
    ready("projected")
    flip(v1, vt)
    for i, span in enumerate(own_spans()):
        attend(i, span, q1, k1, vt, tcol, trow, True, c1, lse1, scores, acc, peak, tally, pump)
    ready("second")
    for i in range(ROW // 256):
        at = slice(i * 256, (i + 1) * 256)
        for out, w in ((k2, 4), (v2, 5)):
            out[at, :] = dot(mem[at, :], win[w * D:(w + 1) * D, :]).astype(BF)
        pump()
    ready("keys")
    for i in range(ROW // 256):
        at = slice(i * 256, (i + 1) * 256)
        xhat, scale = standard(x[at, :].astype(F32) + dot(c1[at, :], wout[0:D, :]))
        xh1[at, :] = xhat
        rs1[at, :] = jnp.broadcast_to(scale, (256, 128))
        h = xhat * norms[0:1, :] + norms[3:4, :]
        q2[at, :] = dot(h.astype(BF), win[3 * D:4 * D, :]).astype(BF) * BF(0.125)
        pump()


FRONT_OUTS = (
    ((ROW, D), BF), ((ROW, D), BF), ((ROW, D), BF), ((ROW, D), BF), ((HEADS, ROW), F32),
    ((ROW, D), F32), ((ROW, 128), F32), ((ROW, D), BF), ((ROW, D), BF), ((ROW, D), BF),
)


def front_scratch():
    return (
        [pltpu.VMEM(s, d) for s, d in FRONT_OUTS]
        + [pltpu.VMEM((8, ROW), F32), pltpu.VMEM((ROW, 128), F32), pltpu.VMEM((D, ROW), BF)]
        + [pltpu.VMEM((ROW, D), F32)] * 4
        + [pltpu.VMEM((D, QT), F32), pltpu.VMEM((HEADS, 8, QT), F32), pltpu.VMEM((HEADS, 8, QT), F32)]
        + [pltpu.VMEM((ROW, D), BF)] * 2
        + [pltpu.VMEM((6 * D, D), BF), pltpu.VMEM((2 * D, D), BF), pltpu.SemaphoreType.DMA((40,))]
    )


def take(refs, k):
    out = refs[:k]
    del refs[:k]
    return out


SEG_OUTS = (((8, ROW), F32), ((ROW, 128), F32), ((ROW, 128), F32))


def segments_of(tlen, slen, trow, tcol, scol, table):
    tends, sends = ends_of(tlen), ends_of(slen)
    store_seg(sends, trow, scol)
    store_seg(tends, trow, tcol)
    store_ranges(table, 0, ranges(tends, sends, False, QT, KT, True))
    store_ranges(table, 8, ranges(tends, sends, False, KT, QT, False))


def front_kernel(tlen, slen, x, mem, win, wout, norms, *refs):
    refs = list(refs)
    outs, segs, table, kept = take(refs, 10), take(refs, 3), refs.pop(0), take(refs, 10)
    trow, tcol, vt = take(refs, 3)
    scores, (acc, peak, tally), (xs, ms, ws, os, sems, scol) = take(refs, 4), take(refs, 3), refs
    mover = Mover(sems)
    coming = [mover.start(x, xs), mover.start(win, ws), mover.start(wout, os), mover.start(mem, ms)]
    segments_of(tlen, slen, trow, tcol, scol, table)
    for k, ref in enumerate((trow, tcol, scol)):
        mover.store(ref, segs[k])

    def ready(stage):
        if stage == "first":
            coming[0].wait()
            coming[1].wait()
        if stage == "second":
            coming[2].wait()
            coming[3].wait()

    front_compute(xs, ms, ws, os, norms, *kept, trow, tcol, vt, scores, acc, peak, tally, ready, lambda: None)
    for k in range(10):
        mover.store(kept[k], outs[k])
    mover.finish()


def middle_kernel(
    tlen, table, mem, cot, q2, k2, v2, xh1, win, wout, up, down, norms, rows_in, cols_in,
    result, mgrad, dh1, gin, gout, gup, gdown, gnorm,
    mem_s, cot_s, q_s, k_s, v_s, xh_s, win_s, wout_s, up_s, down_s,
    result_s, mgrad_s, dh1_s, gin_s, gout_s, gup_s, gdown_s,
    trow, scol, flipped, qt, gt, c2, lse, inner, acc, peak, tally, spare, dr,
    h1b, h2b, act, du, dy, pre, dq, dk, dv, dqt, dk_acc, dv_acc, sems,
):
    mover = Mover(sems)
    half = pl.ds(3 * D, 3 * D)
    pairs = (
        (k2, k_s), (q2, q_s), (v2, v_s), (wout.at[pl.ds(D, D)], wout_s), (xh1, xh_s), (up, up_s), (down, down_s),
        (cot, cot_s), (win.at[half], win_s), (mem, mem_s),
    )
    segs = [mover.start(rows_in, trow), mover.start(cols_in, scol)]
    coming = [mover.start(a, b) for a, b in pairs]
    gnorm[...] = jnp.zeros_like(gnorm)
    heads = head_rows()
    for cp in segs + coming[:3]:
        cp.wait()
    flip(v_s, flipped)

    def forward(i, _):
        span = (table[2 * i], table[2 * i + 1])
        attend(i, span, q_s, k_s, flipped, scol, trow, False, c2, lse, (mgrad_s, dh1_s, dr, spare), acc, peak, tally)
        return 0

    lax.fori_loop(0, ROW // QT, forward, 0)
    for k in range(3, 8):
        coming[k].wait()
    live_end = ends_of(tlen)[SEGS - 2]
    block = 256

    def rows(i, _):
        at = pl.ds(pl.multiple_of(i * block, block), block)
        h = xh_s[at, :] * norms[0:1, :] + norms[3:4, :]
        h1b[at, :] = h.astype(BF)
        xh2, rs2 = standard(h + dot(c2[at, :], wout_s[...]))
        h = xh2 * norms[1:2, :] + norms[4:5, :]
        hb = h.astype(BF)
        h2b[at, :] = hb
        r3 = h
        for j in range(FF // D):
            cols = slice(j * D, (j + 1) * D)
            u = dot(hb, up_s[:, cols])
            pre[:, cols] = u
            a = (u / (1.0 + jnp.exp(-u))).astype(BF)
            act[at, cols] = a
            r3 = r3 + dot(a, down_s[cols, :])
        xhat, rstd = standard(r3)
        result_s[at, :] = (xhat * norms[2:3, :] + norms[5:6, :]).astype(BF)
        place = i * block + lax.broadcasted_iota(jnp.int32, (block, D), 0)
        seed = jnp.where(place < live_end, cot_s[at, :].astype(F32), 0.0)
        gnorm[0:8, :] += fold(seed * xhat)
        gnorm[8:16, :] += fold(seed)
        dr3 = norm_back(seed, xhat, rstd, norms[2:3, :])
        dyb = dr3.astype(BF)
        dy[at, :] = dyb
        dh = dr3
        for j in range(FF // D):
            cols = slice(j * D, (j + 1) * D)
            da = dot_t(dyb, down_s[cols, :])
            u = pre[:, cols]
            sig = 1.0 / (1.0 + jnp.exp(-u))
            d = (da * (sig * (1.0 + u * (1.0 - sig)))).astype(BF)
            du[at, cols] = d
            dh = dh + dot_t(d, up_s[:, cols])
        gnorm[16:24, :] += fold(dh * xh2)
        gnorm[24:32, :] += fold(dh)
        r = norm_back(dh, xh2, rs2, norms[1:2, :])
        dr[at, :] = r
        rb = r.astype(BF)
        dy2 = dot_t(rb, wout_s[...]).astype(BF)
        dq[at, :] = rb
        dk[at, :] = dy2
        into_attention(dy2, c2[at, :], inner, at, heads)
        return 0

    lax.fori_loop(0, ROW // block, rows, 0)
    mover.store(result_s, result)
    for j in range(FF // D):
        cols = slice(j * D, (j + 1) * D)
        gdown_s[cols, :] = t_dot(act[:, cols], dy[...]).astype(BF)
    mover.store(gdown_s, gdown)
    for j in range(FF // D):
        cols = slice(j * D, (j + 1) * D)
        gup_s[:, cols] = t_dot(h2b[...], du[:, cols]).astype(BF)
    mover.store(gup_s, gup)
    gout_s[...] = t_dot(c2[...], dq[...]).astype(BF)
    mover.store(gout_s, gout)
    flip(k_s, flipped)
    flip(q_s, qt)
    flip(dk, gt)
    dqt[...] = jnp.zeros_like(dqt)

    def backward(j, _):
        span = (table[8 + 2 * j], table[9 + 2 * j])
        attend_back(j, span, k_s, v_s, flipped, qt, gt, lse, inner, scol, trow, False, dqt, dk, dv, dk_acc, dv_acc)
        return 0

    lax.fori_loop(0, ROW // KT, backward, 0)
    coming[8].wait()
    coming[9].wait()
    gin_s[D:2 * D, :] = t_dot(mem_s[...], dk[...]).astype(BF)
    gin_s[2 * D:3 * D, :] = t_dot(mem_s[...], dv[...]).astype(BF)

    def end(at):
        q = jnp.transpose(dqt[:, at] * 0.125).astype(BF)
        dq[at, :] = q
        mgrad_s[at, :] = dot_t(dk[at, :], win_s[D:2 * D, :]) + dot_t(dv[at, :], win_s[2 * D:3 * D, :])
        dh1_s[at, :] = dr[at, :] + dot_t(q, win_s[0:D, :])

    for_rows(256, end)
    mover.store(mgrad_s, mgrad)
    mover.store(dh1_s, dh1)
    gin_s[0:D, :] = t_dot(h1b[...], dq[...]).astype(BF)
    mover.store(gin_s, gin)
    mover.finish()


def back_compute(
    x, q1, k1, v1, c1, lse, xh1, rs1, dh1, win, wout, norms, tgrad, gin, gout, gnorm,
    trow, tcol, kt, qt, gt, inner, dr, dc, dq, dk, dv, dqt, dk_acc, dv_acc, ready, pump,
):
    heads = head_rows()
    ready("first")
    for i in range(ROW // 256):
        at = slice(i * 256, (i + 1) * 256)
        dh, xhat = dh1[at, :], xh1[at, :]
        gain, bias = fold(dh * xhat), fold(dh)
        gnorm[0:8, :] = gain if i == 0 else gnorm[0:8, :] + gain
        gnorm[8:16, :] = bias if i == 0 else gnorm[8:16, :] + bias
        r = norm_back(dh, xhat, rs1[at, :], norms[0:1, :])
        dr[at, :] = r
        rb = r.astype(BF)
        g = dot_t(rb, wout[...]).astype(BF)
        dq[at, :] = rb
        dc[at, :] = g
        into_attention(g, c1[at, :], inner, at, heads)
        pump()
    gout[...] = t_dot(c1[...], dq[...]).astype(BF)
    ready("outward")
    flip(k1, kt)
    flip(q1, qt)
    flip(dc, gt)
    pump()
    dqt[...] = jnp.zeros_like(dqt)
    for j, span in enumerate(own_spans_back()):
        attend_back(j, span, k1, v1, kt, qt, gt, lse, inner, tcol, trow, True, dqt, dk, dv, dk_acc, dv_acc)
        pump()
    gin[D:2 * D, :] = t_dot(x[...], dk[...]).astype(BF)
    gin[2 * D:3 * D, :] = t_dot(x[...], dv[...]).astype(BF)
    for i in range(ROW // 256):
        at = slice(i * 256, (i + 1) * 256)
        dq[at, :] = jnp.transpose(dqt[:, at] * 0.125).astype(BF)
    gin[0:D, :] = t_dot(x[...], dq[...]).astype(BF)
    ready("inward")
    for i in range(ROW // 256):
        at = slice(i * 256, (i + 1) * 256)
        t = dr[at, :]
        for k, g in enumerate((dq, dk, dv)):
            t = t + dot_t(g[at, :], win[k * D:(k + 1) * D, :])
        tgrad[at, :] = t
        pump()


BACK_INS = (
    ((ROW, D), BF), ((ROW, D), BF), ((ROW, D), BF), ((ROW, D), BF), ((ROW, D), BF), ((HEADS, ROW), F32),
    ((ROW, D), F32), ((ROW, 128), F32), ((ROW, D), F32), ((3 * D, D), BF), ((D, D), BF),
)


def back_scratch():
    return (
        [pltpu.VMEM(s, d) for s, d in BACK_INS]
        + [pltpu.VMEM((ROW, D), F32)]
        + [pltpu.VMEM((8, ROW), F32), pltpu.VMEM((ROW, 128), F32)]
        + [pltpu.VMEM((D, ROW), BF)] * 3
        + [pltpu.VMEM((HEADS, ROW), F32), pltpu.VMEM((ROW, D), F32)]
        + [pltpu.VMEM((ROW, D), BF)] * 4
        + [pltpu.VMEM((D, ROW), F32), pltpu.VMEM((D, KT), F32), pltpu.VMEM((D, KT), F32), pltpu.SemaphoreType.DMA((40,))]
    )


def back_loads(mover, ins, kept):
    parts = list(ins[:9]) + [ins[9].at[pl.ds(0, 3 * D)], ins[10].at[pl.ds(0, D)]]
    order = (8, 6, 7, 10, 4, 2, 1, 3, 5, 0, 9)
    return [mover.start(parts[k], kept[k]) for k in order]


def back_kernel(norms, *refs):
    refs = list(refs)
    ins, segs, (tgrad, gin, gout, gnorm), kept = take(refs, 11), take(refs, 2), take(refs, 4), take(refs, 11)
    tgrad_s, work, sems = refs[0], refs[1:-1], refs[-1]
    mover = Mover(sems)
    coming = [mover.start(segs[0], work[0]), mover.start(segs[1], work[1])] + back_loads(mover, ins, kept)

    def ready(stage):
        if stage == "first":
            for cp in coming:
                cp.wait()

    back_compute(*kept, norms, tgrad_s, gin, gout, gnorm, *work, ready, lambda: None)
    mover.store(tgrad_s, tgrad)
    mover.finish()


VM = pl.BlockSpec(memory_space=pltpu.VMEM)
SM = pl.BlockSpec(memory_space=pltpu.SMEM)
HB = pl.BlockSpec(memory_space=pltpu.HBM)


def call(kernel, name, ins, in_specs, outs, out_specs, scratch, params):
    return pl.pallas_call(
        kernel,
        out_shape=[jax.ShapeDtypeStruct(s, d) for s, d in outs],
        in_specs=in_specs,
        out_specs=out_specs,
        scratch_shapes=scratch,
        compiler_params=pltpu.CompilerParams(vmem_limit_bytes=62 << 20, **params),
        name=name,
    )(*ins)


def middle(tlen, table, mem, cot, q2, k2, v2, xh1, win, wout, up, down, norms, trow, scol):
    tok, tokf, flat = ((ROW, D), BF), ((ROW, D), F32), ((D, ROW), BF)
    outs = [tok, tokf, tokf, ((3 * D, D), BF), ((D, D), BF), ((D, FF), BF), ((FF, D), BF)]
    ins = [tok] * 5 + [tokf, ((3 * D, D), BF), ((D, D), BF), ((D, FF), BF), ((FF, D), BF)]
    stat, tile = ((HEADS, ROW), F32), ((D, KT), F32)
    work = [((8, ROW), F32), ((ROW, 128), F32), flat, flat, flat, tok, stat, stat, ((D, QT), F32), ((HEADS, 8, QT), F32),
            ((HEADS, 8, QT), F32), tokf, tokf, tok, tok, ((ROW, FF), BF), ((ROW, FF), BF), tok, ((256, FF), F32), tok, tok, tok,
            ((D, ROW), F32), tile, tile]
    scratch = [pltpu.VMEM(*s) for s in ins + outs + work]
    return call(
        middle_kernel, "middle", [tlen, table, mem, cot, q2, k2, v2, xh1, win, wout, up, down, norms, trow, scol],
        [SM, SM] + [HB] * 10 + [VM, HB, HB], outs + [((32, D), F32)], [HB] * 7 + [VM],
        scratch + [pltpu.SemaphoreType.DMA((20,))], {},
    )


def layer(tlen, slen, x, mem, cot, win, wout, up, down, norms):
    q1, k1, v1, c1, lse1, xh1, rs1, q2, k2, v2, trow, tcol, scol, table = call(
        front_kernel, "front", [tlen, slen, x, mem, win, wout, norms], [SM, SM] + [HB] * 4 + [VM],
        [*FRONT_OUTS, *SEG_OUTS, ((32,), jnp.int32)], [HB] * 13 + [SM], front_scratch() + [pltpu.VMEM((ROW, 128), F32)], {},
    )
    result, mgrad, dh1, gin_two, gout_two, gup, gdown, gnorm_rest = middle(
        tlen, table, mem, cot, q2, k2, v2, xh1, win, wout, up, down, norms, trow, scol)
    tgrad, gin_one, gout_one, gnorm_one = call(
        back_kernel, "back", [norms, x, q1, k1, v1, c1, lse1, xh1, rs1, dh1, win, wout, trow, tcol], [VM] + [HB] * 13,
        [((ROW, D), F32), ((3 * D, D), BF), ((D, D), BF), ((16, D), F32)], [HB, VM, VM, VM], back_scratch(), {},
    )
    gin, gout = jnp.concatenate([gin_one, gin_two]), jnp.concatenate([gout_one, gout_two])
    one = jnp.sum(gnorm_one.reshape(2, 8, D), 1)
    rest = jnp.sum(gnorm_rest.reshape(4, 8, D), 1)
    gnorm = jnp.stack([one[0], rest[2], rest[0], one[1], rest[3], rest[1]])
    return result, tgrad, mgrad, gin, gout, gup, gdown, gnorm


def every(dims):
    return [(a, b, c, e) for a in range(dims[0]) for b in range(dims[1]) for c in range(dims[2]) for e in range(dims[3])]


def lanes_up_to(n):
    return lax.broadcasted_iota(jnp.int32, (8, 128), 1) < n


def norms_from_shards(shards, lined, flat, out):
    for i, at in enumerate(every(shards.shape[:4])):
        lined[i:i + 1, :] = shards[at]
    n = [lined[pl.ds(k, 8, stride=4), :] for k in range(4)]
    flat[pl.ds(0, 8, stride=3), :] = jnp.where(lanes_up_to(96), n[0], pltpu.roll(n[1], 96, 1))
    flat[pl.ds(1, 8, stride=3), :] = jnp.where(lanes_up_to(64), pltpu.roll(n[1], 96, 1), pltpu.roll(n[2], 64, 1))
    flat[pl.ds(2, 8, stride=3), :] = jnp.where(lanes_up_to(32), pltpu.roll(n[2], 64, 1), pltpu.roll(n[3], 32, 1))
    for i in range(24):
        out[i // 4:i // 4 + 1, (i % 4) * 128:(i % 4 + 1) * 128] = flat[i:i + 1, :]


def norms_to_shards(rows, flat, lined, shards):
    for i in range(24):
        flat[i:i + 1, :] = rows[i // 4][:, (i % 4) * 128:(i % 4 + 1) * 128]
    r = [flat[pl.ds(k, 8, stride=3), :] for k in range(3)]
    lined[pl.ds(0, 8, stride=4), :] = r[0]
    lined[pl.ds(1, 8, stride=4), :] = jnp.where(lanes_up_to(32), pltpu.roll(r[0], 32, 1), pltpu.roll(r[1], 32, 1))
    lined[pl.ds(2, 8, stride=4), :] = jnp.where(lanes_up_to(64), pltpu.roll(r[1], 64, 1), pltpu.roll(r[2], 64, 1))
    lined[pl.ds(3, 8, stride=4), :] = pltpu.roll(r[2], 96, 1)
    for i, at in enumerate(every(shards.shape[:4])):
        shards[at] = lined[i:i + 1, :]


DONE = "done"


def until_done(flow):
    for _ in flow:
        yield None
    while True:
        yield DONE


def around(place, d):
    n = place.sizes[0]
    return lax.rem(place.at[0] + (d + n), n)


def spot(first, p, q, at_p, at_q, e):
    return (first, at_p, at_q, *e) if p < q else (first, at_q, at_p, *e)


def gather_bulk(place, ref, own, p, q, sems, span=None, part=None, before=None):
    n, e = place.sizes[0], place.at[3]
    low, high = span or (0, n)
    whole = (low, high) == (0, n)
    group = slice(None) if whole else pl.ds(low, high - low)
    rows = (pl.ds(*part),) if part else ()
    after = []

    def inside(coord):
        return None if whole else (coord >= low) & (coord < high)

    def view(first, flip_p, flip_q, core=None):
        at_p = 1 - place.at[p] if flip_p else place.at[p]
        at_q = slice(None) if flip_q is None else 1 - place.at[q] if flip_q else place.at[q]
        return ref.at[(*spot(first, p, q, at_p, at_q, (e if core is None else core,)), *rows)]

    def send(src, dst, device, cond=None):
        pair = sems.take()
        go = remote(src, dst, pair, device)
        when(cond, go.start)
        after.append((cond, go.wait_send))
        return lambda view: remote(view, view, pair, device)

    def to_sibling(flip_p, flip_q):
        come = send(view(group, flip_p, flip_q), view(group, flip_p, flip_q), place.device(3, 1 - e))
        after.append((None, come(view(group, flip_p, flip_q, 1 - e)).wait_recv))

    own = own.at[rows] if rows else own
    mine = inside(place.at[0])
    come = {}
    for d in range(1, n):
        come[d] = send(own, view(place.at[0], 0, 0), place.device(0, around(place, d)), mine)
    yield
    for d in range(1, n):
        src = around(place, -d)
        when(inside(src), come[d](view(src, 0, 0)).wait_recv)
    if before:
        before()
    here = view(group, 0, 0)
    to_p, to_q = place.device(p, 1 - place.at[p]), place.device(q, 1 - place.at[q])
    from_p, from_q = send(here, here, to_p), send(here, here, to_q)
    to_sibling(0, 0)
    yield
    there = view(group, 1, 0)
    from_p(there).wait_recv()
    from_pq = send(there, there, to_q)
    to_sibling(1, 0)
    yield
    from_q(view(group, 0, 1)).wait_recv()
    to_sibling(0, 1)
    from_pq(view(group, 1, 1)).wait_recv()
    to_sibling(1, 1)
    yield
    for cond, f in after:
        when(cond, f)


def gather_bulk_sems(sizes):
    return sizes[0] - 1 + 3 + 4


def add_rows(dst, *srcs):
    v = srcs[0][...].astype(F32)
    for s in srcs[1:]:
        v = v + s[...].astype(F32)
    dst[...] = v.astype(dst.dtype)


def reduce_bulk(place, grad, half, from_q, from_p, from_z, total, p, q, sems, low=0, part=None):
    n, e = place.sizes[0], place.at[3]
    count = grad.shape[0]
    whole = count == n
    rows = (pl.ds(*part),) if part else ()
    after = []
    me_p, me_q, all_of = place.at[p], place.at[q], slice(None)

    def inside(coord):
        return None if whole else (coord >= low) & (coord < low + count)

    def g(first, at_p, at_q, core):
        return grad.at[(*spot(first, p, q, at_p, at_q, (core,)), *rows)]

    def h(first, at_p, at_q):
        return half.at[(*spot(first, p, q, at_p, at_q, ()), *rows)]

    def send(src, dst, device, cond=None):
        go = remote(src, dst, sems.take(), device)
        when(cond, go.start)
        after.append((cond, go.wait_send))
        return go

    def each(f, times):
        def step(i, _):
            f(i)
            return 0

        lax.fori_loop(0, times, step, 0)

    sibling = place.device(3, 1 - e)
    core_q, core_p, core = [
        send(g(all_of, at_p, at_q, 1 - e), h(all_of, at_p, at_q), sibling)
        for at_p, at_q in ((all_of, 1 - me_q), (1 - me_p, me_q), (me_p, me_q))]
    yield
    core_q.wait_recv()

    def far(i):
        a, at_p = lax.div(i, 2), lax.rem(i, 2)
        add_rows(h(a, at_p, 1 - me_q), g(a, at_p, 1 - me_q, e), h(a, at_p, 1 - me_q))

    each(far, 2 * count)
    come_q = send(h(all_of, all_of, 1 - me_q), from_q, place.device(q, 1 - me_q))
    yield
    core_p.wait_recv()
    come_q.wait_recv()
    each(lambda a: add_rows(h(a, 1 - me_p, me_q), g(a, 1 - me_p, me_q, e), h(a, 1 - me_p, me_q), from_q.at[a, 1 - me_p]), count)
    come_p = send(h(all_of, 1 - me_p, me_q), from_p, place.device(p, 1 - me_p))
    yield
    core.wait_recv()
    come_p.wait_recv()
    each(lambda a: add_rows(h(a, me_p, me_q), g(a, me_p, me_q, e), h(a, me_p, me_q), from_q.at[a, me_p], from_p.at[a]), count)
    come_z = []
    for d in range(1, n):
        to = around(place, d)
        pair = sems.take()
        go = remote(h(to - low, me_p, me_q), from_z.at[d - 1], pair, place.device(0, to))
        when(inside(to), go.start)
        after.append((inside(to), go.wait_send))
        come_z.append(remote(from_z.at[d - 1], from_z.at[d - 1], pair, place.device(0, to)))
    yield

    def close():
        for come in come_z:
            come.wait_recv()
        add_rows(total.at[rows] if rows else total, h(place.at[0] - low, me_p, me_q), *[from_z.at[d] for d in range(n - 1)])

    when(inside(place.at[0]), close)
    for cond, f in after:
        when(cond, f)


def reduce_bulk_sems(sizes):
    return 5 + sizes[0] - 1


def reduce_bulk_bufs(sizes, count, shape):
    return [(count, 2, *shape), (count, *shape), (sizes[0] - 1, *shape)]


def front_remote_kernel(sizes, shapes, tlen, slen, x, mem, *refs):
    refs = list(refs)
    masters = take(refs, 5)
    outs, segs, (win, wout, up, down, norms, table), kept = take(refs, 10), take(refs, 3), take(refs, 6), take(refs, 10)
    trow, tcol, vt = take(refs, 3)
    scores, (acc, peak, tally), (xs, ms, ws, os, sems) = take(refs, 4), take(refs, 3), take(refs, 5)
    scol, stage_up, stage_down, shards, lined, flat, send, recv = refs
    place, mover = Place(sizes), Mover(sems)
    coming = [mover.start(x, xs), mover.start(mem, ms)]
    mine = [ws.at[place.at], os.at[place.at], stage_up, stage_down]
    for k in range(4):
        flat_to_rows(masters[k], mine[k], *shapes[k])
    shards[place.at] = jnp.zeros((1, 128), F32)
    width = masters[4].shape[1]
    shards[(*place.at, slice(None), slice(0, width))] = masters[4][...].astype(BF).astype(F32)
    local = [mover.start(stage_up, up.at[place.at]), mover.start(stage_down, down.at[place.at])]
    pool, half, rows = Sems(send, recv), sizes[0] // 2, shapes[0][0] // 2
    low, high, top, low_rows = (0, half), (half, sizes[0]), (0, rows), (rows, rows)

    def flow(ref, own, p, q, *rest):
        return until_done(gather_bulk(place, ref, own, p, q, pool, *rest))

    place.greet(True)
    inward, outward = ws.at[place.at], os.at[place.at]
    flows_by = {
        "a": flow(ws, inward, 2, 1, low, top), "b": flow(ws, inward, 1, 2, low, low_rows),
        "c": flow(ws, inward, 2, 1, high, top), "d": flow(ws, inward, 1, 2, high, low_rows),
        "o": flow(os, outward, 1, 2), "n": flow(shards, shards.at[place.at], 1, 2),
        "u": flow(up, stage_up, 2, 1, None, None, local[0].wait), "v": flow(down, stage_down, 1, 2, None, None, local[1].wait),
    }

    def go_on(names):
        for name in names:
            if name in flows_by and next(flows_by[name]) is DONE:
                del flows_by[name]

    def finish(names):
        while set(names) & set(flows_by):
            go_on(names)

    go_on(BEGIN)
    segments_of(tlen, slen, trow, tcol, scol, table)
    for k, ref in enumerate((trow, tcol, scol)):
        mover.store(ref, segs[k])
    go_on(FIRST)
    finish("ab")
    count = [0]

    def pump():
        count[0] += 1
        go_on(FRONT_PLAN.get(count[0], ""))

    def ready(stage):
        if stage == "first":
            coming[0].wait()
        if stage == "projected":
            for k in range(3):
                mover.store(kept[k], outs[k])
        if stage == "second":
            finish("cdon")
            mover.store(ws, win)
            mover.store(os, wout)
            norms_from_shards(shards, lined, flat, norms)
            coming[1].wait()
        if stage == "keys":
            for k in (3, 4, 8, 9):
                mover.store(kept[k], outs[k])

    front_compute(
        xs, ms, ws.reshape(6 * D, D), os.reshape(2 * D, D), norms, *kept, trow, tcol, vt, scores, acc, peak, tally, ready, pump)
    for k in (5, 6, 7):
        mover.store(kept[k], outs[k])
    finish("uv")
    mover.finish()


BEGIN = "abcdonuv"
FIRST = "abababab"
FRONT_PLAN = {1: "cdon", 3: "uv", 6: "cdon", 8: "uv", 10: "cdon", 12: "uv"}


def front_remote(sizes, shapes, tlen, slen, x, mem, masters):
    weights = [((*sizes, *s), BF) for s in shapes[:4]]
    count = 8 * gather_bulk_sems(sizes)
    scratch = front_scratch()
    scratch[-3:-1] = [pltpu.VMEM(*w) for w in weights[:2]]
    return call(
        functools.partial(front_remote_kernel, sizes, shapes), "front", [tlen, slen, x, mem, *masters],
        [SM, SM, HB, HB] + [VM] * 5, (*FRONT_OUTS, *SEG_OUTS, *weights, ((6, D), F32), ((32,), jnp.int32)),
        [HB] * 17 + [VM, SM],
        scratch
        + [pltpu.VMEM((ROW, 128), F32), pltpu.VMEM(shapes[2], BF), pltpu.VMEM(shapes[3], BF), pltpu.VMEM((*sizes, 1, 128), F32),
           pltpu.VMEM((32, 128), F32), pltpu.VMEM((24, 128), F32)]
        + [pltpu.SemaphoreType.DMA((count,))] * 2,
        dict(collective_id=0, has_side_effects=True),
    )


def back_remote_kernel(sizes, shapes, norms, rest, *refs):
    refs = list(refs)
    ins, segs, grads, tgrad, totals, kept = take(refs, 11), take(refs, 2), take(refs, 4), refs.pop(0), take(refs, 5), take(refs, 11)
    tgrad_s, work = refs.pop(0), take(refs, 14)
    sems, gin, gout, gnorm, lined, flat, shards = take(refs, 7)
    staged, halves = take(refs, 4), take(refs, 7)
    bufs, (send, recv) = [take(refs, 3) for _ in range(8)], refs
    place, mover = Place(sizes), Mover(sems)
    loads = [mover.start(grads[k], staged[k]) for k in (3, 2, 0, 1)]
    coming = [mover.start(segs[0], work[0]), mover.start(segs[1], work[1])] + back_loads(mover, ins, kept)
    place.greet(True)
    pool, half = Sems(send, recv), sizes[0] // 2
    flows_by = {}

    def begin(name, k, grad, into, total, p, q, low=0, part=None):
        flows_by[name] = until_done(reduce_bulk(place, grad, into, *bufs[k], total, p, q, pool, low, part))
        next(flows_by[name])

    def go_on(names):
        for name in names:
            if name in flows_by and next(flows_by[name]) is DONE:
                del flows_by[name]

    for name, cp, k, p, q, low in zip("duio", loads, (3, 2, 0, 1), (2, 1, 2, 1), (1, 2, 1, 2), (0, 0, half, half)):
        cp.wait()
        begin(name, k, staged[k], halves[k], totals[k], p, q, low)
    count = [0]

    def pump():
        count[0] += 1
        go_on(PLAN.get(count[0], ""))

    def ready(stage):
        if stage == "first":
            for cp in coming:
                cp.wait()
        if stage == "outward":
            begin("w", 4, gout, halves[5], totals[1], 1, 2)
            one = [jnp.sum(gnorm[8 * i:8 * i + 8, :], 0, keepdims=True) for i in range(2)]
            more = [jnp.sum(rest[8 * i:8 * i + 8, :], 0, keepdims=True) for i in range(4)]
            norms_to_shards([one[0], more[2], more[0], one[1], more[3], more[1]], flat, lined, shards)
            begin("n", 5, shards, halves[6], totals[4], 1, 2)
        if stage == "inward":
            rows = shapes[0][0] // 2
            begin("a", 6, gin, halves[4], totals[0], 2, 1, 0, (0, rows))
            begin("b", 7, gin, halves[4], totals[0], 1, 2, 0, (rows, rows))

    back_compute(
        *kept, norms, tgrad_s, gin.reshape(3 * D, D), gout.reshape(D, D), gnorm, *work, ready, pump)
    mover.store(tgrad_s, tgrad)
    go_on(REST)
    while flows_by:
        go_on("abiowndu")
    mover.finish()


PLAN = {3: "du", 4: "io", 8: "duwn", 10: "duo", 12: "wni", 13: "wn", 15: "ab", 16: "io"}
REST = "ab"


def back_remote(sizes, shapes, norms, rest, ins, segs, grads):
    half = sizes[0] // 2
    counts = (half, half, sizes[0], sizes[0])
    grads = [g.reshape(n, *sizes[1:], *s) for g, n, s in zip(grads, counts, shapes)]
    halves = [((n, *sizes[1:3], *s), BF) for n, s in zip((*counts, half, half), (*shapes[:4], *shapes[:2]))]
    halves.append(((*sizes[:3], *shapes[4]), F32))
    rows, cols = shapes[0]
    flows_of = [(n, s, BF) for n, s in zip(counts, shapes)] + [
        (half, shapes[1], BF), (sizes[0], shapes[4], F32), (half, (rows // 2, cols), BF), (half, (rows // 2, cols), BF)]
    bufs = [pltpu.VMEM(s, d) for n, shape, d in flows_of for s in reduce_bulk_bufs(sizes, n, shape)]
    return call(
        functools.partial(back_remote_kernel, sizes, shapes), "back", [norms, rest, *ins, *segs, *grads],
        [VM, VM] + [HB] * 17,
        [((ROW, D), F32)] + [(s, F32) for s in shapes], [HB] + [VM] * 5,
        back_scratch()
        + [pltpu.VMEM((half, *sizes[1:], *shapes[0]), BF), pltpu.VMEM((half, *sizes[1:], *shapes[1]), BF),
           pltpu.VMEM((16, D), F32), pltpu.VMEM((32, 128), F32), pltpu.VMEM((24, 128), F32), pltpu.VMEM((*sizes, 1, 128), F32)]
        + [pltpu.VMEM(g.shape, BF) for g in grads] + [pltpu.VMEM(*h) for h in halves]
        + bufs + [pltpu.SemaphoreType.DMA((8 * reduce_bulk_sems(sizes),))] * 2,
        dict(collective_id=1, has_side_effects=True),
    )


def shard_views(inward, outward, expand, shrink, norms):
    arrays, shapes = [], []
    for x, wide in ((inward, D), (outward, D), (expand, FF), (shrink, D)):
        cols = wide if x.shape[0] >= 16 * wide else D
        arrays.append(x.reshape(-1, 128))
        shapes.append((x.shape[0] // cols, cols))
    arrays.append(norms.reshape(1, -1))
    shapes.append((1, -(-norms.shape[0] // 128) * 128))
    return arrays, tuple(shapes)


def body(
    sizes, target, memory, cotangent, target_lengths, source_lengths,
    inward_master, inward_mean, inward_square, outward_master, outward_mean, outward_square,
    expand_master, expand_mean, expand_square, shrink_master, shrink_mean, shrink_square,
    norms_master, norms_mean, norms_square,
):
    flat, shapes = shard_views(inward_master, outward_master, expand_master, shrink_master, norms_master)
    norm_count = norms_master.shape[0]
    means, _ = shard_views(inward_mean, outward_mean, expand_mean, shrink_mean, norms_mean)
    squares, _ = shard_views(inward_square, outward_square, expand_square, shrink_square, norms_square)
    x, mem, cot = target[0], memory[0], cotangent[0]
    if sizes[1:] == (2, 2, 2) and norm_count == 96 and all(s[0] % 16 == 0 for s in shapes[:4]):
        *kept, trow, tcol, scol, win, wout, up, down, norms, table = front_remote(
            sizes, shapes, target_lengths, source_lengths, x, mem, flat)
        win, wout = win.reshape(6 * D, D), wout.reshape(2 * D, D)
        q1, k1, v1, c1, lse1, xh1, rs1, q2, k2, v2 = kept
        result, mgrad, dh1, gin, gout, gup, gdown, rest = middle(
            target_lengths, table, mem, cot, q2, k2, v2, xh1, win, wout, up.reshape(D, FF), down.reshape(FF, D), norms, trow, scol)
        tgrad, *sums = back_remote(
            sizes, shapes, norms, rest, [x, q1, k1, v1, c1, lse1, xh1, rs1, dh1, win, wout], [trow, tcol], [gin, gout, gup, gdown])
    else:
        padding = ((0, 0), (0, shapes[4][1] - norm_count))
        win, wout, up, down, norms = gather_all(
            sizes, [*flat[:4], jnp.pad(flat[4], padding)], shapes, [BF, BF, BF, BF, F32])
        norms = norms.reshape(-1, norms.shape[-1])[:, :norm_count].reshape(6, D)
        result, tgrad, mgrad, gin, gout, gup, gdown, gnorm = layer(
            target_lengths, source_lengths, x, mem, cot,
            win.reshape(6 * D, D), wout.reshape(2 * D, D), up.reshape(D, FF), down.reshape(FF, D), norms,
        )
        gnorm = jnp.pad(gnorm.reshape(-1, norm_count), padding)
        grads = [g.reshape(*sizes, *s) for g, s in zip((gin, gout, gup, gdown, gnorm), shapes)]
        sums = reduce_all(sizes, grads, shapes)
    tgrad, *outs = adam_all(tgrad, sums, means, squares, (*shapes[:4], (1, norm_count)))
    return (result[None], tgrad[None], mgrad[None], *[x.reshape(-1) for x in outs])


def solution(mesh):
    rows, cols = mesh.shape["dp"], mesh.shape["shard"]
    both = ("dp", "shard")
    row, flat = P(both, None, None), P(both)
    return jax.shard_map(
        functools.partial(body, (rows // 2, 2, cols // 2, 2)),
        mesh=mesh,
        in_specs=(row, row, row, P(both, None), P(both, None), *[flat] * 15),
        out_specs=(row, row, row, *[flat] * 15),
        check_vma=False,
    )
```

```python
import functools
import jax
import jax.numpy as jnp
from jax import lax
from jax.experimental import pallas as pl
from jax.experimental.pallas import tpu as pltpu
from jax.sharding import PartitionSpec as P

MESH = pl.DeviceIdType.MESH
BF = jnp.bfloat16
F32 = jnp.float32
learn_rate = 0.001
beta_one = 0.9
beta_two = 0.999
STEP = 10


class Place:
    def __init__(self, sizes):
        self.sizes = sizes
        dp, sh = lax.axis_index("dp"), lax.axis_index("shard")
        self.at = (dp // sizes[1], dp % sizes[1], sh // sizes[3], sh % sizes[3])

    def device(self, axis, coord):
        a, b, c, e = [coord if i == axis else v for i, v in enumerate(self.at)]
        return (a * self.sizes[1] + b, c * self.sizes[3] + e)

    def greet(self, far=False):
        barrier = pltpu.get_barrier_semaphore()
        count = 0
        for axis in range(4):
            n, me = self.sizes[axis], self.at[axis]
            if n == 2:
                pl.semaphore_signal(barrier, inc=1, device_id=self.device(axis, 1 - me), device_id_type=MESH)
                count = count + 1
            else:
                for step in [s for d in range(1, n if far else 2) for s in (-d, d)]:
                    there = me + step
                    ok = (there >= 0) & (there < n)

                    @pl.when(ok)
                    def _():
                        pl.semaphore_signal(barrier, inc=1, device_id=self.device(axis, there), device_id_type=MESH)

                    count = count + ok.astype(jnp.int32)
        pl.semaphore_wait(barrier, count)


class Sems:
    def __init__(self, send, recv):
        self.send, self.recv, self.used = send, recv, 0

    def take(self):
        k = self.used
        self.used += 1
        return self.send.at[k], self.recv.at[k]


def gather_sems(order, sizes):
    return 1 + sum(2 if sizes[x] == 2 else 4 * (sizes[x] - 1) for x in order)


def gather_rounds(place, ref, order, sems):
    sizes = place.sizes
    after = []
    held = []

    def group(axis=None, coord=None):
        idx = [slice(None) if i in held else place.at[i] for i in range(4)]
        if axis is not None:
            idx[axis] = coord
        return ref.at[tuple(idx)]

    def copy(block, axis, coord, pair):
        return pltpu.make_async_remote_copy(
            src_ref=block, dst_ref=block, send_sem=pair[0], recv_sem=pair[1],
            device_id=place.device(axis, coord), device_id_type=MESH)

    def to_sibling(axis, coord, cond):
        pair = sems.take()
        idx = [slice(None) if i in held else place.at[i] for i in range(4)]
        if axis is not None:
            idx[axis] = coord
        mine = ref.at[tuple(idx)]
        idx[3] = 1 - place.at[3]
        theirs = ref.at[tuple(idx)]
        e = place.at[3]
        go = copy(mine, 3, 1 - e, pair)
        come = copy(theirs, 3, 1 - e, pair)

        def run(f):
            if cond is None:
                f()
            else:
                pl.when(cond)(f)

        run(go.start)

        def finish():
            go.wait_send()
            come.wait_recv()

        after.append(lambda: run(finish))

    to_sibling(None, None, None)
    for axis in order:
        n, me = sizes[axis], place.at[axis]
        if n == 2:
            pair = sems.take()
            go = copy(group(), axis, 1 - me, pair)
            come = copy(group(axis, 1 - me), axis, 1 - me, pair)
            go.start()
            after.append(go.wait_send)
            yield
            come.wait_recv()
            to_sibling(axis, 1 - me, None)
        else:
            for t in range(1, n):
                pending = []
                for step in (1, -1):
                    pair = sems.take()
                    out_c, in_c, to = me - step * (t - 1), me - step * t, me + step
                    can = (out_c >= 0) & (out_c < n) & (to >= 0) & (to < n)
                    gets = (in_c >= 0) & (in_c < n)
                    go = copy(group(axis, out_c), axis, to, pair)
                    come = copy(group(axis, in_c), axis, to, pair)
                    pl.when(can)(go.start)
                    after.append(lambda go=go, can=can: pl.when(can)(go.wait_send))
                    pending.append((come, gets, in_c))
                yield
                for come, gets, in_c in pending:
                    pl.when(gets)(come.wait_recv)
                    to_sibling(axis, in_c, gets)
        held.append(axis)
    yield
    for f in after:
        f()


def interleave(rounds):
    live = list(rounds)
    while live:
        still = []
        for r in live:
            try:
                next(r)
                still.append(r)
            except StopIteration:
                pass
        live = still


def flat_to_rows(src, dst, rows, cols):
    w = cols // 128
    for j in range(w):
        dst[:, j * 128:(j + 1) * 128] = src[pl.ds(j, rows, stride=w), :].astype(dst.dtype)


def rows_to_flat(value, dst, rows, cols):
    w = cols // 128
    for j in range(w):
        dst[pl.ds(j, rows, stride=w), :] = value[:, j * 128:(j + 1) * 128]


def both(a, b):
    return b if a is None else a if b is None else a & b


def when(cond, f):
    if cond is None:
        f()
    else:
        pl.when(cond)(f)


def remote(src, dst, pair, device):
    return pltpu.make_async_remote_copy(
        src_ref=src, dst_ref=dst, send_sem=pair[0], recv_sem=pair[1], device_id=device, device_id_type=MESH)


ORDERS = ((0, 2, 1), (0, 1, 2), (1, 2, 0), (0, 1, 2), (0, 1, 2))


def gather_kernel(sizes, shapes, *refs):
    n = len(shapes)
    masters, outs = refs[:n], refs[n:2 * n]
    stage, local, send, recv = refs[2 * n:3 * n], refs[3 * n], refs[3 * n + 1], refs[3 * n + 2]
    place = Place(sizes)
    copies = []
    for k, (rows, cols) in enumerate(shapes):
        if rows == 1:
            stage[k][...] = masters[k][...].astype(BF).astype(stage[k].dtype)
        else:
            flat_to_rows(masters[k], stage[k], rows, cols)
        cp = pltpu.make_async_copy(stage[k], outs[k].at[place.at], local.at[k])
        cp.start()
        copies.append(cp)
    place.greet()
    for cp in copies:
        cp.wait()
    sems = Sems(send, recv)
    interleave([gather_rounds(place, outs[k], ORDERS[k], sems) for k in range(n)])


def gather_all(mesh_sizes, masters, shapes, dtypes):
    n = len(shapes)
    total = sum(gather_sems(ORDERS[k], mesh_sizes) for k in range(n))
    vm = pl.BlockSpec(memory_space=pltpu.VMEM)
    return pl.pallas_call(
        functools.partial(gather_kernel, mesh_sizes, shapes),
        out_shape=[jax.ShapeDtypeStruct((*mesh_sizes, *s), d) for s, d in zip(shapes, dtypes)],
        in_specs=[vm] * n,
        out_specs=[pl.BlockSpec(memory_space=pl.ANY)] * n,
        scratch_shapes=[pltpu.VMEM(s, d) for s, d in zip(shapes, dtypes)]
        + [pltpu.SemaphoreType.DMA((n,)), pltpu.SemaphoreType.DMA((total,)), pltpu.SemaphoreType.DMA((total,))],
        compiler_params=pltpu.CompilerParams(collective_id=0, has_side_effects=True, vmem_limit_bytes=48 << 20),
        name="gather_weights",
    )(*masters)


def reduce_sems(order, sizes):
    return 1 + sum(1 if sizes[x] == 2 else 2 * (sizes[x] - 1) for x in order)


def reduce_rounds(place, grad, order, got, bufs, total, sems):
    sizes = place.sizes
    after = []
    e = place.at[3]

    def rdma(src, dst, axis, coord, pair):
        return pltpu.make_async_remote_copy(
            src_ref=src, dst_ref=dst, send_sem=pair[0], recv_sem=pair[1],
            device_id=place.device(axis, coord), device_id_type=MESH)

    def add_into(dst, src):
        dst[...] = (dst[...].astype(F32) + src[...].astype(F32)).astype(dst.dtype)

    def each(dims, f):
        count = 1
        for d in dims:
            count *= d
        if count == 1:
            f(tuple(0 for _ in dims))
            return

        def step(i, _):
            idx = []
            for d in reversed(dims):
                idx.append(i % d)
                i = i // d
            f(tuple(reversed(idx)))
            return 0

        lax.fori_loop(0, count, step, 0)

    cp = rdma(grad.at[:, :, :, 1 - e], got, 3, 1 - e, sems.take())
    cp.start()
    yield
    cp.wait()
    each(sizes[:3], lambda i: add_into(got.at[i], grad.at[(*i, e)]))
    cur, left = got, [0, 1, 2]
    for axis, buf in zip(order, bufs):
        n, me = sizes[axis], place.at[axis]
        pos = left.index(axis)
        rest = [x for x in left if x != axis]
        dims = [sizes[x] for x in rest]

        def part(ref, coord):
            return ref.at[tuple(coord if i == pos else slice(None) for i in range(len(left)))]

        def one(ref, coord, i):
            i = list(i)
            i.insert(pos, coord)
            return ref.at[tuple(i)]

        last = not rest
        if n == 2:
            cp = rdma(part(cur, 1 - me), buf, axis, 1 - me, sems.take())
            cp.start()
            yield
            cp.wait()
            if last:
                total[...] = buf[...].astype(F32) + cur[me].astype(F32)
            else:
                each(dims, lambda i: add_into(buf.at[i], one(cur, me, i)))
        else:
            for t in range(n - 1):
                for way, step in enumerate((1, -1)):
                    j = n - 1 - t if step == 1 else t
                    to, back = me + step, me - step
                    ahead = (j > me) if step == 1 else (j < me)
                    gets = ahead & (back >= 0) & (back < n)
                    pair = sems.take()
                    come = rdma(part(cur, j), buf.at[way, j], axis, to, pair)

                    @pl.when(gets)
                    def _():
                        come.wait_recv()
                        each(dims, lambda i: add_into(one(cur, j, i), buf.at[(way, j, *i)]))

                    pl.when(ahead)(come.start)
                    after.append(lambda come=come, ahead=ahead: pl.when(ahead)(come.wait_send))
                    ends = (j == me) & (back >= 0) & (back < n)
                    after.append(lambda come=come, ends=ends: pl.when(ends)(come.wait_recv))
                yield
            for f in after:
                f()
            after = []
            keep = buf.at[0, me]

            def close(i):
                mine = one(cur, me, i)[...].astype(F32)
                v = mine + jnp.where(me > 0, buf[(0, me, *i)].astype(F32), 0.0)
                v = v + jnp.where(me < n - 1, buf[(1, me, *i)].astype(F32), 0.0)
                if last:
                    total[...] = v
                else:
                    buf[(0, me, *i)] = v.astype(buf.dtype)

            each(dims, close)
            buf = keep
        cur, left = buf, rest
    for f in after:
        f()


def reduce_bufs(order, sizes, shape):
    left, out = [0, 1, 2], [(*sizes[:3], *shape)]
    for axis in order:
        rest = [x for x in left if x != axis]
        dims = tuple(sizes[x] for x in rest)
        out.append((*dims, *shape) if sizes[axis] == 2 else (2, sizes[axis], *dims, *shape))
        left = rest
    return out


BACK = tuple(tuple(reversed(o)) for o in ORDERS)


def adam(mean_old, square_old, grad):
    mean_new = beta_one * mean_old + (1.0 - beta_one) * grad
    square_new = beta_two * square_old + (1.0 - beta_two) * grad * grad
    steps = float(STEP)
    mean_hat = mean_new / (1.0 - beta_one**steps)
    square_hat = square_new / (1.0 - beta_two**steps)
    return -learn_rate * mean_hat / (jnp.sqrt(square_hat) + 1e-08), mean_new


def reduce_kernel(sizes, shapes, counts, *refs):
    n = len(shapes)
    refs = list(refs)

    def take(k):
        out = refs[:k]
        del refs[:k]
        return out

    grads, totals = take(n), take(n)
    bufs = [take(c) for c in counts]
    send, recv = take(2)
    place = Place(sizes)
    place.greet()
    sems = Sems(send, recv)
    interleave([reduce_rounds(place, grads[k], BACK[k], bufs[k][0], bufs[k][1:], totals[k], sems) for k in range(n)])


def reduce_all(mesh_sizes, grads, shapes):
    n = len(shapes)
    lists = [reduce_bufs(BACK[k], mesh_sizes, shapes[k]) for k in range(n)]
    total = sum(reduce_sems(BACK[k], mesh_sizes) for k in range(n))
    vm = pl.BlockSpec(memory_space=pltpu.VMEM)
    scratch = []
    for k in range(n):
        scratch += [pltpu.VMEM(s, grads[k].dtype) for s in lists[k]]
    scratch += [pltpu.SemaphoreType.DMA((total,)), pltpu.SemaphoreType.DMA((total,))]
    return pl.pallas_call(
        functools.partial(reduce_kernel, mesh_sizes, shapes, [len(x) for x in lists]),
        out_shape=[jax.ShapeDtypeStruct(s, F32) for s in shapes],
        in_specs=[vm] * n,
        out_specs=[vm] * n,
        scratch_shapes=scratch,
        compiler_params=pltpu.CompilerParams(collective_id=1, has_side_effects=True, vmem_limit_bytes=60 << 20),
        name="reduce_gradients",
    )(*grads)


def adam_kernel(shapes, count, *refs):
    n = len(shapes)
    refs = list(refs)
    rows_in, grads, means, squares = refs[:count], refs[count:count + n], refs[count + n:count + 2 * n], refs[count + 2 * n:count + 3 * n]
    refs = refs[count + 3 * n:]
    rows_out, outs, held, sem = refs[:count], refs[count:-count - 1], refs[-count - 1:-1], refs[-1]
    copies = [pltpu.make_async_copy(a, b, sem.at[i]) for i, (a, b) in enumerate(zip(rows_in, held))]
    copies += [pltpu.make_async_copy(a, b, sem.at[count + i]) for i, (a, b) in enumerate(zip(held, rows_out))]
    for cp in copies[:count]:
        cp.start()
    for k, (rows, cols) in enumerate(shapes):
        change, mean, summed = outs[3 * k:3 * k + 3]
        if rows == 1:
            summed[...] = grads[k][:, 0:cols]
        else:
            rows_to_flat(grads[k], summed, rows, cols)
        change[...], mean[...] = adam(means[k][...], squares[k][...], summed[...])
        if k < count:
            copies[k].wait()
            copies[count + k].start()
    for cp in copies[count:]:
        cp.wait()


def adam_all(rows, grads, means, squares, shapes):
    vm, hb = pl.BlockSpec(memory_space=pltpu.VMEM), pl.BlockSpec(memory_space=pltpu.HBM)
    flat = [((r * c) // 128, 128) if r > 1 else (1, c) for r, c in shapes]
    count = len(rows)
    return pl.pallas_call(
        functools.partial(adam_kernel, shapes, count),
        out_shape=[jax.ShapeDtypeStruct(r.shape, F32) for r in rows] + [jax.ShapeDtypeStruct(f, F32) for f in flat for _ in range(3)],
        in_specs=[hb] * count + [vm] * (3 * len(shapes)),
        out_specs=[hb] * count + [vm] * (3 * len(shapes)),
        scratch_shapes=[pltpu.VMEM(r.shape, F32) for r in rows] + [pltpu.SemaphoreType.DMA((2 * count,))],
        name="adam",
    )(*rows, *grads, *means, *squares)

D = 512
HEADS = 8
HD = 64
FF = 2048
ROW = 1024
SEGS = 24
MOST = 512
QT = 256
KT = 128
PAIR = 128
NEG = -1000000000.0


def dot(a, b):
    return jnp.dot(a, b, preferred_element_type=F32)


def dot_t(a, b):
    return lax.dot_general(a, b, (((1,), (1,)), ((), ())), preferred_element_type=F32)


def t_dot(a, b):
    return lax.dot_general(a, b, (((0,), (0,)), ((), ())), preferred_element_type=F32)


def for_rows(block, f, rows=ROW):
    def step(i, _):
        f(pl.ds(pl.multiple_of(i * block, block), block))
        return 0

    lax.fori_loop(0, rows // block, step, 0)


def ends_of(lengths):
    out, total = [], jnp.int32(0)
    for i in range(SEGS):
        total = total + lengths[0, i]
        out.append(total)
    return out


def seg_at(ends, place):
    count = jnp.int32(0)
    for e in ends:
        count = count + (e <= place).astype(jnp.int32)
    return count


def pick(values, index):
    out = values[-1]
    for i in range(len(values) - 2, -1, -1):
        out = jnp.where(index <= i, values[i], out)
    return out


def seg_row(ends):
    place = lax.broadcasted_iota(jnp.int32, (1, ROW), 1)
    out = jnp.zeros((1, ROW), jnp.int32)
    for e in ends:
        out = out + (place >= e).astype(jnp.int32)
    return out.astype(F32)


def store_seg(ends, row_ref, col_ref):
    row_ref[...] = jnp.broadcast_to(seg_row(ends), (8, ROW))
    for i in range(ROW // 128):
        block = jnp.broadcast_to(row_ref[0:1, i * 128:(i + 1) * 128], (128, 128))
        col_ref[i * 128:(i + 1) * 128, :] = jnp.transpose(block)


def ranges(query_ends, key_ends, causal, tile, other, by_query):
    out = []
    here, there = (query_ends, key_ends) if by_query else (key_ends, query_ends)
    starts = [jnp.int32(0)] + there[:-1]
    for i in range(ROW // tile):
        first, last = i * tile, (i + 1) * tile - 1
        low = pick(starts, seg_at(here, first)) // other
        high = (pick(there, seg_at(here, last)) + other - 1) // other
        if causal and by_query:
            high = jnp.int32((i + 1) * tile // other)
        if causal and not by_query:
            low = jnp.int32(i * tile // other)
        out.append((low, high))
    return out


def store_ranges(ref, base, pairs):
    for i, (low, high) in enumerate(pairs):
        ref[base + 2 * i] = low
        ref[base + 2 * i + 1] = high


def head_masks():
    lane = lax.broadcasted_iota(jnp.int32, (1, PAIR), 1)
    left = (lane < HD).astype(F32).astype(BF)
    return left, (1.0 - left.astype(F32)).astype(BF)


def stack_heads(block, masks):
    return jnp.concatenate([block * masks[0], block * masks[1]], 0)


def block_diag(pair_t):
    zero = jnp.zeros((HD, pair_t.shape[1]), pair_t.dtype)
    top = jnp.concatenate([pair_t[:HD], zero], 1)
    low = jnp.concatenate([zero, pair_t[HD:]], 1)
    return jnp.concatenate([top, low], 0)


def bias_tile(key_col, query_row, k0, q0, causal):
    keys = key_col[pl.ds(k0, KT), :]
    keys = jnp.concatenate([keys] * (QT // 128), 1)
    ok = keys == query_row[0:1, pl.ds(q0, QT)]
    if causal:
        kpos = k0 + lax.broadcasted_iota(jnp.int32, (KT, QT), 0)
        qpos = q0 + lax.broadcasted_iota(jnp.int32, (KT, QT), 1)
        ok = ok & (kpos <= qpos)
    return jnp.where(ok, 0.0, NEG)


def norm_back(dh, xhat, rstd, gain):
    dx = dh * gain
    mean_dx = jnp.mean(dx, -1, keepdims=True)
    mean_xx = jnp.mean(dx * xhat, -1, keepdims=True)
    return rstd[:, 0:1] * (dx - mean_dx - xhat * mean_xx)


def fold(x):
    return jnp.sum(x.reshape(-1, 8, x.shape[-1]), 0)


def pipeline(count, *stages):
    values = {}
    last = len(stages) - 1
    for tick in range(count + last):
        for i in reversed(range(count)):
            st = tick - i
            if 0 <= st <= last:
                values[i] = stages[st](i) if st == 0 else stages[st](i, values[i])


def columns(hp):
    return slice(hp * PAIR, (hp + 1) * PAIR)


def score_tile(k0, q0, q, k, key_col, query_row, causal, scores, peak, masks):
    bias = bias_tile(key_col, query_row, k0, q0, causal)

    def meet(hp):
        return dot_t(stack_heads(k[pl.ds(k0, KT), columns(hp)], masks), q[pl.ds(q0, QT), columns(hp)])

    def keep(hp, s):
        for side in range(2):
            h = 2 * hp + side
            sh = s[side * KT:(side + 1) * KT] + bias
            scores[hp][pl.ds(k0, KT), side * QT:(side + 1) * QT] = sh
            peak[h] = jnp.maximum(peak[h], jnp.max(sh.reshape(KT // 8, 8, QT), 0))

    pipeline(HEADS // 2, meet, keep)


def weigh_tile(k0, vt, scores, acc, peak, tally):
    def weigh(hp):
        probs = []
        for side in range(2):
            h = 2 * hp + side
            sh = scores[hp][pl.ds(k0, KT), side * QT:(side + 1) * QT]
            p = jnp.exp(sh.reshape(KT // 8, 8, QT) - peak[h][None])
            tally[h] += jnp.sum(p, 0)
            probs.append(p.reshape(KT, QT).astype(BF))
        return jnp.concatenate(probs, 0)

    def spread(hp, probs):
        return dot(block_diag(vt[columns(hp), pl.ds(k0, KT)]), probs)

    def add(hp, o):
        acc[columns(hp), :] += o

    pipeline(HEADS // 2, weigh, spread, add)


def attend(tile, span, q, k, vt, key_col, query_row, causal, out, lse, scores, acc, peak, tally, pump=None):
    masks = head_masks()
    q0 = pl.multiple_of(tile * QT, QT) if not isinstance(tile, int) else tile * QT
    first, end = span
    peak[...] = jnp.full_like(peak, -3e38)

    def score(j, _):
        score_tile(pl.multiple_of(j * KT, KT), q0, q, k, key_col, query_row, causal, scores, peak, masks)
        return 0

    lax.fori_loop(first, end, score, 0)
    if pump:
        pump()
    for h in range(HEADS):
        peak[h] = jnp.broadcast_to(jnp.max(peak[h], 0, keepdims=True), (8, QT))
    acc[...] = jnp.zeros_like(acc)
    tally[...] = jnp.zeros_like(tally)

    def weigh(j, _):
        weigh_tile(pl.multiple_of(j * KT, KT), vt, scores, acc, peak, tally)
        return 0

    lax.fori_loop(first, end, weigh, 0)
    if pump:
        pump()
    for hp in range(HEADS // 2):
        rows = []
        for side in range(2):
            h = 2 * hp + side
            total = jnp.sum(tally[h], 0, keepdims=True)
            lse[h:h + 1, pl.ds(q0, QT)] = peak[h, 0:1, :] + jnp.log(total)
            rows.append(acc[hp * PAIR + side * HD:hp * PAIR + (side + 1) * HD, :] * (1.0 / total))
        out[pl.ds(q0, QT), hp * PAIR:(hp + 1) * PAIR] = jnp.transpose(jnp.concatenate(rows, 0)).astype(BF)


def attend_back(tile, span, k, v, kt, qt, gt, lse, inner, key_col, query_row, causal, dqt, dk, dv, dk_acc, dv_acc):
    masks = head_masks()
    k0 = pl.multiple_of(tile * KT, KT) if not isinstance(tile, int) else tile * KT
    dk_acc[...] = jnp.zeros_like(dk_acc)
    dv_acc[...] = jnp.zeros_like(dv_acc)

    def step(i, _):
        q0 = pl.multiple_of(i * QT, QT)
        bias = bias_tile(key_col, query_row, k0, q0, causal)
        at = pl.ds(q0, QT)

        def meet(hp):
            cols = columns(hp)
            s = dot(stack_heads(k[pl.ds(k0, KT), cols], masks), qt[cols, at])
            return s, dot(stack_heads(v[pl.ds(k0, KT), cols], masks), gt[cols, at])

        def weigh(hp, both):
            s, dp = both
            probs, slopes = [], []
            for side in range(2):
                h = 2 * hp + side
                rows = slice(side * KT, (side + 1) * KT)
                p = jnp.exp(s[rows] + bias - lse[h:h + 1, at])
                slopes.append((p * (dp[rows] - inner[h:h + 1, at])).astype(BF))
                probs.append(p.astype(BF))
            return jnp.concatenate(probs, 0), jnp.concatenate(slopes, 0)

        def spread(hp, both):
            cols = columns(hp)
            probs, slopes = both
            to_q = dot(block_diag(kt[cols, pl.ds(k0, KT)]), slopes)
            return dot_t(gt[cols, at], probs), dot_t(qt[cols, at], slopes), to_q

        def add(hp, terms):
            to_v, to_k, to_q = terms
            for acc, to in ((dv_acc, to_v), (dk_acc, to_k)):
                acc[hp * PAIR:hp * PAIR + HD, :] += to[:HD, :KT]
                acc[hp * PAIR + HD:(hp + 1) * PAIR, :] += to[HD:, KT:]
            dqt[columns(hp), at] += to_q

        pipeline(HEADS // 2, meet, weigh, spread, add)
        return 0

    lax.fori_loop(span[0], span[1], step, 0)
    dk[pl.ds(k0, KT), :] = jnp.transpose(dk_acc[...]).astype(BF)
    dv[pl.ds(k0, KT), :] = jnp.transpose(dv_acc[...]).astype(BF)


def flip(src, dst):
    for i in range(ROW // 128):
        dst[:, i * 128:(i + 1) * 128] = jnp.transpose(src[i * 128:(i + 1) * 128, :])


def standard(r):
    centered = r - jnp.mean(r, -1, keepdims=True)
    spread = jnp.mean(centered * centered, -1, keepdims=True)
    scale = lax.rsqrt(spread + 1e-05)
    return centered * scale, scale


def into_attention(g, c, inner, at, heads):
    both = g.astype(F32) * c.astype(F32)
    high = both.astype(BF)
    low = (both - high.astype(F32)).astype(BF)
    inner[:, at] = dot_t(heads, high) + dot_t(heads, low)


def head_rows():
    at = lax.broadcasted_iota(jnp.int32, (HEADS, D), 1) // HD == lax.broadcasted_iota(jnp.int32, (HEADS, D), 0)
    return at.astype(F32).astype(BF)


class Mover:
    def __init__(self, sems):
        self.sems, self.used, self.out = sems, 0, []

    def start(self, src, dst):
        cp = pltpu.make_async_copy(src, dst, self.sems.at[self.used])
        self.used += 1
        cp.start()
        return cp

    def store(self, src, dst):
        self.out.append(self.start(src, dst))

    def finish(self):
        for cp in self.out:
            cp.wait()


def own_spans():
    return [(max(0, (i * QT - MOST + 1) // KT), (i + 1) * QT // KT) for i in range(ROW // QT)]


def own_spans_back():
    return [(j * KT // QT, min(ROW // QT, ((j + 1) * KT - 1 + MOST - 1) // QT + 1)) for j in range(ROW // KT)]


def front_compute(x, mem, win, wout, norms, q1, k1, v1, c1, lse1, xh1, rs1, q2, k2, v2, trow, tcol, vt, scores, acc, peak, tally, ready, pump):
    ready("first")
    for i in range(ROW // 256):
        at = slice(i * 256, (i + 1) * 256)
        for out, w in ((q1, 0), (k1, 1), (v1, 2)):
            y = dot(x[at, :], win[w * D:(w + 1) * D, :]).astype(BF)
            out[at, :] = y * BF(0.125) if w == 0 else y
        pump()
    ready("projected")
    flip(v1, vt)
    for i, span in enumerate(own_spans()):
        attend(i, span, q1, k1, vt, tcol, trow, True, c1, lse1, scores, acc, peak, tally, pump)
    ready("second")
    for i in range(ROW // 256):
        at = slice(i * 256, (i + 1) * 256)
        for out, w in ((k2, 4), (v2, 5)):
            out[at, :] = dot(mem[at, :], win[w * D:(w + 1) * D, :]).astype(BF)
        pump()
    ready("keys")
    for i in range(ROW // 256):
        at = slice(i * 256, (i + 1) * 256)
        xhat, scale = standard(x[at, :].astype(F32) + dot(c1[at, :], wout[0:D, :]))
        xh1[at, :] = xhat
        rs1[at, :] = jnp.broadcast_to(scale, (256, 128))
        h = xhat * norms[0:1, :] + norms[3:4, :]
        q2[at, :] = dot(h.astype(BF), win[3 * D:4 * D, :]).astype(BF) * BF(0.125)
        pump()


FRONT_OUTS = (
    ((ROW, D), BF), ((ROW, D), BF), ((ROW, D), BF), ((ROW, D), BF), ((HEADS, ROW), F32),
    ((ROW, D), F32), ((ROW, 128), F32), ((ROW, D), BF), ((ROW, D), BF), ((ROW, D), BF),
)
KEPT = len(FRONT_OUTS)


def front_scratch():
    return (
        [pltpu.VMEM(s, d) for s, d in FRONT_OUTS]
        + [pltpu.VMEM((8, ROW), F32), pltpu.VMEM((ROW, 128), F32), pltpu.VMEM((D, ROW), BF)]
        + [pltpu.VMEM((ROW, D), F32)] * 4
        + [pltpu.VMEM((D, QT), F32), pltpu.VMEM((HEADS, 8, QT), F32), pltpu.VMEM((HEADS, 8, QT), F32)]
        + [pltpu.VMEM((ROW, D), BF)] * 2
        + [pltpu.VMEM((6 * D, D), BF), pltpu.VMEM((2 * D, D), BF), pltpu.SemaphoreType.DMA((40,))]
    )


def take(refs, k):
    out = refs[:k]
    del refs[:k]
    return out


SEG_OUTS = (((8, ROW), F32), ((ROW, 128), F32), ((ROW, 128), F32))


def segments_of(tlen, slen, trow, tcol, scol, table):
    tends, sends = ends_of(tlen), ends_of(slen)
    store_seg(sends, trow, scol)
    store_seg(tends, trow, tcol)
    store_ranges(table, 0, ranges(tends, sends, False, QT, KT, True))
    store_ranges(table, 8, ranges(tends, sends, False, KT, QT, False))


def front_kernel(tlen, slen, x, mem, win, wout, norms, *refs):
    refs = list(refs)
    outs, segs, table, kept = take(refs, 10), take(refs, 3), refs.pop(0), take(refs, 10)
    trow, tcol, vt = take(refs, 3)
    scores, (acc, peak, tally), (xs, ms, ws, os, sems, scol) = take(refs, 4), take(refs, 3), refs
    mover = Mover(sems)
    coming = [mover.start(x, xs), mover.start(win, ws), mover.start(wout, os), mover.start(mem, ms)]
    segments_of(tlen, slen, trow, tcol, scol, table)
    for k, ref in enumerate((trow, tcol, scol)):
        mover.store(ref, segs[k])

    def ready(stage):
        if stage == "first":
            coming[0].wait()
            coming[1].wait()
        if stage == "second":
            coming[2].wait()
            coming[3].wait()

    front_compute(xs, ms, ws, os, norms, *kept, trow, tcol, vt, scores, acc, peak, tally, ready, lambda: None)
    for k in range(10):
        mover.store(kept[k], outs[k])
    mover.finish()


def middle_kernel(
    tlen, table, mem, cot, q2, k2, v2, xh1, win, wout, up, down, norms, rows_in, cols_in,
    result, dk_out, dv_out, dh1, gin, gout, gup, gdown, gnorm,
    mem_s, cot_s, q_s, k_s, v_s, xh_s, win_s, wout_s, up_s, down_s,
    result_s, dk, dv, dh1_s, gin_s, gout_s, gup_s, gdown_s,
    trow, scol, flipped, qt, gt, c2, lse, inner, acc, peak, tally, spare, other, dr,
    h1b, h2b, act, du, dy, pre, turn, dc, dq, dqt, dk_acc, dv_acc, sems,
):
    mover = Mover(sems)
    pairs = (
        (k2, k_s), (q2, q_s), (v2, v_s), (wout.at[pl.ds(D, D)], wout_s), (xh1, xh_s), (up, up_s), (down, down_s),
        (cot, cot_s), (win.at[pl.ds(3 * D, D)], win_s), (mem, mem_s),
    )
    segs = [mover.start(rows_in, trow), mover.start(cols_in, scol)]
    coming = [mover.start(a, b) for a, b in pairs]
    gnorm[...] = jnp.zeros_like(gnorm)
    heads = head_rows()
    for cp in segs + coming[:3]:
        cp.wait()
    flip(v_s, flipped)

    def forward(i, _):
        span = (table[2 * i], table[2 * i + 1])
        attend(i, span, q_s, k_s, flipped, scol, trow, False, c2, lse, (other, dh1_s, dr, spare), acc, peak, tally)
        return 0

    lax.fori_loop(0, ROW // QT, forward, 0)
    for k in range(3, 8):
        coming[k].wait()
    live_end = ends_of(tlen)[SEGS - 2]
    block = 256

    def rows(i, _):
        at = pl.ds(pl.multiple_of(i * block, block), block)
        h = xh_s[at, :] * norms[0:1, :] + norms[3:4, :]
        h1b[at, :] = h.astype(BF)
        xh2, rs2 = standard(h + dot(c2[at, :], wout_s[...]))
        h = xh2 * norms[1:2, :] + norms[4:5, :]
        hb = h.astype(BF)
        h2b[at, :] = hb
        r3 = h
        for j in range(FF // D):
            cols = slice(j * D, (j + 1) * D)
            u = dot(hb, up_s[:, cols])
            pre[:, cols] = u
            a = (u / (1.0 + jnp.exp(-u))).astype(BF)
            act[at, cols] = a
            r3 = r3 + dot(a, down_s[cols, :])
        xhat, rstd = standard(r3)
        result_s[at, :] = (xhat * norms[2:3, :] + norms[5:6, :]).astype(BF)
        place = i * block + lax.broadcasted_iota(jnp.int32, (block, D), 0)
        seed = jnp.where(place < live_end, cot_s[at, :].astype(F32), 0.0)
        gnorm[0:8, :] += fold(seed * xhat)
        gnorm[8:16, :] += fold(seed)
        dr3 = norm_back(seed, xhat, rstd, norms[2:3, :])
        dyb = dr3.astype(BF)
        dy[at, :] = dyb
        dh = dr3
        for j in range(FF // D):
            cols = slice(j * D, (j + 1) * D)
            da = dot_t(dyb, down_s[cols, :])
            u = pre[:, cols]
            sig = 1.0 / (1.0 + jnp.exp(-u))
            d = (da * (sig * (1.0 + u * (1.0 - sig)))).astype(BF)
            du[at, cols] = d
            dh = dh + dot_t(d, up_s[:, cols])
        gnorm[16:24, :] += fold(dh * xh2)
        gnorm[24:32, :] += fold(dh)
        r = norm_back(dh, xh2, rs2, norms[1:2, :])
        dr[at, :] = r
        rb = r.astype(BF)
        dy2 = dot_t(rb, wout_s[...]).astype(BF)
        turn[at, :] = rb
        dc[at, :] = dy2
        into_attention(dy2, c2[at, :], inner, at, heads)
        return 0

    lax.fori_loop(0, ROW // block, rows, 0)
    mover.store(result_s, result)
    for j in range(FF // D):
        cols = slice(j * D, (j + 1) * D)
        gdown_s[cols, :] = t_dot(act[:, cols], dy[...]).astype(BF)
    mover.store(gdown_s, gdown)
    for j in range(FF // D):
        cols = slice(j * D, (j + 1) * D)
        gup_s[:, cols] = t_dot(h2b[...], du[:, cols]).astype(BF)
    mover.store(gup_s, gup)
    gout_s[...] = t_dot(c2[...], turn[...]).astype(BF)
    mover.store(gout_s, gout)
    flip(k_s, flipped)
    flip(q_s, qt)
    flip(dc, gt)
    dqt[...] = jnp.zeros_like(dqt)

    def backward(j, _):
        span = (table[8 + 2 * j], table[9 + 2 * j])
        attend_back(j, span, k_s, v_s, flipped, qt, gt, lse, inner, scol, trow, False, dqt, dk, dv, dk_acc, dv_acc)
        return 0

    lax.fori_loop(0, ROW // KT, backward, 0)
    mover.store(dk, dk_out)
    mover.store(dv, dv_out)
    coming[8].wait()
    coming[9].wait()
    gin_s[D:2 * D, :] = t_dot(mem_s[...], dk[...]).astype(BF)
    gin_s[2 * D:3 * D, :] = t_dot(mem_s[...], dv[...]).astype(BF)

    def end(at):
        q = jnp.transpose(dqt[:, at] * 0.125).astype(BF)
        dq[at, :] = q
        dh1_s[at, :] = dr[at, :] + dot_t(q, win_s[...])

    for_rows(256, end)
    mover.store(dh1_s, dh1)
    gin_s[0:D, :] = t_dot(h1b[...], dq[...]).astype(BF)
    mover.store(gin_s, gin)
    mover.finish()


def back_compute(
    x, q1, k1, v1, c1, lse, xh1, rs1, dh1, win, wout, dk2, dv2, win2, norms, tgrad, mgrad, gin, gout, gnorm,
    trow, tcol, kt, qt, gt, inner, dr, dc, dq, dk, dv, dqt, dk_acc, dv_acc, ready, pump,
):
    heads = head_rows()
    ready("first")
    for i in range(ROW // 256):
        at = slice(i * 256, (i + 1) * 256)
        dh, xhat = dh1[at, :], xh1[at, :]
        gain, bias = fold(dh * xhat), fold(dh)
        gnorm[0:8, :] = gain if i == 0 else gnorm[0:8, :] + gain
        gnorm[8:16, :] = bias if i == 0 else gnorm[8:16, :] + bias
        r = norm_back(dh, xhat, rs1[at, :], norms[0:1, :])
        dr[at, :] = r
        rb = r.astype(BF)
        g = dot_t(rb, wout[...]).astype(BF)
        dq[at, :] = rb
        dc[at, :] = g
        into_attention(g, c1[at, :], inner, at, heads)
        pump()
    gout[...] = t_dot(c1[...], dq[...]).astype(BF)
    ready("outward")
    flip(k1, kt)
    flip(q1, qt)
    flip(dc, gt)
    pump()
    dqt[...] = jnp.zeros_like(dqt)
    for j, span in enumerate(own_spans_back()):
        attend_back(j, span, k1, v1, kt, qt, gt, lse, inner, tcol, trow, True, dqt, dk, dv, dk_acc, dv_acc)
        pump()
    gin[D:2 * D, :] = t_dot(x[...], dk[...]).astype(BF)
    gin[2 * D:3 * D, :] = t_dot(x[...], dv[...]).astype(BF)
    for i in range(ROW // 256):
        at = slice(i * 256, (i + 1) * 256)
        dq[at, :] = jnp.transpose(dqt[:, at] * 0.125).astype(BF)
    gin[0:D, :] = t_dot(x[...], dq[...]).astype(BF)
    ready("inward")
    for i in range(ROW // 256):
        at = slice(i * 256, (i + 1) * 256)
        t = dr[at, :]
        for k, g in enumerate((dq, dk, dv)):
            t = t + dot_t(g[at, :], win[k * D:(k + 1) * D, :])
        tgrad[at, :] = t
        pump()
    ready("target")
    for i in range(ROW // 256):
        at = slice(i * 256, (i + 1) * 256)
        mgrad[at, :] = dot_t(dk2[at, :], win2[0:D, :]) + dot_t(dv2[at, :], win2[D:2 * D, :])
        pump()
    ready("memory")


BACK_INS = (
    ((ROW, D), BF), ((ROW, D), BF), ((ROW, D), BF), ((ROW, D), BF), ((ROW, D), BF), ((HEADS, ROW), F32),
    ((ROW, D), F32), ((ROW, 128), F32), ((ROW, D), F32), ((3 * D, D), BF), ((D, D), BF),
    ((ROW, D), BF), ((ROW, D), BF), ((2 * D, D), BF),
)
TAKEN = len(BACK_INS)


def back_scratch():
    return (
        [pltpu.VMEM(s, d) for s, d in BACK_INS]
        + [pltpu.VMEM((ROW, D), F32)] * 2
        + [pltpu.VMEM((8, ROW), F32), pltpu.VMEM((ROW, 128), F32)]
        + [pltpu.VMEM((D, ROW), BF)] * 3
        + [pltpu.VMEM((HEADS, ROW), F32), pltpu.VMEM((ROW, D), F32)]
        + [pltpu.VMEM((ROW, D), BF)] * 4
        + [pltpu.VMEM((D, ROW), F32), pltpu.VMEM((D, KT), F32), pltpu.VMEM((D, KT), F32), pltpu.SemaphoreType.DMA((40,))]
    )


def back_loads(mover, ins, kept):
    win, wout = ins[9], ins[10]
    parts = list(ins[:9]) + [win.at[pl.ds(0, 3 * D)], wout.at[pl.ds(0, D)], ins[11], ins[12], win.at[pl.ds(4 * D, 2 * D)]]
    order = (8, 6, 7, 10, 4, 2, 1, 3, 5, 0, 9, 11, 12, 13)
    return [mover.start(parts[k], kept[k]) for k in order]


def back_kernel(norms, *refs):
    refs = list(refs)
    ins, segs, (tgrad, mgrad, gin, gout, gnorm), kept = take(refs, TAKEN - 1), take(refs, 2), take(refs, 5), take(refs, TAKEN)
    (tgrad_s, mgrad_s), work, sems = refs[:2], refs[2:-1], refs[-1]
    mover = Mover(sems)
    coming = [mover.start(segs[0], work[0]), mover.start(segs[1], work[1])] + back_loads(mover, ins, kept)

    def ready(stage):
        if stage == "first":
            for cp in coming:
                cp.wait()

    back_compute(*kept, norms, tgrad_s, mgrad_s, gin, gout, gnorm, *work, ready, lambda: None)
    mover.store(tgrad_s, tgrad)
    mover.store(mgrad_s, mgrad)
    mover.finish()


VM = pl.BlockSpec(memory_space=pltpu.VMEM)
SM = pl.BlockSpec(memory_space=pltpu.SMEM)
HB = pl.BlockSpec(memory_space=pltpu.HBM)


def call(kernel, name, ins, in_specs, outs, out_specs, scratch, params):
    return pl.pallas_call(
        kernel,
        out_shape=[jax.ShapeDtypeStruct(s, d) for s, d in outs],
        in_specs=in_specs,
        out_specs=out_specs,
        scratch_shapes=scratch,
        compiler_params=pltpu.CompilerParams(vmem_limit_bytes=62 << 20, **params),
        name=name,
    )(*ins)


def middle(tlen, table, mem, cot, q2, k2, v2, xh1, win, wout, up, down, norms, trow, scol):
    tok, tokf, flat = ((ROW, D), BF), ((ROW, D), F32), ((D, ROW), BF)
    outs = [tok, tok, tok, tokf, ((3 * D, D), BF), ((D, D), BF), ((D, FF), BF), ((FF, D), BF)]
    ins = [tok] * 5 + [tokf, ((D, D), BF), ((D, D), BF), ((D, FF), BF), ((FF, D), BF)]
    stat, tile = ((HEADS, ROW), F32), ((D, KT), F32)
    work = [((8, ROW), F32), ((ROW, 128), F32), flat, flat, flat, tok, stat, stat, ((D, QT), F32), ((HEADS, 8, QT), F32),
            ((HEADS, 8, QT), F32), tokf, tokf, tokf, tok, tok, ((ROW, FF), BF), ((ROW, FF), BF), tok, ((256, FF), F32), tok, tok, tok,
            ((D, ROW), F32), tile, tile]
    scratch = [pltpu.VMEM(*s) for s in ins + outs + work]
    return call(
        middle_kernel, "middle", [tlen, table, mem, cot, q2, k2, v2, xh1, win, wout, up, down, norms, trow, scol],
        [SM, SM] + [HB] * 10 + [VM, HB, HB], outs + [((32, D), F32)], [HB] * 8 + [VM],
        scratch + [pltpu.SemaphoreType.DMA((20,))], {},
    )


def layer(tlen, slen, x, mem, cot, win, wout, up, down, norms):
    q1, k1, v1, c1, lse1, xh1, rs1, q2, k2, v2, trow, tcol, scol, table = call(
        front_kernel, "front", [tlen, slen, x, mem, win, wout, norms], [SM, SM] + [HB] * 4 + [VM],
        [*FRONT_OUTS, *SEG_OUTS, ((32,), jnp.int32)], [HB] * 13 + [SM], front_scratch() + [pltpu.VMEM((ROW, 128), F32)], {},
    )
    result, dk2, dv2, dh1, gin_two, gout_two, gup, gdown, gnorm_rest = middle(
        tlen, table, mem, cot, q2, k2, v2, xh1, win, wout, up, down, norms, trow, scol)
    tgrad, mgrad, gin_one, gout_one, gnorm_one = call(
        back_kernel, "back", [norms, x, q1, k1, v1, c1, lse1, xh1, rs1, dh1, win, wout, dk2, dv2, trow, tcol],
        [VM] + [HB] * (TAKEN + 1),
        [((ROW, D), F32), ((ROW, D), F32), ((3 * D, D), BF), ((D, D), BF), ((16, D), F32)], [HB, HB, VM, VM, VM], back_scratch(), {},
    )
    gin, gout = jnp.concatenate([gin_one, gin_two]), jnp.concatenate([gout_one, gout_two])
    one = jnp.sum(gnorm_one.reshape(2, 8, D), 1)
    rest = jnp.sum(gnorm_rest.reshape(4, 8, D), 1)
    gnorm = jnp.stack([one[0], rest[2], rest[0], one[1], rest[3], rest[1]])
    return result, tgrad, mgrad, gin, gout, gup, gdown, gnorm


def every(dims):
    return [(a, b, c, e) for a in range(dims[0]) for b in range(dims[1]) for c in range(dims[2]) for e in range(dims[3])]


def lanes_up_to(n):
    return lax.broadcasted_iota(jnp.int32, (8, 128), 1) < n


def norms_from_shards(shards, lined, flat, out):
    for i, at in enumerate(every(shards.shape[:4])):
        lined[i:i + 1, :] = shards[at]
    n = [lined[pl.ds(k, 8, stride=4), :] for k in range(4)]
    flat[pl.ds(0, 8, stride=3), :] = jnp.where(lanes_up_to(96), n[0], pltpu.roll(n[1], 96, 1))
    flat[pl.ds(1, 8, stride=3), :] = jnp.where(lanes_up_to(64), pltpu.roll(n[1], 96, 1), pltpu.roll(n[2], 64, 1))
    flat[pl.ds(2, 8, stride=3), :] = jnp.where(lanes_up_to(32), pltpu.roll(n[2], 64, 1), pltpu.roll(n[3], 32, 1))
    for i in range(24):
        out[i // 4:i // 4 + 1, (i % 4) * 128:(i % 4 + 1) * 128] = flat[i:i + 1, :]


def norms_to_shards(rows, flat, lined, shards):
    for i in range(24):
        flat[i:i + 1, :] = rows[i // 4][:, (i % 4) * 128:(i % 4 + 1) * 128]
    r = [flat[pl.ds(k, 8, stride=3), :] for k in range(3)]
    lined[pl.ds(0, 8, stride=4), :] = r[0]
    lined[pl.ds(1, 8, stride=4), :] = jnp.where(lanes_up_to(32), pltpu.roll(r[0], 32, 1), pltpu.roll(r[1], 32, 1))
    lined[pl.ds(2, 8, stride=4), :] = jnp.where(lanes_up_to(64), pltpu.roll(r[1], 64, 1), pltpu.roll(r[2], 64, 1))
    lined[pl.ds(3, 8, stride=4), :] = pltpu.roll(r[2], 96, 1)
    for i, at in enumerate(every(shards.shape[:4])):
        shards[at] = lined[i:i + 1, :]


DONE = "done"


def until_done(flow):
    for _ in flow:
        yield None
    while True:
        yield DONE


def around(place, d):
    n = place.sizes[0]
    return lax.rem(place.at[0] + (d + n), n)


def spot(first, p, q, at_p, at_q, e):
    return (first, at_p, at_q, *e) if p < q else (first, at_q, at_p, *e)


def gather_bulk(place, ref, own, p, q, sems, span=None, part=None, before=None):
    n, e = place.sizes[0], place.at[3]
    low, high = span or (0, n)
    whole = (low, high) == (0, n)
    group = slice(None) if whole else pl.ds(low, high - low)
    rows = (pl.ds(*part),) if part else ()
    after = []

    def inside(coord):
        return None if whole else (coord >= low) & (coord < high)

    def view(first, flip_p, flip_q, core=None):
        at_p = 1 - place.at[p] if flip_p else place.at[p]
        at_q = slice(None) if flip_q is None else 1 - place.at[q] if flip_q else place.at[q]
        return ref.at[(*spot(first, p, q, at_p, at_q, (e if core is None else core,)), *rows)]

    def send(src, dst, device, cond=None):
        pair = sems.take()
        go = remote(src, dst, pair, device)
        when(cond, go.start)
        after.append((cond, go.wait_send))
        return lambda view: remote(view, view, pair, device)

    def to_sibling(flip_p, flip_q):
        come = send(view(group, flip_p, flip_q), view(group, flip_p, flip_q), place.device(3, 1 - e))
        after.append((None, come(view(group, flip_p, flip_q, 1 - e)).wait_recv))

    own = own.at[rows] if rows else own
    mine = inside(place.at[0])
    come = {}
    for d in range(1, n):
        come[d] = send(own, view(place.at[0], 0, 0), place.device(0, around(place, d)), mine)
    yield
    for d in range(1, n):
        src = around(place, -d)
        when(inside(src), come[d](view(src, 0, 0)).wait_recv)
    if before:
        before()
    here = view(group, 0, 0)
    to_p, to_q = place.device(p, 1 - place.at[p]), place.device(q, 1 - place.at[q])
    from_p, from_q = send(here, here, to_p), send(here, here, to_q)
    to_sibling(0, 0)
    yield
    there = view(group, 1, 0)
    from_p(there).wait_recv()
    from_pq = send(there, there, to_q)
    to_sibling(1, 0)
    yield
    from_q(view(group, 0, 1)).wait_recv()
    to_sibling(0, 1)
    from_pq(view(group, 1, 1)).wait_recv()
    to_sibling(1, 1)
    yield
    for cond, f in after:
        when(cond, f)


def gather_bulk_sems(sizes):
    return sizes[0] - 1 + 3 + 4


def add_rows(dst, *srcs):
    v = srcs[0][...].astype(F32)
    for s in srcs[1:]:
        v = v + s[...].astype(F32)
    dst[...] = v.astype(dst.dtype)


def reduce_bulk(place, grad, half, from_q, from_p, from_z, total, p, q, sems, low=0, part=None):
    n, e = place.sizes[0], place.at[3]
    count = grad.shape[0]
    whole = count == n
    rows = (pl.ds(*part),) if part else ()
    after = []
    me_p, me_q, all_of = place.at[p], place.at[q], slice(None)

    def inside(coord):
        return None if whole else (coord >= low) & (coord < low + count)

    def g(first, at_p, at_q, core):
        return grad.at[(*spot(first, p, q, at_p, at_q, (core,)), *rows)]

    def h(first, at_p, at_q):
        return half.at[(*spot(first, p, q, at_p, at_q, ()), *rows)]

    def send(src, dst, device, cond=None):
        go = remote(src, dst, sems.take(), device)
        when(cond, go.start)
        after.append((cond, go.wait_send))
        return go

    def each(f, times):
        def step(i, _):
            f(i)
            return 0

        lax.fori_loop(0, times, step, 0)

    sibling = place.device(3, 1 - e)
    core_q, core_p, core = [
        send(g(all_of, at_p, at_q, 1 - e), h(all_of, at_p, at_q), sibling)
        for at_p, at_q in ((all_of, 1 - me_q), (1 - me_p, me_q), (me_p, me_q))]
    yield
    core_q.wait_recv()

    def far(i):
        a, at_p = lax.div(i, 2), lax.rem(i, 2)
        add_rows(h(a, at_p, 1 - me_q), g(a, at_p, 1 - me_q, e), h(a, at_p, 1 - me_q))

    each(far, 2 * count)
    come_q = send(h(all_of, all_of, 1 - me_q), from_q, place.device(q, 1 - me_q))
    yield
    core_p.wait_recv()
    come_q.wait_recv()
    each(lambda a: add_rows(h(a, 1 - me_p, me_q), g(a, 1 - me_p, me_q, e), h(a, 1 - me_p, me_q), from_q.at[a, 1 - me_p]), count)
    come_p = send(h(all_of, 1 - me_p, me_q), from_p, place.device(p, 1 - me_p))
    yield
    core.wait_recv()
    come_p.wait_recv()
    each(lambda a: add_rows(h(a, me_p, me_q), g(a, me_p, me_q, e), h(a, me_p, me_q), from_q.at[a, me_p], from_p.at[a]), count)
    come_z = []
    for d in range(1, n):
        to = around(place, d)
        pair = sems.take()
        go = remote(h(to - low, me_p, me_q), from_z.at[d - 1], pair, place.device(0, to))
        when(inside(to), go.start)
        after.append((inside(to), go.wait_send))
        come_z.append(remote(from_z.at[d - 1], from_z.at[d - 1], pair, place.device(0, to)))
    yield

    def close():
        for come in come_z:
            come.wait_recv()
        add_rows(total.at[rows] if rows else total, h(place.at[0] - low, me_p, me_q), *[from_z.at[d] for d in range(n - 1)])

    when(inside(place.at[0]), close)
    for cond, f in after:
        when(cond, f)


def reduce_bulk_sems(sizes):
    return 5 + sizes[0] - 1


def reduce_bulk_bufs(sizes, count, shape):
    return [(count, 2, *shape), (count, *shape), (sizes[0] - 1, *shape)]


def front_remote_kernel(sizes, shapes, tlen, slen, x, mem, *refs):
    refs = list(refs)
    masters = take(refs, 5)
    outs, segs, (win, wout, up, down, norms, table), kept = take(refs, KEPT), take(refs, 3), take(refs, 6), take(refs, KEPT)
    trow, tcol, vt = take(refs, 3)
    scores, (acc, peak, tally), (xs, ms, ws, os, sems) = take(refs, 4), take(refs, 3), take(refs, 5)
    scol, stage_up, stage_down, shards, lined, flat, send, recv = refs
    place, mover = Place(sizes), Mover(sems)
    coming = [mover.start(x, xs), mover.start(mem, ms)]
    mine = [ws.at[place.at], os.at[place.at], stage_up, stage_down]
    for k in range(4):
        flat_to_rows(masters[k], mine[k], *shapes[k])
    shards[place.at] = jnp.zeros((1, 128), F32)
    width = masters[4].shape[1]
    shards[(*place.at, slice(None), slice(0, width))] = masters[4][...].astype(BF).astype(F32)
    local = [mover.start(stage_up, up.at[place.at]), mover.start(stage_down, down.at[place.at])]
    pool, half, rows = Sems(send, recv), sizes[0] // 2, shapes[0][0] // 2
    low, high, top, low_rows = (0, half), (half, sizes[0]), (0, rows), (rows, rows)

    def flow(ref, own, p, q, *rest):
        return until_done(gather_bulk(place, ref, own, p, q, pool, *rest))

    place.greet(True)
    inward, outward = ws.at[place.at], os.at[place.at]
    flows_by = {
        "a": flow(ws, inward, 2, 1, low, top), "b": flow(ws, inward, 1, 2, low, low_rows),
        "c": flow(ws, inward, 2, 1, high, top), "d": flow(ws, inward, 1, 2, high, low_rows),
        "o": flow(os, outward, 1, 2), "n": flow(shards, shards.at[place.at], 1, 2),
        "u": flow(up, stage_up, 2, 1, None, None, local[0].wait), "v": flow(down, stage_down, 1, 2, None, None, local[1].wait),
    }

    def go_on(names):
        for name in names:
            if name in flows_by and next(flows_by[name]) is DONE:
                del flows_by[name]

    def finish(names):
        while set(names) & set(flows_by):
            go_on(names)

    go_on(BEGIN)
    segments_of(tlen, slen, trow, tcol, scol, table)
    for k, ref in enumerate((trow, tcol, scol)):
        mover.store(ref, segs[k])
    go_on(FIRST)
    finish("ab")
    count = [0]

    def pump():
        count[0] += 1
        go_on(FRONT_PLAN.get(count[0], ""))

    def ready(stage):
        if stage == "first":
            coming[0].wait()
        if stage == "projected":
            for k in range(3):
                mover.store(kept[k], outs[k])
        if stage == "second":
            finish("cdon")
            mover.store(ws, win)
            mover.store(os, wout)
            norms_from_shards(shards, lined, flat, norms)
            coming[1].wait()
        if stage == "keys":
            for k in (3, 4, 8, 9):
                mover.store(kept[k], outs[k])

    front_compute(
        xs, ms, ws.reshape(6 * D, D), os.reshape(2 * D, D), norms, *kept, trow, tcol, vt, scores, acc, peak, tally, ready, pump)
    for k in (5, 6, 7):
        mover.store(kept[k], outs[k])
    finish("uv")
    mover.finish()


BEGIN = "abcdon"
FIRST = "ababcdonuvabab"
FRONT_PLAN = {1: "cdon", 5: "uv", 6: "cdon", 10: "cdon", 11: "uv", 16: "uv"}


def front_remote(sizes, shapes, tlen, slen, x, mem, masters):
    weights = [((*sizes, *s), BF) for s in shapes[:4]]
    count = 8 * gather_bulk_sems(sizes)
    scratch = front_scratch()
    scratch[-3:-1] = [pltpu.VMEM(*w) for w in weights[:2]]
    return call(
        functools.partial(front_remote_kernel, sizes, shapes), "front", [tlen, slen, x, mem, *masters],
        [SM, SM, HB, HB] + [VM] * 5, (*FRONT_OUTS, *SEG_OUTS, *weights, ((6, D), F32), ((32,), jnp.int32)),
        [HB] * (KEPT + 7) + [VM, SM],
        scratch
        + [pltpu.VMEM((ROW, 128), F32), pltpu.VMEM(shapes[2], BF), pltpu.VMEM(shapes[3], BF), pltpu.VMEM((*sizes, 1, 128), F32),
           pltpu.VMEM((32, 128), F32), pltpu.VMEM((24, 128), F32)]
        + [pltpu.SemaphoreType.DMA((count,))] * 2,
        dict(collective_id=0, has_side_effects=True),
    )


def back_remote_kernel(sizes, shapes, norms, rest, *refs):
    refs = list(refs)
    ins, segs, grads, (tgrad, mgrad), totals = take(refs, TAKEN - 1), take(refs, 2), take(refs, 4), take(refs, 2), take(refs, 5)
    kept, (tgrad_s, mgrad_s), work = take(refs, TAKEN), take(refs, 2), take(refs, 14)
    sems, gin, gout, gnorm, lined, flat, shards = take(refs, 7)
    staged, halves = take(refs, 4), take(refs, 7)
    bufs, (send, recv) = [take(refs, 3) for _ in range(8)], refs
    place, mover = Place(sizes), Mover(sems)
    loads = [mover.start(grads[k], staged[k]) for k in (3, 2, 0, 1)]
    coming = [mover.start(segs[0], work[0]), mover.start(segs[1], work[1])] + back_loads(mover, ins, kept)
    place.greet(True)
    pool, half = Sems(send, recv), sizes[0] // 2
    flows_by = {}

    def begin(name, k, grad, into, total, p, q, low=0, part=None):
        flows_by[name] = until_done(reduce_bulk(place, grad, into, *bufs[k], total, p, q, pool, low, part))
        next(flows_by[name])

    def go_on(names):
        for name in names:
            if name in flows_by and next(flows_by[name]) is DONE:
                del flows_by[name]

    for name, cp, k, p, q, low in zip("duio", loads, (3, 2, 0, 1), (2, 1, 2, 1), (1, 2, 1, 2), (0, 0, half, half)):
        cp.wait()
        begin(name, k, staged[k], halves[k], totals[k], p, q, low)
    count = [0]

    def pump():
        count[0] += 1
        go_on(PLAN.get(count[0], ""))

    def ready(stage):
        if stage == "first":
            for cp in coming[:-3]:
                cp.wait()
        if stage == "target":
            mover.store(tgrad_s, tgrad)
            for cp in coming[-3:]:
                cp.wait()
        if stage == "memory":
            mover.store(mgrad_s, mgrad)
        if stage == "outward":
            begin("w", 4, gout, halves[5], totals[1], 1, 2)
            one = [jnp.sum(gnorm[8 * i:8 * i + 8, :], 0, keepdims=True) for i in range(2)]
            more = [jnp.sum(rest[8 * i:8 * i + 8, :], 0, keepdims=True) for i in range(4)]
            norms_to_shards([one[0], more[2], more[0], one[1], more[3], more[1]], flat, lined, shards)
            begin("n", 5, shards, halves[6], totals[4], 1, 2)
        if stage == "inward":
            rows = shapes[0][0] // 2
            begin("a", 6, gin, halves[4], totals[0], 2, 1, 0, (0, rows))
            begin("b", 7, gin, halves[4], totals[0], 1, 2, 0, (rows, rows))

    back_compute(
        *kept, norms, tgrad_s, mgrad_s, gin.reshape(3 * D, D), gout.reshape(D, D), gnorm, *work, ready, pump)
    go_on(REST)
    while flows_by:
        go_on("abiowndu")
    mover.finish()


PLAN = {3: "du", 4: "io", 8: "duwn", 10: "duo", 12: "wni", 13: "wn", 15: "ab", 16: "io"}
REST = "ab"


def back_remote(sizes, shapes, norms, rest, ins, segs, grads):
    half = sizes[0] // 2
    counts = (half, half, sizes[0], sizes[0])
    grads = [g.reshape(n, *sizes[1:], *s) for g, n, s in zip(grads, counts, shapes)]
    halves = [((n, *sizes[1:3], *s), BF) for n, s in zip((*counts, half, half), (*shapes[:4], *shapes[:2]))]
    halves.append(((*sizes[:3], *shapes[4]), F32))
    rows, cols = shapes[0]
    flows_of = [(n, s, BF) for n, s in zip(counts, shapes)] + [
        (half, shapes[1], BF), (sizes[0], shapes[4], F32), (half, (rows // 2, cols), BF), (half, (rows // 2, cols), BF)]
    bufs = [pltpu.VMEM(s, d) for n, shape, d in flows_of for s in reduce_bulk_bufs(sizes, n, shape)]
    return call(
        functools.partial(back_remote_kernel, sizes, shapes), "back", [norms, rest, *ins, *segs, *grads],
        [VM, VM] + [HB] * (TAKEN + 5),
        [((ROW, D), F32)] * 2 + [(s, F32) for s in shapes], [HB] * 2 + [VM] * 5,
        back_scratch()
        + [pltpu.VMEM((half, *sizes[1:], *shapes[0]), BF), pltpu.VMEM((half, *sizes[1:], *shapes[1]), BF),
           pltpu.VMEM((16, D), F32), pltpu.VMEM((32, 128), F32), pltpu.VMEM((24, 128), F32), pltpu.VMEM((*sizes, 1, 128), F32)]
        + [pltpu.VMEM(g.shape, BF) for g in grads] + [pltpu.VMEM(*h) for h in halves]
        + bufs + [pltpu.SemaphoreType.DMA((8 * reduce_bulk_sems(sizes),))] * 2,
        dict(collective_id=1, has_side_effects=True),
    )


def shard_views(inward, outward, expand, shrink, norms):
    arrays, shapes = [], []
    for x, wide in ((inward, D), (outward, D), (expand, FF), (shrink, D)):
        cols = wide if x.shape[0] >= 16 * wide else D
        arrays.append(x.reshape(-1, 128))
        shapes.append((x.shape[0] // cols, cols))
    arrays.append(norms.reshape(1, -1))
    shapes.append((1, -(-norms.shape[0] // 128) * 128))
    return arrays, tuple(shapes)


def body(
    sizes, target, memory, cotangent, target_lengths, source_lengths,
    inward_master, inward_mean, inward_square, outward_master, outward_mean, outward_square,
    expand_master, expand_mean, expand_square, shrink_master, shrink_mean, shrink_square,
    norms_master, norms_mean, norms_square,
):
    flat, shapes = shard_views(inward_master, outward_master, expand_master, shrink_master, norms_master)
    norm_count = norms_master.shape[0]
    means, _ = shard_views(inward_mean, outward_mean, expand_mean, shrink_mean, norms_mean)
    squares, _ = shard_views(inward_square, outward_square, expand_square, shrink_square, norms_square)
    x, mem, cot = target[0], memory[0], cotangent[0]
    if sizes[1:] == (2, 2, 2) and norm_count == 96 and all(s[0] % 16 == 0 for s in shapes[:4]):
        *kept, trow, tcol, scol, win, wout, up, down, norms, table = front_remote(
            sizes, shapes, target_lengths, source_lengths, x, mem, flat)
        win, wout = win.reshape(6 * D, D), wout.reshape(2 * D, D)
        q1, k1, v1, c1, lse1, xh1, rs1, q2, k2, v2 = kept
        result, dk2, dv2, dh1, gin, gout, gup, gdown, rest = middle(
            target_lengths, table, mem, cot, q2, k2, v2, xh1, win, wout, up.reshape(D, FF), down.reshape(FF, D), norms,
            trow, scol)
        tgrad, mgrad, *sums = back_remote(
            sizes, shapes, norms, rest, [x, q1, k1, v1, c1, lse1, xh1, rs1, dh1, win, wout, dk2, dv2], [trow, tcol],
            [gin, gout, gup, gdown])
    else:
        padding = ((0, 0), (0, shapes[4][1] - norm_count))
        win, wout, up, down, norms = gather_all(
            sizes, [*flat[:4], jnp.pad(flat[4], padding)], shapes, [BF, BF, BF, BF, F32])
        norms = norms.reshape(-1, norms.shape[-1])[:, :norm_count].reshape(6, D)
        result, tgrad, mgrad, gin, gout, gup, gdown, gnorm = layer(
            target_lengths, source_lengths, x, mem, cot,
            win.reshape(6 * D, D), wout.reshape(2 * D, D), up.reshape(D, FF), down.reshape(FF, D), norms,
        )
        gnorm = jnp.pad(gnorm.reshape(-1, norm_count), padding)
        grads = [g.reshape(*sizes, *s) for g, s in zip((gin, gout, gup, gdown, gnorm), shapes)]
        sums = reduce_all(sizes, grads, shapes)
    tgrad, mgrad, *outs = adam_all([tgrad, mgrad], sums, means, squares, (*shapes[:4], (1, norm_count)))
    return (result[None], tgrad[None], mgrad[None], *[x.reshape(-1) for x in outs])


def solution(mesh):
    rows, cols = mesh.shape["dp"], mesh.shape["shard"]
    both = ("dp", "shard")
    row, flat = P(both, None, None), P(both)
    return jax.shard_map(
        functools.partial(body, (rows // 2, 2, cols // 2, 2)),
        mesh=mesh,
        in_specs=(row, row, row, P(both, None), P(both, None), *[flat] * 15),
        out_specs=(row, row, row, *[flat] * 15),
        check_vma=False,
    )
```

```python
import functools
import jax
import jax.numpy as jnp
from jax import lax
from jax.experimental import pallas as pl
from jax.experimental.pallas import tpu as pltpu
from jax.sharding import PartitionSpec as P

MESH = pl.DeviceIdType.MESH
BF = jnp.bfloat16
F32 = jnp.float32
learn_rate = 0.001
beta_one = 0.9
beta_two = 0.999
STEP = 10


class Place:
    def __init__(self, sizes):
        self.sizes = sizes
        dp, sh = lax.axis_index("dp"), lax.axis_index("shard")
        self.at = (dp // sizes[1], dp % sizes[1], sh // sizes[3], sh % sizes[3])

    def device(self, axis, coord):
        a, b, c, e = [coord if i == axis else v for i, v in enumerate(self.at)]
        return (a * self.sizes[1] + b, c * self.sizes[3] + e)

    def greet(self, far=False):
        barrier = pltpu.get_barrier_semaphore()
        count = 0
        for axis in range(4):
            n, me = self.sizes[axis], self.at[axis]
            if n == 2:
                pl.semaphore_signal(barrier, inc=1, device_id=self.device(axis, 1 - me), device_id_type=MESH)
                count = count + 1
            else:
                for step in [s for d in range(1, n if far else 2) for s in (-d, d)]:
                    there = me + step
                    ok = (there >= 0) & (there < n)

                    @pl.when(ok)
                    def _():
                        pl.semaphore_signal(barrier, inc=1, device_id=self.device(axis, there), device_id_type=MESH)

                    count = count + ok.astype(jnp.int32)
        pl.semaphore_wait(barrier, count)


class Sems:
    def __init__(self, send, recv):
        self.send, self.recv, self.used = send, recv, 0

    def take(self):
        k = self.used
        self.used += 1
        return self.send.at[k], self.recv.at[k]


def gather_sems(order, sizes):
    return 1 + sum(2 if sizes[x] == 2 else 4 * (sizes[x] - 1) for x in order)


def gather_rounds(place, ref, order, sems):
    sizes = place.sizes
    after = []
    held = []

    def group(axis=None, coord=None):
        idx = [slice(None) if i in held else place.at[i] for i in range(4)]
        if axis is not None:
            idx[axis] = coord
        return ref.at[tuple(idx)]

    def copy(block, axis, coord, pair):
        return pltpu.make_async_remote_copy(
            src_ref=block, dst_ref=block, send_sem=pair[0], recv_sem=pair[1],
            device_id=place.device(axis, coord), device_id_type=MESH)

    def to_sibling(axis, coord, cond):
        pair = sems.take()
        idx = [slice(None) if i in held else place.at[i] for i in range(4)]
        if axis is not None:
            idx[axis] = coord
        mine = ref.at[tuple(idx)]
        idx[3] = 1 - place.at[3]
        theirs = ref.at[tuple(idx)]
        e = place.at[3]
        go = copy(mine, 3, 1 - e, pair)
        come = copy(theirs, 3, 1 - e, pair)

        def run(f):
            if cond is None:
                f()
            else:
                pl.when(cond)(f)

        run(go.start)

        def finish():
            go.wait_send()
            come.wait_recv()

        after.append(lambda: run(finish))

    to_sibling(None, None, None)
    for axis in order:
        n, me = sizes[axis], place.at[axis]
        if n == 2:
            pair = sems.take()
            go = copy(group(), axis, 1 - me, pair)
            come = copy(group(axis, 1 - me), axis, 1 - me, pair)
            go.start()
            after.append(go.wait_send)
            yield
            come.wait_recv()
            to_sibling(axis, 1 - me, None)
        else:
            for t in range(1, n):
                pending = []
                for step in (1, -1):
                    pair = sems.take()
                    out_c, in_c, to = me - step * (t - 1), me - step * t, me + step
                    can = (out_c >= 0) & (out_c < n) & (to >= 0) & (to < n)
                    gets = (in_c >= 0) & (in_c < n)
                    go = copy(group(axis, out_c), axis, to, pair)
                    come = copy(group(axis, in_c), axis, to, pair)
                    pl.when(can)(go.start)
                    after.append(lambda go=go, can=can: pl.when(can)(go.wait_send))
                    pending.append((come, gets, in_c))
                yield
                for come, gets, in_c in pending:
                    pl.when(gets)(come.wait_recv)
                    to_sibling(axis, in_c, gets)
        held.append(axis)
    yield
    for f in after:
        f()


def interleave(rounds):
    live = list(rounds)
    while live:
        still = []
        for r in live:
            try:
                next(r)
                still.append(r)
            except StopIteration:
                pass
        live = still


def flat_to_rows(src, dst, rows, cols):
    w = cols // 128
    for j in range(w):
        dst[:, j * 128:(j + 1) * 128] = src[pl.ds(j, rows, stride=w), :].astype(dst.dtype)


def rows_to_flat(value, dst, rows, cols):
    w = cols // 128
    for j in range(w):
        dst[pl.ds(j, rows, stride=w), :] = value[:, j * 128:(j + 1) * 128]


def both(a, b):
    return b if a is None else a if b is None else a & b


def when(cond, f):
    if cond is None:
        f()
    else:
        pl.when(cond)(f)


def remote(src, dst, pair, device):
    return pltpu.make_async_remote_copy(
        src_ref=src, dst_ref=dst, send_sem=pair[0], recv_sem=pair[1], device_id=device, device_id_type=MESH)


ORDERS = ((0, 2, 1), (0, 1, 2), (1, 2, 0), (0, 1, 2), (0, 1, 2))


def gather_kernel(sizes, shapes, *refs):
    n = len(shapes)
    masters, outs = refs[:n], refs[n:2 * n]
    stage, local, send, recv = refs[2 * n:3 * n], refs[3 * n], refs[3 * n + 1], refs[3 * n + 2]
    place = Place(sizes)
    copies = []
    for k, (rows, cols) in enumerate(shapes):
        if rows == 1:
            stage[k][...] = masters[k][...].astype(BF).astype(stage[k].dtype)
        else:
            flat_to_rows(masters[k], stage[k], rows, cols)
        cp = pltpu.make_async_copy(stage[k], outs[k].at[place.at], local.at[k])
        cp.start()
        copies.append(cp)
    place.greet()
    for cp in copies:
        cp.wait()
    sems = Sems(send, recv)
    interleave([gather_rounds(place, outs[k], ORDERS[k], sems) for k in range(n)])


def gather_all(mesh_sizes, masters, shapes, dtypes):
    n = len(shapes)
    total = sum(gather_sems(ORDERS[k], mesh_sizes) for k in range(n))
    vm = pl.BlockSpec(memory_space=pltpu.VMEM)
    return pl.pallas_call(
        functools.partial(gather_kernel, mesh_sizes, shapes),
        out_shape=[jax.ShapeDtypeStruct((*mesh_sizes, *s), d) for s, d in zip(shapes, dtypes)],
        in_specs=[vm] * n,
        out_specs=[pl.BlockSpec(memory_space=pl.ANY)] * n,
        scratch_shapes=[pltpu.VMEM(s, d) for s, d in zip(shapes, dtypes)]
        + [pltpu.SemaphoreType.DMA((n,)), pltpu.SemaphoreType.DMA((total,)), pltpu.SemaphoreType.DMA((total,))],
        compiler_params=pltpu.CompilerParams(collective_id=0, has_side_effects=True, vmem_limit_bytes=48 << 20),
        name="gather_weights",
    )(*masters)


def reduce_sems(order, sizes):
    return 1 + sum(1 if sizes[x] == 2 else 2 * (sizes[x] - 1) for x in order)


def reduce_rounds(place, grad, order, got, bufs, total, sems):
    sizes = place.sizes
    after = []
    e = place.at[3]

    def rdma(src, dst, axis, coord, pair):
        return pltpu.make_async_remote_copy(
            src_ref=src, dst_ref=dst, send_sem=pair[0], recv_sem=pair[1],
            device_id=place.device(axis, coord), device_id_type=MESH)

    def add_into(dst, src):
        dst[...] = (dst[...].astype(F32) + src[...].astype(F32)).astype(dst.dtype)

    def each(dims, f):
        count = 1
        for d in dims:
            count *= d
        if count == 1:
            f(tuple(0 for _ in dims))
            return

        def step(i, _):
            idx = []
            for d in reversed(dims):
                idx.append(i % d)
                i = i // d
            f(tuple(reversed(idx)))
            return 0

        lax.fori_loop(0, count, step, 0)

    cp = rdma(grad.at[:, :, :, 1 - e], got, 3, 1 - e, sems.take())
    cp.start()
    yield
    cp.wait()
    each(sizes[:3], lambda i: add_into(got.at[i], grad.at[(*i, e)]))
    cur, left = got, [0, 1, 2]
    for axis, buf in zip(order, bufs):
        n, me = sizes[axis], place.at[axis]
        pos = left.index(axis)
        rest = [x for x in left if x != axis]
        dims = [sizes[x] for x in rest]

        def part(ref, coord):
            return ref.at[tuple(coord if i == pos else slice(None) for i in range(len(left)))]

        def one(ref, coord, i):
            i = list(i)
            i.insert(pos, coord)
            return ref.at[tuple(i)]

        last = not rest
        if n == 2:
            cp = rdma(part(cur, 1 - me), buf, axis, 1 - me, sems.take())
            cp.start()
            yield
            cp.wait()
            if last:
                total[...] = buf[...].astype(F32) + cur[me].astype(F32)
            else:
                each(dims, lambda i: add_into(buf.at[i], one(cur, me, i)))
        else:
            for t in range(n - 1):
                for way, step in enumerate((1, -1)):
                    j = n - 1 - t if step == 1 else t
                    to, back = me + step, me - step
                    ahead = (j > me) if step == 1 else (j < me)
                    gets = ahead & (back >= 0) & (back < n)
                    pair = sems.take()
                    come = rdma(part(cur, j), buf.at[way, j], axis, to, pair)

                    @pl.when(gets)
                    def _():
                        come.wait_recv()
                        each(dims, lambda i: add_into(one(cur, j, i), buf.at[(way, j, *i)]))

                    pl.when(ahead)(come.start)
                    after.append(lambda come=come, ahead=ahead: pl.when(ahead)(come.wait_send))
                    ends = (j == me) & (back >= 0) & (back < n)
                    after.append(lambda come=come, ends=ends: pl.when(ends)(come.wait_recv))
                yield
            for f in after:
                f()
            after = []
            keep = buf.at[0, me]

            def close(i):
                mine = one(cur, me, i)[...].astype(F32)
                v = mine + jnp.where(me > 0, buf[(0, me, *i)].astype(F32), 0.0)
                v = v + jnp.where(me < n - 1, buf[(1, me, *i)].astype(F32), 0.0)
                if last:
                    total[...] = v
                else:
                    buf[(0, me, *i)] = v.astype(buf.dtype)

            each(dims, close)
            buf = keep
        cur, left = buf, rest
    for f in after:
        f()


def reduce_bufs(order, sizes, shape):
    left, out = [0, 1, 2], [(*sizes[:3], *shape)]
    for axis in order:
        rest = [x for x in left if x != axis]
        dims = tuple(sizes[x] for x in rest)
        out.append((*dims, *shape) if sizes[axis] == 2 else (2, sizes[axis], *dims, *shape))
        left = rest
    return out


BACK = tuple(tuple(reversed(o)) for o in ORDERS)


def adam(mean_old, square_old, grad):
    mean_new = beta_one * mean_old + (1.0 - beta_one) * grad
    square_new = beta_two * square_old + (1.0 - beta_two) * grad * grad
    steps = float(STEP)
    mean_hat = mean_new / (1.0 - beta_one**steps)
    square_hat = square_new / (1.0 - beta_two**steps)
    return -learn_rate * mean_hat / (jnp.sqrt(square_hat) + 1e-08), mean_new


def reduce_kernel(sizes, shapes, counts, *refs):
    n = len(shapes)
    refs = list(refs)

    def take(k):
        out = refs[:k]
        del refs[:k]
        return out

    grads, totals = take(n), take(n)
    bufs = [take(c) for c in counts]
    send, recv = take(2)
    place = Place(sizes)
    place.greet()
    sems = Sems(send, recv)
    interleave([reduce_rounds(place, grads[k], BACK[k], bufs[k][0], bufs[k][1:], totals[k], sems) for k in range(n)])


def reduce_all(mesh_sizes, grads, shapes):
    n = len(shapes)
    lists = [reduce_bufs(BACK[k], mesh_sizes, shapes[k]) for k in range(n)]
    total = sum(reduce_sems(BACK[k], mesh_sizes) for k in range(n))
    vm = pl.BlockSpec(memory_space=pltpu.VMEM)
    scratch = []
    for k in range(n):
        scratch += [pltpu.VMEM(s, grads[k].dtype) for s in lists[k]]
    scratch += [pltpu.SemaphoreType.DMA((total,)), pltpu.SemaphoreType.DMA((total,))]
    return pl.pallas_call(
        functools.partial(reduce_kernel, mesh_sizes, shapes, [len(x) for x in lists]),
        out_shape=[jax.ShapeDtypeStruct(s, F32) for s in shapes],
        in_specs=[vm] * n,
        out_specs=[vm] * n,
        scratch_shapes=scratch,
        compiler_params=pltpu.CompilerParams(collective_id=1, has_side_effects=True, vmem_limit_bytes=60 << 20),
        name="reduce_gradients",
    )(*grads)


def adam_kernel(shapes, count, *refs):
    n = len(shapes)
    refs = list(refs)
    rows_in, grads, means, squares = refs[:count], refs[count:count + n], refs[count + n:count + 2 * n], refs[count + 2 * n:count + 3 * n]
    refs = refs[count + 3 * n:]
    rows_out, outs, held, sem = refs[:count], refs[count:-count - 1], refs[-count - 1:-1], refs[-1]
    copies = [pltpu.make_async_copy(a, b, sem.at[i]) for i, (a, b) in enumerate(zip(rows_in, held))]
    copies += [pltpu.make_async_copy(a, b, sem.at[count + i]) for i, (a, b) in enumerate(zip(held, rows_out))]
    for cp in copies[:count]:
        cp.start()
    for k, (rows, cols) in enumerate(shapes):
        change, mean, summed = outs[3 * k:3 * k + 3]
        if rows == 1:
            summed[...] = grads[k][:, 0:cols]
        else:
            rows_to_flat(grads[k], summed, rows, cols)
        change[...], mean[...] = adam(means[k][...], squares[k][...], summed[...])
        if k < count:
            copies[k].wait()
            copies[count + k].start()
    for cp in copies[count:]:
        cp.wait()


def adam_all(rows, grads, means, squares, shapes):
    vm, hb = pl.BlockSpec(memory_space=pltpu.VMEM), pl.BlockSpec(memory_space=pltpu.HBM)
    flat = [((r * c) // 128, 128) if r > 1 else (1, c) for r, c in shapes]
    count = len(rows)
    return pl.pallas_call(
        functools.partial(adam_kernel, shapes, count),
        out_shape=[jax.ShapeDtypeStruct(r.shape, F32) for r in rows] + [jax.ShapeDtypeStruct(f, F32) for f in flat for _ in range(3)],
        in_specs=[hb] * count + [vm] * (3 * len(shapes)),
        out_specs=[hb] * count + [vm] * (3 * len(shapes)),
        scratch_shapes=[pltpu.VMEM(r.shape, F32) for r in rows] + [pltpu.SemaphoreType.DMA((2 * count,))],
        name="adam",
    )(*rows, *grads, *means, *squares)

D = 512
HEADS = 8
HD = 64
FF = 2048
ROW = 1024
SEGS = 24
MOST = 512
QT = 256
KT = 128
PAIR = 128
NEG = -1000000000.0


def dot(a, b):
    return jnp.dot(a, b, preferred_element_type=F32)


def dot_t(a, b):
    return lax.dot_general(a, b, (((1,), (1,)), ((), ())), preferred_element_type=F32)


def t_dot(a, b):
    return lax.dot_general(a, b, (((0,), (0,)), ((), ())), preferred_element_type=F32)


def for_rows(block, f, rows=ROW):
    def step(i, _):
        f(pl.ds(pl.multiple_of(i * block, block), block))
        return 0

    lax.fori_loop(0, rows // block, step, 0)


def ends_of(lengths):
    out, total = [], jnp.int32(0)
    for i in range(SEGS):
        total = total + lengths[0, i]
        out.append(total)
    return out


def seg_at(ends, place):
    count = jnp.int32(0)
    for e in ends:
        count = count + (e <= place).astype(jnp.int32)
    return count


def pick(values, index):
    out = values[-1]
    for i in range(len(values) - 2, -1, -1):
        out = jnp.where(index <= i, values[i], out)
    return out


def seg_row(ends):
    place = lax.broadcasted_iota(jnp.int32, (1, ROW), 1)
    out = jnp.zeros((1, ROW), jnp.int32)
    for e in ends:
        out = out + (place >= e).astype(jnp.int32)
    return out.astype(F32)


def store_seg(ends, row_ref, col_ref):
    row_ref[...] = jnp.broadcast_to(seg_row(ends), (8, ROW))
    for i in range(ROW // 128):
        block = jnp.broadcast_to(row_ref[0:1, i * 128:(i + 1) * 128], (128, 128))
        col_ref[i * 128:(i + 1) * 128, :] = jnp.transpose(block)


def ranges(query_ends, key_ends, causal, tile, other, by_query):
    out = []
    here, there = (query_ends, key_ends) if by_query else (key_ends, query_ends)
    starts = [jnp.int32(0)] + there[:-1]
    for i in range(ROW // tile):
        first, last = i * tile, (i + 1) * tile - 1
        low = pick(starts, seg_at(here, first)) // other
        high = (pick(there, seg_at(here, last)) + other - 1) // other
        if causal and by_query:
            high = jnp.int32((i + 1) * tile // other)
        if causal and not by_query:
            low = jnp.int32(i * tile // other)
        out.append((low, high))
    return out


def store_ranges(ref, base, pairs):
    for i, (low, high) in enumerate(pairs):
        ref[base + 2 * i] = low
        ref[base + 2 * i + 1] = high


def head_masks():
    lane = lax.broadcasted_iota(jnp.int32, (1, PAIR), 1)
    left = (lane < HD).astype(F32).astype(BF)
    return left, (1.0 - left.astype(F32)).astype(BF)


def stack_heads(block, masks):
    return jnp.concatenate([block * masks[0], block * masks[1]], 0)


def block_diag(pair_t):
    zero = jnp.zeros((HD, pair_t.shape[1]), pair_t.dtype)
    top = jnp.concatenate([pair_t[:HD], zero], 1)
    low = jnp.concatenate([zero, pair_t[HD:]], 1)
    return jnp.concatenate([top, low], 0)


def bias_tile(key_col, query_row, k0, q0, causal):
    keys = key_col[pl.ds(k0, KT), :]
    keys = jnp.concatenate([keys] * (QT // 128), 1)
    ok = keys == query_row[0:1, pl.ds(q0, QT)]
    if causal:
        kpos = k0 + lax.broadcasted_iota(jnp.int32, (KT, QT), 0)
        qpos = q0 + lax.broadcasted_iota(jnp.int32, (KT, QT), 1)
        ok = ok & (kpos <= qpos)
    return jnp.where(ok, 0.0, NEG)


def norm_back(dh, xhat, rstd, gain):
    dx = dh * gain
    mean_dx = jnp.mean(dx, -1, keepdims=True)
    mean_xx = jnp.mean(dx * xhat, -1, keepdims=True)
    return rstd[:, 0:1] * (dx - mean_dx - xhat * mean_xx)


def fold(x):
    return jnp.sum(x.reshape(-1, 8, x.shape[-1]), 0)


def pipeline(count, *stages):
    values = {}
    last = len(stages) - 1
    for tick in range(count + last):
        for i in reversed(range(count)):
            st = tick - i
            if 0 <= st <= last:
                values[i] = stages[st](i) if st == 0 else stages[st](i, values[i])
    return [values[i] for i in range(count)]


def columns(hp):
    return slice(hp * PAIR, (hp + 1) * PAIR)


def score_tile(k0, q0, q, k, key_col, query_row, causal, scores, peak, masks):
    bias = bias_tile(key_col, query_row, k0, q0, causal)

    def meet(hp):
        return dot_t(stack_heads(k[pl.ds(k0, KT), columns(hp)], masks), q[pl.ds(q0, QT), columns(hp)])

    def keep(hp, s):
        for side in range(2):
            h = 2 * hp + side
            sh = s[side * KT:(side + 1) * KT] + bias
            scores[hp][pl.ds(k0, KT), side * QT:(side + 1) * QT] = sh
            peak[h] = jnp.maximum(peak[h], jnp.max(sh.reshape(KT // 8, 8, QT), 0))

    pipeline(HEADS // 2, meet, keep)


def weigh_tile(k0, vt, scores, acc, peak, tally):
    def weigh(hp):
        probs = []
        for side in range(2):
            h = 2 * hp + side
            sh = scores[hp][pl.ds(k0, KT), side * QT:(side + 1) * QT]
            p = jnp.exp(sh.reshape(KT // 8, 8, QT) - peak[h][None])
            tally[h] += jnp.sum(p, 0)
            probs.append(p.reshape(KT, QT).astype(BF))
        return jnp.concatenate(probs, 0)

    def spread(hp, probs):
        return dot(block_diag(vt[columns(hp), pl.ds(k0, KT)]), probs)

    def add(hp, o):
        acc[columns(hp), :] += o

    pipeline(HEADS // 2, weigh, spread, add)


def attend(tile, span, q, k, vt, key_col, query_row, causal, out, lse, scores, acc, peak, tally, pump=None):
    masks = head_masks()
    q0 = pl.multiple_of(tile * QT, QT) if not isinstance(tile, int) else tile * QT
    first, end = span
    peak[...] = jnp.full_like(peak, -3e38)

    def score(j, _):
        score_tile(pl.multiple_of(j * KT, KT), q0, q, k, key_col, query_row, causal, scores, peak, masks)
        return 0

    lax.fori_loop(first, end, score, 0)
    if pump:
        pump()
    for h in range(HEADS):
        peak[h] = jnp.broadcast_to(jnp.max(peak[h], 0, keepdims=True), (8, QT))
    acc[...] = jnp.zeros_like(acc)
    tally[...] = jnp.zeros_like(tally)

    def weigh(j, _):
        weigh_tile(pl.multiple_of(j * KT, KT), vt, scores, acc, peak, tally)
        return 0

    lax.fori_loop(first, end, weigh, 0)
    if pump:
        pump()
    for hp in range(HEADS // 2):
        rows = []
        for side in range(2):
            h = 2 * hp + side
            total = jnp.sum(tally[h], 0, keepdims=True)
            lse[h:h + 1, pl.ds(q0, QT)] = peak[h, 0:1, :] + jnp.log(total)
            rows.append(acc[hp * PAIR + side * HD:hp * PAIR + (side + 1) * HD, :] * (1.0 / total))
        out[pl.ds(q0, QT), hp * PAIR:(hp + 1) * PAIR] = jnp.transpose(jnp.concatenate(rows, 0)).astype(BF)


def attend_back(tile, span, k, v, kt, qt, gt, lse, inner, key_col, query_row, causal, dqt, dk, dv, dk_acc, dv_acc):
    masks = head_masks()
    k0 = pl.multiple_of(tile * KT, KT) if not isinstance(tile, int) else tile * KT
    dk_acc[...] = jnp.zeros_like(dk_acc)
    dv_acc[...] = jnp.zeros_like(dv_acc)

    def step(i, _):
        q0 = pl.multiple_of(i * QT, QT)
        bias = bias_tile(key_col, query_row, k0, q0, causal)
        at = pl.ds(q0, QT)

        def meet(hp):
            cols = columns(hp)
            s = dot(stack_heads(k[pl.ds(k0, KT), cols], masks), qt[cols, at])
            return s, dot(stack_heads(v[pl.ds(k0, KT), cols], masks), gt[cols, at])

        def weigh(hp, both):
            s, dp = both
            probs, slopes = [], []
            for side in range(2):
                h = 2 * hp + side
                rows = slice(side * KT, (side + 1) * KT)
                p = jnp.exp(s[rows] + bias - lse[h:h + 1, at])
                slopes.append((p * (dp[rows] - inner[h:h + 1, at])).astype(BF))
                probs.append(p.astype(BF))
            return jnp.concatenate(probs, 0), jnp.concatenate(slopes, 0)

        def spread(hp, both):
            cols = columns(hp)
            probs, slopes = both
            to_q = dot(block_diag(kt[cols, pl.ds(k0, KT)]), slopes)
            return dot_t(gt[cols, at], probs), dot_t(qt[cols, at], slopes), to_q

        def add(hp, terms):
            to_v, to_k, to_q = terms
            for acc, to in ((dv_acc, to_v), (dk_acc, to_k)):
                acc[hp * PAIR:hp * PAIR + HD, :] += to[:HD, :KT]
                acc[hp * PAIR + HD:(hp + 1) * PAIR, :] += to[HD:, KT:]
            dqt[columns(hp), at] += to_q

        pipeline(HEADS // 2, meet, weigh, spread, add)
        return 0

    lax.fori_loop(span[0], span[1], step, 0)
    dk[pl.ds(k0, KT), :] = jnp.transpose(dk_acc[...]).astype(BF)
    dv[pl.ds(k0, KT), :] = jnp.transpose(dv_acc[...]).astype(BF)


def flip(src, dst):
    for i in range(ROW // 128):
        dst[:, i * 128:(i + 1) * 128] = jnp.transpose(src[i * 128:(i + 1) * 128, :])


def standard(r):
    centered = r - jnp.mean(r, -1, keepdims=True)
    spread = jnp.mean(centered * centered, -1, keepdims=True)
    scale = lax.rsqrt(spread + 1e-05)
    return centered * scale, scale


def into_attention(g, c, inner, at, heads):
    both = g.astype(F32) * c.astype(F32)
    high = both.astype(BF)
    low = (both - high.astype(F32)).astype(BF)
    inner[:, at] = dot_t(heads, high) + dot_t(heads, low)


def head_rows():
    at = lax.broadcasted_iota(jnp.int32, (HEADS, D), 1) // HD == lax.broadcasted_iota(jnp.int32, (HEADS, D), 0)
    return at.astype(F32).astype(BF)


class Mover:
    def __init__(self, sems):
        self.sems, self.used, self.out = sems, 0, []

    def start(self, src, dst):
        cp = pltpu.make_async_copy(src, dst, self.sems.at[self.used])
        self.used += 1
        cp.start()
        return cp

    def store(self, src, dst):
        self.out.append(self.start(src, dst))

    def finish(self):
        for cp in self.out:
            cp.wait()


def own_spans():
    return [(max(0, (i * QT - MOST + 1) // KT), (i + 1) * QT // KT) for i in range(ROW // QT)]


def own_spans_back():
    return [(j * KT // QT, min(ROW // QT, ((j + 1) * KT - 1 + MOST - 1) // QT + 1)) for j in range(ROW // KT)]


def front_compute(x, mem, win, wout, norms, q1, k1, v1, c1, lse1, xh1, rs1, q2, k2, v2, trow, tcol, vt, scores, acc, peak, tally, ready, pump):
    ready("first")
    for i in range(ROW // 256):
        at = slice(i * 256, (i + 1) * 256)
        for out, w in ((q1, 0), (k1, 1), (v1, 2)):
            y = dot(x[at, :], win[w * D:(w + 1) * D, :]).astype(BF)
            out[at, :] = y * BF(0.125) if w == 0 else y
        pump()
    ready("projected")
    flip(v1, vt)
    for i, span in enumerate(own_spans()):
        attend(i, span, q1, k1, vt, tcol, trow, True, c1, lse1, scores, acc, peak, tally, pump)
    ready("second")
    for i in range(ROW // 256):
        at = slice(i * 256, (i + 1) * 256)
        for out, w in ((k2, 4), (v2, 5)):
            out[at, :] = dot(mem[at, :], win[w * D:(w + 1) * D, :]).astype(BF)
        pump()
    ready("keys")
    for i in range(ROW // 256):
        at = slice(i * 256, (i + 1) * 256)
        xhat, scale = standard(x[at, :].astype(F32) + dot(c1[at, :], wout[0:D, :]))
        xh1[at, :] = xhat
        rs1[at, :] = jnp.broadcast_to(scale, (256, 128))
        h = xhat * norms[0:1, :] + norms[3:4, :]
        q2[at, :] = dot(h.astype(BF), win[3 * D:4 * D, :]).astype(BF) * BF(0.125)
        pump()


FRONT_OUTS = (
    ((ROW, D), BF), ((ROW, D), BF), ((ROW, D), BF), ((ROW, D), BF), ((HEADS, ROW), F32),
    ((ROW, D), F32), ((ROW, 128), F32), ((ROW, D), BF), ((ROW, D), BF), ((ROW, D), BF),
)
KEPT = len(FRONT_OUTS)


def front_scratch():
    return (
        [pltpu.VMEM(s, d) for s, d in FRONT_OUTS]
        + [pltpu.VMEM((8, ROW), F32), pltpu.VMEM((ROW, 128), F32), pltpu.VMEM((D, ROW), BF)]
        + [pltpu.VMEM((ROW, D), F32)] * 4
        + [pltpu.VMEM((D, QT), F32), pltpu.VMEM((HEADS, 8, QT), F32), pltpu.VMEM((HEADS, 8, QT), F32)]
        + [pltpu.VMEM((ROW, D), BF)] * 2
        + [pltpu.VMEM((6 * D, D), BF), pltpu.VMEM((2 * D, D), BF), pltpu.SemaphoreType.DMA((40,))]
    )


def take(refs, k):
    out = refs[:k]
    del refs[:k]
    return out


SEG_OUTS = (((8, ROW), F32), ((ROW, 128), F32), ((ROW, 128), F32))


def segments_of(tlen, slen, trow, tcol, scol, table):
    tends, sends = ends_of(tlen), ends_of(slen)
    store_seg(sends, trow, scol)
    store_seg(tends, trow, tcol)
    store_ranges(table, 0, ranges(tends, sends, False, QT, KT, True))
    store_ranges(table, 8, ranges(tends, sends, False, KT, QT, False))


def front_kernel(tlen, slen, x, mem, win, wout, norms, *refs):
    refs = list(refs)
    outs, segs, table, kept = take(refs, 10), take(refs, 3), refs.pop(0), take(refs, 10)
    trow, tcol, vt = take(refs, 3)
    scores, (acc, peak, tally), (xs, ms, ws, os, sems, scol) = take(refs, 4), take(refs, 3), refs
    mover = Mover(sems)
    coming = [mover.start(x, xs), mover.start(win, ws), mover.start(wout, os), mover.start(mem, ms)]
    segments_of(tlen, slen, trow, tcol, scol, table)
    for k, ref in enumerate((trow, tcol, scol)):
        mover.store(ref, segs[k])

    def ready(stage):
        if stage == "first":
            coming[0].wait()
            coming[1].wait()
        if stage == "second":
            coming[2].wait()
            coming[3].wait()

    front_compute(xs, ms, ws, os, norms, *kept, trow, tcol, vt, scores, acc, peak, tally, ready, lambda: None)
    for k in range(10):
        mover.store(kept[k], outs[k])
    mover.finish()


def middle_kernel(
    tlen, table, mem, cot, q2, k2, v2, xh1, win, wout, up, down, norms, rows_in, cols_in,
    result, dk_out, dv_out, dh1, gin, gout, gup, gdown, gnorm,
    mem_s, cot_s, q_s, k_s, v_s, xh_s, win_s, wout_s, up_s, down_s,
    result_s, dk, dv, dh1_s, gin_s, gout_s, gup_s, gdown_s,
    trow, scol, flipped, qt, gt, c2, lse, inner, acc, peak, tally, spare, other, dr,
    h1b, h2b, act, du, dy, pre, turn, dc, dq, dqt, dk_acc, dv_acc, sems,
):
    mover = Mover(sems)
    pairs = (
        (k2, k_s), (q2, q_s), (v2, v_s), (wout.at[pl.ds(D, D)], wout_s), (xh1, xh_s), (up, up_s), (down, down_s),
        (cot, cot_s), (win.at[pl.ds(3 * D, D)], win_s), (mem, mem_s),
    )
    segs = [mover.start(rows_in, trow), mover.start(cols_in, scol)]
    coming = [mover.start(a, b) for a, b in pairs]
    gnorm[...] = jnp.zeros_like(gnorm)
    heads = head_rows()
    for cp in segs + coming[:3]:
        cp.wait()
    flip(v_s, flipped)

    def forward(i, _):
        span = (table[2 * i], table[2 * i + 1])
        attend(i, span, q_s, k_s, flipped, scol, trow, False, c2, lse, (other, dh1_s, dr, spare), acc, peak, tally)
        return 0

    lax.fori_loop(0, ROW // QT, forward, 0)
    for k in range(3, 8):
        coming[k].wait()
    live_end = ends_of(tlen)[SEGS - 2]
    block = 256

    def rows(i, _):
        at = pl.ds(pl.multiple_of(i * block, block), block)
        h = xh_s[at, :] * norms[0:1, :] + norms[3:4, :]
        h1b[at, :] = h.astype(BF)
        xh2, rs2 = standard(h + dot(c2[at, :], wout_s[...]))
        h = xh2 * norms[1:2, :] + norms[4:5, :]
        hb = h.astype(BF)
        h2b[at, :] = hb

        def cols_of(j):
            return slice(j * D, (j + 1) * D)

        def widen(j):
            u = dot(hb, up_s[:, cols_of(j)])
            pre[:, cols_of(j)] = u
            return u

        def gate(j, u):
            a = (u / (1.0 + jnp.exp(-u))).astype(BF)
            act[at, cols_of(j)] = a
            return a

        def narrow(j, a):
            return dot(a, down_s[cols_of(j), :])

        parts = pipeline(FF // D, widen, gate, narrow)
        r3 = h + ((parts[0] + parts[1]) + (parts[2] + parts[3]))
        xhat, rstd = standard(r3)
        result_s[at, :] = (xhat * norms[2:3, :] + norms[5:6, :]).astype(BF)
        place = i * block + lax.broadcasted_iota(jnp.int32, (block, D), 0)
        seed = jnp.where(place < live_end, cot_s[at, :].astype(F32), 0.0)
        gnorm[0:8, :] += fold(seed * xhat)
        gnorm[8:16, :] += fold(seed)
        dr3 = norm_back(seed, xhat, rstd, norms[2:3, :])
        dyb = dr3.astype(BF)
        dy[at, :] = dyb

        def widen_back(j):
            return dot_t(dyb, down_s[cols_of(j), :])

        def gate_back(j, grad):
            u = pre[:, cols_of(j)]
            sig = 1.0 / (1.0 + jnp.exp(-u))
            d = (grad * (sig * (1.0 + u * (1.0 - sig)))).astype(BF)
            du[at, cols_of(j)] = d
            return d

        def narrow_back(j, d):
            return dot_t(d, up_s[:, cols_of(j)])

        parts = pipeline(FF // D, widen_back, gate_back, narrow_back)
        dh = dr3 + ((parts[0] + parts[1]) + (parts[2] + parts[3]))
        gnorm[16:24, :] += fold(dh * xh2)
        gnorm[24:32, :] += fold(dh)
        r = norm_back(dh, xh2, rs2, norms[1:2, :])
        dr[at, :] = r
        rb = r.astype(BF)
        dy2 = dot_t(rb, wout_s[...]).astype(BF)
        turn[at, :] = rb
        dc[at, :] = dy2
        into_attention(dy2, c2[at, :], inner, at, heads)
        return 0

    lax.fori_loop(0, ROW // block, rows, 0)
    mover.store(result_s, result)
    for j in range(FF // D):
        cols = slice(j * D, (j + 1) * D)
        gdown_s[cols, :] = t_dot(act[:, cols], dy[...]).astype(BF)
    mover.store(gdown_s, gdown)
    for j in range(FF // D):
        cols = slice(j * D, (j + 1) * D)
        gup_s[:, cols] = t_dot(h2b[...], du[:, cols]).astype(BF)
    mover.store(gup_s, gup)
    gout_s[...] = t_dot(c2[...], turn[...]).astype(BF)
    mover.store(gout_s, gout)
    flip(k_s, flipped)
    flip(q_s, qt)
    flip(dc, gt)
    dqt[...] = jnp.zeros_like(dqt)

    def backward(j, _):
        span = (table[8 + 2 * j], table[9 + 2 * j])
        attend_back(j, span, k_s, v_s, flipped, qt, gt, lse, inner, scol, trow, False, dqt, dk, dv, dk_acc, dv_acc)
        return 0

    lax.fori_loop(0, ROW // KT, backward, 0)
    mover.store(dk, dk_out)
    mover.store(dv, dv_out)
    coming[8].wait()
    coming[9].wait()
    gin_s[D:2 * D, :] = t_dot(mem_s[...], dk[...]).astype(BF)
    gin_s[2 * D:3 * D, :] = t_dot(mem_s[...], dv[...]).astype(BF)

    def end(at):
        q = jnp.transpose(dqt[:, at] * 0.125).astype(BF)
        dq[at, :] = q
        dh1_s[at, :] = dr[at, :] + dot_t(q, win_s[...])

    for_rows(256, end)
    mover.store(dh1_s, dh1)
    gin_s[0:D, :] = t_dot(h1b[...], dq[...]).astype(BF)
    mover.store(gin_s, gin)
    mover.finish()


def back_compute(
    x, q1, k1, v1, c1, lse, xh1, rs1, dh1, win, wout, dk2, dv2, win2, norms, tgrad, mgrad, gin, gout, gnorm,
    trow, tcol, kt, qt, gt, inner, dr, dc, dq, dk, dv, dqt, dk_acc, dv_acc, ready, pump,
):
    heads = head_rows()
    ready("first")
    for i in range(ROW // 256):
        at = slice(i * 256, (i + 1) * 256)
        dh, xhat = dh1[at, :], xh1[at, :]
        gain, bias = fold(dh * xhat), fold(dh)
        gnorm[0:8, :] = gain if i == 0 else gnorm[0:8, :] + gain
        gnorm[8:16, :] = bias if i == 0 else gnorm[8:16, :] + bias
        r = norm_back(dh, xhat, rs1[at, :], norms[0:1, :])
        dr[at, :] = r
        rb = r.astype(BF)
        g = dot_t(rb, wout[...]).astype(BF)
        dq[at, :] = rb
        dc[at, :] = g
        into_attention(g, c1[at, :], inner, at, heads)
        pump()
    gout[...] = t_dot(c1[...], dq[...]).astype(BF)
    ready("outward")
    flip(k1, kt)
    flip(q1, qt)
    flip(dc, gt)
    pump()
    dqt[...] = jnp.zeros_like(dqt)
    for j, span in enumerate(own_spans_back()):
        attend_back(j, span, k1, v1, kt, qt, gt, lse, inner, tcol, trow, True, dqt, dk, dv, dk_acc, dv_acc)
        pump()
    gin[D:2 * D, :] = t_dot(x[...], dk[...]).astype(BF)
    gin[2 * D:3 * D, :] = t_dot(x[...], dv[...]).astype(BF)
    for i in range(ROW // 256):
        at = slice(i * 256, (i + 1) * 256)
        dq[at, :] = jnp.transpose(dqt[:, at] * 0.125).astype(BF)
    gin[0:D, :] = t_dot(x[...], dq[...]).astype(BF)
    ready("inward")
    for i in range(ROW // 256):
        at = slice(i * 256, (i + 1) * 256)
        t = dr[at, :]
        for k, g in enumerate((dq, dk, dv)):
            t = t + dot_t(g[at, :], win[k * D:(k + 1) * D, :])
        tgrad[at, :] = t
        pump()
    ready("target")
    for i in range(ROW // 256):
        at = slice(i * 256, (i + 1) * 256)
        mgrad[at, :] = dot_t(dk2[at, :], win2[0:D, :]) + dot_t(dv2[at, :], win2[D:2 * D, :])
        pump()
    ready("memory")


BACK_INS = (
    ((ROW, D), BF), ((ROW, D), BF), ((ROW, D), BF), ((ROW, D), BF), ((ROW, D), BF), ((HEADS, ROW), F32),
    ((ROW, D), F32), ((ROW, 128), F32), ((ROW, D), F32), ((3 * D, D), BF), ((D, D), BF),
    ((ROW, D), BF), ((ROW, D), BF), ((2 * D, D), BF),
)
TAKEN = len(BACK_INS)


def back_scratch():
    return (
        [pltpu.VMEM(s, d) for s, d in BACK_INS]
        + [pltpu.VMEM((ROW, D), F32)] * 2
        + [pltpu.VMEM((8, ROW), F32), pltpu.VMEM((ROW, 128), F32)]
        + [pltpu.VMEM((D, ROW), BF)] * 3
        + [pltpu.VMEM((HEADS, ROW), F32), pltpu.VMEM((ROW, D), F32)]
        + [pltpu.VMEM((ROW, D), BF)] * 4
        + [pltpu.VMEM((D, ROW), F32), pltpu.VMEM((D, KT), F32), pltpu.VMEM((D, KT), F32), pltpu.SemaphoreType.DMA((40,))]
    )


def back_loads(mover, ins, kept):
    win, wout = ins[9], ins[10]
    parts = list(ins[:9]) + [win.at[pl.ds(0, 3 * D)], wout.at[pl.ds(0, D)], ins[11], ins[12], win.at[pl.ds(4 * D, 2 * D)]]
    order = (8, 6, 7, 10, 4, 2, 1, 3, 5, 0, 9, 11, 12, 13)
    return [mover.start(parts[k], kept[k]) for k in order]


def back_kernel(norms, *refs):
    refs = list(refs)
    ins, segs, (tgrad, mgrad, gin, gout, gnorm), kept = take(refs, TAKEN - 1), take(refs, 2), take(refs, 5), take(refs, TAKEN)
    (tgrad_s, mgrad_s), work, sems = refs[:2], refs[2:-1], refs[-1]
    mover = Mover(sems)
    coming = [mover.start(segs[0], work[0]), mover.start(segs[1], work[1])] + back_loads(mover, ins, kept)

    def ready(stage):
        if stage == "first":
            for cp in coming:
                cp.wait()

    back_compute(*kept, norms, tgrad_s, mgrad_s, gin, gout, gnorm, *work, ready, lambda: None)
    mover.store(tgrad_s, tgrad)
    mover.store(mgrad_s, mgrad)
    mover.finish()


VM = pl.BlockSpec(memory_space=pltpu.VMEM)
SM = pl.BlockSpec(memory_space=pltpu.SMEM)
HB = pl.BlockSpec(memory_space=pltpu.HBM)


def call(kernel, name, ins, in_specs, outs, out_specs, scratch, params):
    return pl.pallas_call(
        kernel,
        out_shape=[jax.ShapeDtypeStruct(s, d) for s, d in outs],
        in_specs=in_specs,
        out_specs=out_specs,
        scratch_shapes=scratch,
        compiler_params=pltpu.CompilerParams(vmem_limit_bytes=62 << 20, **params),
        name=name,
    )(*ins)


def middle(tlen, table, mem, cot, q2, k2, v2, xh1, win, wout, up, down, norms, trow, scol):
    tok, tokf, flat = ((ROW, D), BF), ((ROW, D), F32), ((D, ROW), BF)
    outs = [tok, tok, tok, tokf, ((3 * D, D), BF), ((D, D), BF), ((D, FF), BF), ((FF, D), BF)]
    ins = [tok] * 5 + [tokf, ((D, D), BF), ((D, D), BF), ((D, FF), BF), ((FF, D), BF)]
    stat, tile = ((HEADS, ROW), F32), ((D, KT), F32)
    work = [((8, ROW), F32), ((ROW, 128), F32), flat, flat, flat, tok, stat, stat, ((D, QT), F32), ((HEADS, 8, QT), F32),
            ((HEADS, 8, QT), F32), tokf, tokf, tokf, tok, tok, ((ROW, FF), BF), ((ROW, FF), BF), tok, ((256, FF), F32), tok, tok, tok,
            ((D, ROW), F32), tile, tile]
    scratch = [pltpu.VMEM(*s) for s in ins + outs + work]
    return call(
        middle_kernel, "middle", [tlen, table, mem, cot, q2, k2, v2, xh1, win, wout, up, down, norms, trow, scol],
        [SM, SM] + [HB] * 10 + [VM, HB, HB], outs + [((32, D), F32)], [HB] * 8 + [VM],
        scratch + [pltpu.SemaphoreType.DMA((20,))], {},
    )


def layer(tlen, slen, x, mem, cot, win, wout, up, down, norms):
    q1, k1, v1, c1, lse1, xh1, rs1, q2, k2, v2, trow, tcol, scol, table = call(
        front_kernel, "front", [tlen, slen, x, mem, win, wout, norms], [SM, SM] + [HB] * 4 + [VM],
        [*FRONT_OUTS, *SEG_OUTS, ((32,), jnp.int32)], [HB] * 13 + [SM], front_scratch() + [pltpu.VMEM((ROW, 128), F32)], {},
    )
    result, dk2, dv2, dh1, gin_two, gout_two, gup, gdown, gnorm_rest = middle(
        tlen, table, mem, cot, q2, k2, v2, xh1, win, wout, up, down, norms, trow, scol)
    tgrad, mgrad, gin_one, gout_one, gnorm_one = call(
        back_kernel, "back", [norms, x, q1, k1, v1, c1, lse1, xh1, rs1, dh1, win, wout, dk2, dv2, trow, tcol],
        [VM] + [HB] * (TAKEN + 1),
        [((ROW, D), F32), ((ROW, D), F32), ((3 * D, D), BF), ((D, D), BF), ((16, D), F32)], [HB, HB, VM, VM, VM], back_scratch(), {},
    )
    gin, gout = jnp.concatenate([gin_one, gin_two]), jnp.concatenate([gout_one, gout_two])
    one = jnp.sum(gnorm_one.reshape(2, 8, D), 1)
    rest = jnp.sum(gnorm_rest.reshape(4, 8, D), 1)
    gnorm = jnp.stack([one[0], rest[2], rest[0], one[1], rest[3], rest[1]])
    return result, tgrad, mgrad, gin, gout, gup, gdown, gnorm


def every(dims):
    return [(a, b, c, e) for a in range(dims[0]) for b in range(dims[1]) for c in range(dims[2]) for e in range(dims[3])]


def lanes_up_to(n):
    return lax.broadcasted_iota(jnp.int32, (8, 128), 1) < n


def norms_from_shards(shards, lined, flat, out):
    for i, at in enumerate(every(shards.shape[:4])):
        lined[i:i + 1, :] = shards[at]
    n = [lined[pl.ds(k, 8, stride=4), :] for k in range(4)]
    flat[pl.ds(0, 8, stride=3), :] = jnp.where(lanes_up_to(96), n[0], pltpu.roll(n[1], 96, 1))
    flat[pl.ds(1, 8, stride=3), :] = jnp.where(lanes_up_to(64), pltpu.roll(n[1], 96, 1), pltpu.roll(n[2], 64, 1))
    flat[pl.ds(2, 8, stride=3), :] = jnp.where(lanes_up_to(32), pltpu.roll(n[2], 64, 1), pltpu.roll(n[3], 32, 1))
    for i in range(24):
        out[i // 4:i // 4 + 1, (i % 4) * 128:(i % 4 + 1) * 128] = flat[i:i + 1, :]


def norms_to_shards(rows, flat, lined, shards):
    for i in range(24):
        flat[i:i + 1, :] = rows[i // 4][:, (i % 4) * 128:(i % 4 + 1) * 128]
    r = [flat[pl.ds(k, 8, stride=3), :] for k in range(3)]
    lined[pl.ds(0, 8, stride=4), :] = r[0]
    lined[pl.ds(1, 8, stride=4), :] = jnp.where(lanes_up_to(32), pltpu.roll(r[0], 32, 1), pltpu.roll(r[1], 32, 1))
    lined[pl.ds(2, 8, stride=4), :] = jnp.where(lanes_up_to(64), pltpu.roll(r[1], 64, 1), pltpu.roll(r[2], 64, 1))
    lined[pl.ds(3, 8, stride=4), :] = pltpu.roll(r[2], 96, 1)
    for i, at in enumerate(every(shards.shape[:4])):
        shards[at] = lined[i:i + 1, :]


DONE = "done"


def until_done(flow):
    for _ in flow:
        yield None
    while True:
        yield DONE


def around(place, d):
    n = place.sizes[0]
    return lax.rem(place.at[0] + (d + n), n)


def spot(first, p, q, at_p, at_q, e):
    return (first, at_p, at_q, *e) if p < q else (first, at_q, at_p, *e)


def gather_bulk(place, ref, own, p, q, sems, span=None, part=None, before=None):
    n, e = place.sizes[0], place.at[3]
    low, high = span or (0, n)
    whole = (low, high) == (0, n)
    group = slice(None) if whole else pl.ds(low, high - low)
    rows = (pl.ds(*part),) if part else ()
    after = []

    def inside(coord):
        return None if whole else (coord >= low) & (coord < high)

    def view(first, flip_p, flip_q, core=None):
        at_p = 1 - place.at[p] if flip_p else place.at[p]
        at_q = slice(None) if flip_q is None else 1 - place.at[q] if flip_q else place.at[q]
        return ref.at[(*spot(first, p, q, at_p, at_q, (e if core is None else core,)), *rows)]

    def send(src, dst, device, cond=None):
        pair = sems.take()
        go = remote(src, dst, pair, device)
        when(cond, go.start)
        after.append((cond, go.wait_send))
        return lambda view: remote(view, view, pair, device)

    def to_sibling(flip_p, flip_q):
        come = send(view(group, flip_p, flip_q), view(group, flip_p, flip_q), place.device(3, 1 - e))
        after.append((None, come(view(group, flip_p, flip_q, 1 - e)).wait_recv))

    own = own.at[rows] if rows else own
    mine = inside(place.at[0])
    come = {}
    for d in range(1, n):
        come[d] = send(own, view(place.at[0], 0, 0), place.device(0, around(place, d)), mine)
    yield
    for d in range(1, n):
        src = around(place, -d)
        when(inside(src), come[d](view(src, 0, 0)).wait_recv)
    if before:
        before()
    here = view(group, 0, 0)
    to_p, to_q = place.device(p, 1 - place.at[p]), place.device(q, 1 - place.at[q])
    from_p, from_q = send(here, here, to_p), send(here, here, to_q)
    to_sibling(0, 0)
    yield
    there = view(group, 1, 0)
    from_p(there).wait_recv()
    from_pq = send(there, there, to_q)
    to_sibling(1, 0)
    yield
    from_q(view(group, 0, 1)).wait_recv()
    to_sibling(0, 1)
    from_pq(view(group, 1, 1)).wait_recv()
    to_sibling(1, 1)
    yield
    for cond, f in after:
        when(cond, f)


def gather_bulk_sems(sizes):
    return sizes[0] - 1 + 3 + 4


def add_rows(dst, *srcs):
    v = srcs[0][...].astype(F32)
    for s in srcs[1:]:
        v = v + s[...].astype(F32)
    dst[...] = v.astype(dst.dtype)


def reduce_bulk(place, grad, half, from_q, from_p, from_z, total, p, q, sems, low=0, part=None):
    n, e = place.sizes[0], place.at[3]
    count = grad.shape[0]
    whole = count == n
    rows = (pl.ds(*part),) if part else ()
    after = []
    me_p, me_q, all_of = place.at[p], place.at[q], slice(None)

    def inside(coord):
        return None if whole else (coord >= low) & (coord < low + count)

    def g(first, at_p, at_q, core):
        return grad.at[(*spot(first, p, q, at_p, at_q, (core,)), *rows)]

    def h(first, at_p, at_q):
        return half.at[(*spot(first, p, q, at_p, at_q, ()), *rows)]

    def send(src, dst, device, cond=None):
        go = remote(src, dst, sems.take(), device)
        when(cond, go.start)
        after.append((cond, go.wait_send))
        return go

    def each(f, times):
        def step(i, _):
            f(i)
            return 0

        lax.fori_loop(0, times, step, 0)

    sibling = place.device(3, 1 - e)
    core_q, core_p, core = [
        send(g(all_of, at_p, at_q, 1 - e), h(all_of, at_p, at_q), sibling)
        for at_p, at_q in ((all_of, 1 - me_q), (1 - me_p, me_q), (me_p, me_q))]
    yield
    core_q.wait_recv()

    def far(i):
        a, at_p = lax.div(i, 2), lax.rem(i, 2)
        add_rows(h(a, at_p, 1 - me_q), g(a, at_p, 1 - me_q, e), h(a, at_p, 1 - me_q))

    each(far, 2 * count)
    come_q = send(h(all_of, all_of, 1 - me_q), from_q, place.device(q, 1 - me_q))
    yield
    core_p.wait_recv()
    come_q.wait_recv()
    each(lambda a: add_rows(h(a, 1 - me_p, me_q), g(a, 1 - me_p, me_q, e), h(a, 1 - me_p, me_q), from_q.at[a, 1 - me_p]), count)
    come_p = send(h(all_of, 1 - me_p, me_q), from_p, place.device(p, 1 - me_p))
    yield
    core.wait_recv()
    come_p.wait_recv()
    each(lambda a: add_rows(h(a, me_p, me_q), g(a, me_p, me_q, e), h(a, me_p, me_q), from_q.at[a, me_p], from_p.at[a]), count)
    come_z = []
    for d in range(1, n):
        to = around(place, d)
        pair = sems.take()
        go = remote(h(to - low, me_p, me_q), from_z.at[d - 1], pair, place.device(0, to))
        when(inside(to), go.start)
        after.append((inside(to), go.wait_send))
        come_z.append(remote(from_z.at[d - 1], from_z.at[d - 1], pair, place.device(0, to)))
    yield

    def close():
        for come in come_z:
            come.wait_recv()
        add_rows(total.at[rows] if rows else total, h(place.at[0] - low, me_p, me_q), *[from_z.at[d] for d in range(n - 1)])

    when(inside(place.at[0]), close)
    for cond, f in after:
        when(cond, f)


def reduce_bulk_sems(sizes):
    return 5 + sizes[0] - 1


def reduce_bulk_bufs(sizes, count, shape):
    return [(count, 2, *shape), (count, *shape), (sizes[0] - 1, *shape)]


def front_remote_kernel(sizes, shapes, tlen, slen, x, mem, *refs):
    refs = list(refs)
    masters = take(refs, 5)
    outs, segs, (win, wout, up, down, norms, table), kept = take(refs, KEPT), take(refs, 3), take(refs, 6), take(refs, KEPT)
    trow, tcol, vt = take(refs, 3)
    scores, (acc, peak, tally), (xs, ms, ws, os, sems) = take(refs, 4), take(refs, 3), take(refs, 5)
    scol, stage_up, stage_down, shards, lined, flat, send, recv = refs
    place, mover = Place(sizes), Mover(sems)
    coming = [mover.start(x, xs), mover.start(mem, ms)]
    mine = [ws.at[place.at], os.at[place.at], stage_up, stage_down]
    for k in range(4):
        flat_to_rows(masters[k], mine[k], *shapes[k])
    shards[place.at] = jnp.zeros((1, 128), F32)
    width = masters[4].shape[1]
    shards[(*place.at, slice(None), slice(0, width))] = masters[4][...].astype(BF).astype(F32)
    local = [mover.start(stage_up, up.at[place.at]), mover.start(stage_down, down.at[place.at])]
    pool, half, rows = Sems(send, recv), sizes[0] // 2, shapes[0][0] // 2
    low, high, top, low_rows = (0, half), (half, sizes[0]), (0, rows), (rows, rows)

    def flow(ref, own, p, q, *rest):
        return until_done(gather_bulk(place, ref, own, p, q, pool, *rest))

    place.greet(True)
    inward, outward = ws.at[place.at], os.at[place.at]
    flows_by = {
        "a": flow(ws, inward, 2, 1, low, top), "b": flow(ws, inward, 1, 2, low, low_rows),
        "c": flow(ws, inward, 2, 1, high, top), "d": flow(ws, inward, 1, 2, high, low_rows),
        "o": flow(os, outward, 1, 2), "n": flow(shards, shards.at[place.at], 1, 2),
        "u": flow(up, stage_up, 2, 1, None, None, local[0].wait), "v": flow(down, stage_down, 1, 2, None, None, local[1].wait),
    }

    def go_on(names):
        for name in names:
            if name in flows_by and next(flows_by[name]) is DONE:
                del flows_by[name]

    def finish(names):
        while set(names) & set(flows_by):
            go_on(names)

    go_on(BEGIN)
    segments_of(tlen, slen, trow, tcol, scol, table)
    for k, ref in enumerate((trow, tcol, scol)):
        mover.store(ref, segs[k])
    go_on(FIRST)
    finish("ab")
    count = [0]

    def pump():
        count[0] += 1
        go_on(FRONT_PLAN.get(count[0], ""))

    def ready(stage):
        if stage == "first":
            coming[0].wait()
        if stage == "projected":
            for k in range(3):
                mover.store(kept[k], outs[k])
        if stage == "second":
            finish("cdon")
            mover.store(ws, win)
            mover.store(os, wout)
            norms_from_shards(shards, lined, flat, norms)
            coming[1].wait()
        if stage == "keys":
            for k in (3, 4, 8, 9):
                mover.store(kept[k], outs[k])

    front_compute(
        xs, ms, ws.reshape(6 * D, D), os.reshape(2 * D, D), norms, *kept, trow, tcol, vt, scores, acc, peak, tally, ready, pump)
    for k in (5, 6, 7):
        mover.store(kept[k], outs[k])
    finish("uv")
    mover.finish()


BEGIN = "abcdon"
FIRST = "ababcdonuvabab"
FRONT_PLAN = {1: "cdon", 5: "uv", 6: "cdon", 10: "cdon", 11: "uv", 16: "uv"}


def front_remote(sizes, shapes, tlen, slen, x, mem, masters):
    weights = [((*sizes, *s), BF) for s in shapes[:4]]
    count = 8 * gather_bulk_sems(sizes)
    scratch = front_scratch()
    scratch[-3:-1] = [pltpu.VMEM(*w) for w in weights[:2]]
    return call(
        functools.partial(front_remote_kernel, sizes, shapes), "front", [tlen, slen, x, mem, *masters],
        [SM, SM, HB, HB] + [VM] * 5, (*FRONT_OUTS, *SEG_OUTS, *weights, ((6, D), F32), ((32,), jnp.int32)),
        [HB] * (KEPT + 7) + [VM, SM],
        scratch
        + [pltpu.VMEM((ROW, 128), F32), pltpu.VMEM(shapes[2], BF), pltpu.VMEM(shapes[3], BF), pltpu.VMEM((*sizes, 1, 128), F32),
           pltpu.VMEM((32, 128), F32), pltpu.VMEM((24, 128), F32)]
        + [pltpu.SemaphoreType.DMA((count,))] * 2,
        dict(collective_id=0, has_side_effects=True),
    )


def back_remote_kernel(sizes, shapes, norms, rest, *refs):
    refs = list(refs)
    ins, segs, grads, (tgrad, mgrad), totals = take(refs, TAKEN - 1), take(refs, 2), take(refs, 4), take(refs, 2), take(refs, 5)
    kept, (tgrad_s, mgrad_s), work = take(refs, TAKEN), take(refs, 2), take(refs, 14)
    sems, gin, gout, gnorm, lined, flat, shards = take(refs, 7)
    staged, halves = take(refs, 4), take(refs, 7)
    bufs, (send, recv) = [take(refs, 3) for _ in range(8)], refs
    place, mover = Place(sizes), Mover(sems)
    loads = [mover.start(grads[k], staged[k]) for k in (3, 2, 0, 1)]
    coming = [mover.start(segs[0], work[0]), mover.start(segs[1], work[1])] + back_loads(mover, ins, kept)
    place.greet(True)
    pool, half = Sems(send, recv), sizes[0] // 2
    flows_by = {}

    def begin(name, k, grad, into, total, p, q, low=0, part=None):
        flows_by[name] = until_done(reduce_bulk(place, grad, into, *bufs[k], total, p, q, pool, low, part))
        next(flows_by[name])

    def go_on(names):
        for name in names:
            if name in flows_by and next(flows_by[name]) is DONE:
                del flows_by[name]

    for name, cp, k, p, q, low in zip("duio", loads, (3, 2, 0, 1), (2, 1, 2, 1), (1, 2, 1, 2), (0, 0, half, half)):
        cp.wait()
        begin(name, k, staged[k], halves[k], totals[k], p, q, low)
    count = [0]

    def pump():
        count[0] += 1
        go_on(PLAN.get(count[0], ""))

    def ready(stage):
        if stage == "first":
            for cp in coming[:-3]:
                cp.wait()
        if stage == "target":
            mover.store(tgrad_s, tgrad)
            for cp in coming[-3:]:
                cp.wait()
        if stage == "memory":
            mover.store(mgrad_s, mgrad)
        if stage == "outward":
            begin("w", 4, gout, halves[5], totals[1], 1, 2)
            one = [jnp.sum(gnorm[8 * i:8 * i + 8, :], 0, keepdims=True) for i in range(2)]
            more = [jnp.sum(rest[8 * i:8 * i + 8, :], 0, keepdims=True) for i in range(4)]
            norms_to_shards([one[0], more[2], more[0], one[1], more[3], more[1]], flat, lined, shards)
            begin("n", 5, shards, halves[6], totals[4], 1, 2)
        if stage == "inward":
            rows = shapes[0][0] // 2
            begin("a", 6, gin, halves[4], totals[0], 2, 1, 0, (0, rows))
            begin("b", 7, gin, halves[4], totals[0], 1, 2, 0, (rows, rows))

    back_compute(
        *kept, norms, tgrad_s, mgrad_s, gin.reshape(3 * D, D), gout.reshape(D, D), gnorm, *work, ready, pump)
    go_on(REST)
    while flows_by:
        go_on("abiowndu")
    mover.finish()


PLAN = {3: "du", 4: "io", 8: "duwn", 10: "duo", 12: "wni", 13: "wn", 15: "ab", 16: "io"}
REST = "ab"


def back_remote(sizes, shapes, norms, rest, ins, segs, grads):
    half = sizes[0] // 2
    counts = (half, half, sizes[0], sizes[0])
    grads = [g.reshape(n, *sizes[1:], *s) for g, n, s in zip(grads, counts, shapes)]
    halves = [((n, *sizes[1:3], *s), BF) for n, s in zip((*counts, half, half), (*shapes[:4], *shapes[:2]))]
    halves.append(((*sizes[:3], *shapes[4]), F32))
    rows, cols = shapes[0]
    flows_of = [(n, s, BF) for n, s in zip(counts, shapes)] + [
        (half, shapes[1], BF), (sizes[0], shapes[4], F32), (half, (rows // 2, cols), BF), (half, (rows // 2, cols), BF)]
    bufs = [pltpu.VMEM(s, d) for n, shape, d in flows_of for s in reduce_bulk_bufs(sizes, n, shape)]
    return call(
        functools.partial(back_remote_kernel, sizes, shapes), "back", [norms, rest, *ins, *segs, *grads],
        [VM, VM] + [HB] * (TAKEN + 5),
        [((ROW, D), F32)] * 2 + [(s, F32) for s in shapes], [HB] * 2 + [VM] * 5,
        back_scratch()
        + [pltpu.VMEM((half, *sizes[1:], *shapes[0]), BF), pltpu.VMEM((half, *sizes[1:], *shapes[1]), BF),
           pltpu.VMEM((16, D), F32), pltpu.VMEM((32, 128), F32), pltpu.VMEM((24, 128), F32), pltpu.VMEM((*sizes, 1, 128), F32)]
        + [pltpu.VMEM(g.shape, BF) for g in grads] + [pltpu.VMEM(*h) for h in halves]
        + bufs + [pltpu.SemaphoreType.DMA((8 * reduce_bulk_sems(sizes),))] * 2,
        dict(collective_id=1, has_side_effects=True),
    )


def shard_views(inward, outward, expand, shrink, norms):
    arrays, shapes = [], []
    for x, wide in ((inward, D), (outward, D), (expand, FF), (shrink, D)):
        cols = wide if x.shape[0] >= 16 * wide else D
        arrays.append(x.reshape(-1, 128))
        shapes.append((x.shape[0] // cols, cols))
    arrays.append(norms.reshape(1, -1))
    shapes.append((1, -(-norms.shape[0] // 128) * 128))
    return arrays, tuple(shapes)


def body(
    sizes, target, memory, cotangent, target_lengths, source_lengths,
    inward_master, inward_mean, inward_square, outward_master, outward_mean, outward_square,
    expand_master, expand_mean, expand_square, shrink_master, shrink_mean, shrink_square,
    norms_master, norms_mean, norms_square,
):
    flat, shapes = shard_views(inward_master, outward_master, expand_master, shrink_master, norms_master)
    norm_count = norms_master.shape[0]
    means, _ = shard_views(inward_mean, outward_mean, expand_mean, shrink_mean, norms_mean)
    squares, _ = shard_views(inward_square, outward_square, expand_square, shrink_square, norms_square)
    x, mem, cot = target[0], memory[0], cotangent[0]
    if sizes[1:] == (2, 2, 2) and norm_count == 96 and all(s[0] % 16 == 0 for s in shapes[:4]):
        *kept, trow, tcol, scol, win, wout, up, down, norms, table = front_remote(
            sizes, shapes, target_lengths, source_lengths, x, mem, flat)
        win, wout = win.reshape(6 * D, D), wout.reshape(2 * D, D)
        q1, k1, v1, c1, lse1, xh1, rs1, q2, k2, v2 = kept
        result, dk2, dv2, dh1, gin, gout, gup, gdown, rest = middle(
            target_lengths, table, mem, cot, q2, k2, v2, xh1, win, wout, up.reshape(D, FF), down.reshape(FF, D), norms,
            trow, scol)
        tgrad, mgrad, *sums = back_remote(
            sizes, shapes, norms, rest, [x, q1, k1, v1, c1, lse1, xh1, rs1, dh1, win, wout, dk2, dv2], [trow, tcol],
            [gin, gout, gup, gdown])
    else:
        padding = ((0, 0), (0, shapes[4][1] - norm_count))
        win, wout, up, down, norms = gather_all(
            sizes, [*flat[:4], jnp.pad(flat[4], padding)], shapes, [BF, BF, BF, BF, F32])
        norms = norms.reshape(-1, norms.shape[-1])[:, :norm_count].reshape(6, D)
        result, tgrad, mgrad, gin, gout, gup, gdown, gnorm = layer(
            target_lengths, source_lengths, x, mem, cot,
            win.reshape(6 * D, D), wout.reshape(2 * D, D), up.reshape(D, FF), down.reshape(FF, D), norms,
        )
        gnorm = jnp.pad(gnorm.reshape(-1, norm_count), padding)
        grads = [g.reshape(*sizes, *s) for g, s in zip((gin, gout, gup, gdown, gnorm), shapes)]
        sums = reduce_all(sizes, grads, shapes)
    tgrad, mgrad, *outs = adam_all([tgrad, mgrad], sums, means, squares, (*shapes[:4], (1, norm_count)))
    return (result[None], tgrad[None], mgrad[None], *[x.reshape(-1) for x in outs])


def solution(mesh):
    rows, cols = mesh.shape["dp"], mesh.shape["shard"]
    both = ("dp", "shard")
    row, flat = P(both, None, None), P(both)
    return jax.shard_map(
        functools.partial(body, (rows // 2, 2, cols // 2, 2)),
        mesh=mesh,
        in_specs=(row, row, row, P(both, None), P(both, None), *[flat] * 15),
        out_specs=(row, row, row, *[flat] * 15),
        check_vma=False,
    )
```

```python
import functools
import jax
import jax.numpy as jnp
from jax import lax
from jax.experimental import pallas as pl
from jax.experimental.pallas import tpu as pltpu
from jax.sharding import PartitionSpec as P

MESH = pl.DeviceIdType.MESH
BF = jnp.bfloat16
F32 = jnp.float32
learn_rate = 0.001
beta_one = 0.9
beta_two = 0.999
STEP = 10


class Place:
    def __init__(self, sizes):
        self.sizes = sizes
        dp, sh = lax.axis_index("dp"), lax.axis_index("shard")
        self.at = (dp // sizes[1], dp % sizes[1], sh // sizes[3], sh % sizes[3])

    def device(self, axis, coord):
        a, b, c, e = [coord if i == axis else v for i, v in enumerate(self.at)]
        return (a * self.sizes[1] + b, c * self.sizes[3] + e)

    def greet(self, far=False):
        barrier = pltpu.get_barrier_semaphore()
        count = 0
        for axis in range(4):
            n, me = self.sizes[axis], self.at[axis]
            if n == 2:
                pl.semaphore_signal(barrier, inc=1, device_id=self.device(axis, 1 - me), device_id_type=MESH)
                count = count + 1
            else:
                for step in [s for d in range(1, n if far else 2) for s in (-d, d)]:
                    there = me + step
                    ok = (there >= 0) & (there < n)

                    @pl.when(ok)
                    def _():
                        pl.semaphore_signal(barrier, inc=1, device_id=self.device(axis, there), device_id_type=MESH)

                    count = count + ok.astype(jnp.int32)
        pl.semaphore_wait(barrier, count)


class Sems:
    def __init__(self, send, recv):
        self.send, self.recv, self.used = send, recv, 0

    def take(self):
        k = self.used
        self.used += 1
        return self.send.at[k], self.recv.at[k]


def gather_sems(order, sizes):
    return 1 + sum(2 if sizes[x] == 2 else 4 * (sizes[x] - 1) for x in order)


def gather_rounds(place, ref, order, sems):
    sizes = place.sizes
    after = []
    held = []

    def group(axis=None, coord=None):
        idx = [slice(None) if i in held else place.at[i] for i in range(4)]
        if axis is not None:
            idx[axis] = coord
        return ref.at[tuple(idx)]

    def copy(block, axis, coord, pair):
        return pltpu.make_async_remote_copy(
            src_ref=block, dst_ref=block, send_sem=pair[0], recv_sem=pair[1],
            device_id=place.device(axis, coord), device_id_type=MESH)

    def to_sibling(axis, coord, cond):
        pair = sems.take()
        idx = [slice(None) if i in held else place.at[i] for i in range(4)]
        if axis is not None:
            idx[axis] = coord
        mine = ref.at[tuple(idx)]
        idx[3] = 1 - place.at[3]
        theirs = ref.at[tuple(idx)]
        e = place.at[3]
        go = copy(mine, 3, 1 - e, pair)
        come = copy(theirs, 3, 1 - e, pair)

        def run(f):
            if cond is None:
                f()
            else:
                pl.when(cond)(f)

        run(go.start)

        def finish():
            go.wait_send()
            come.wait_recv()

        after.append(lambda: run(finish))

    to_sibling(None, None, None)
    for axis in order:
        n, me = sizes[axis], place.at[axis]
        if n == 2:
            pair = sems.take()
            go = copy(group(), axis, 1 - me, pair)
            come = copy(group(axis, 1 - me), axis, 1 - me, pair)
            go.start()
            after.append(go.wait_send)
            yield
            come.wait_recv()
            to_sibling(axis, 1 - me, None)
        else:
            for t in range(1, n):
                pending = []
                for step in (1, -1):
                    pair = sems.take()
                    out_c, in_c, to = me - step * (t - 1), me - step * t, me + step
                    can = (out_c >= 0) & (out_c < n) & (to >= 0) & (to < n)
                    gets = (in_c >= 0) & (in_c < n)
                    go = copy(group(axis, out_c), axis, to, pair)
                    come = copy(group(axis, in_c), axis, to, pair)
                    pl.when(can)(go.start)
                    after.append(lambda go=go, can=can: pl.when(can)(go.wait_send))
                    pending.append((come, gets, in_c))
                yield
                for come, gets, in_c in pending:
                    pl.when(gets)(come.wait_recv)
                    to_sibling(axis, in_c, gets)
        held.append(axis)
    yield
    for f in after:
        f()


def interleave(rounds):
    live = list(rounds)
    while live:
        still = []
        for r in live:
            try:
                next(r)
                still.append(r)
            except StopIteration:
                pass
        live = still


def flat_to_rows(src, dst, rows, cols):
    w = cols // 128
    for j in range(w):
        dst[:, j * 128:(j + 1) * 128] = src[pl.ds(j, rows, stride=w), :].astype(dst.dtype)


def rows_to_flat(value, dst, rows, cols):
    w = cols // 128
    for j in range(w):
        dst[pl.ds(j, rows, stride=w), :] = value[:, j * 128:(j + 1) * 128]


def both(a, b):
    return b if a is None else a if b is None else a & b


def when(cond, f):
    if cond is None:
        f()
    else:
        pl.when(cond)(f)


def remote(src, dst, pair, device):
    return pltpu.make_async_remote_copy(
        src_ref=src, dst_ref=dst, send_sem=pair[0], recv_sem=pair[1], device_id=device, device_id_type=MESH)


ORDERS = ((0, 2, 1), (0, 1, 2), (1, 2, 0), (0, 1, 2), (0, 1, 2))


def gather_kernel(sizes, shapes, *refs):
    n = len(shapes)
    masters, outs = refs[:n], refs[n:2 * n]
    stage, local, send, recv = refs[2 * n:3 * n], refs[3 * n], refs[3 * n + 1], refs[3 * n + 2]
    place = Place(sizes)
    copies = []
    for k, (rows, cols) in enumerate(shapes):
        if rows == 1:
            stage[k][...] = masters[k][...].astype(BF).astype(stage[k].dtype)
        else:
            flat_to_rows(masters[k], stage[k], rows, cols)
        cp = pltpu.make_async_copy(stage[k], outs[k].at[place.at], local.at[k])
        cp.start()
        copies.append(cp)
    place.greet()
    for cp in copies:
        cp.wait()
    sems = Sems(send, recv)
    interleave([gather_rounds(place, outs[k], ORDERS[k], sems) for k in range(n)])


def gather_all(mesh_sizes, masters, shapes, dtypes):
    n = len(shapes)
    total = sum(gather_sems(ORDERS[k], mesh_sizes) for k in range(n))
    vm = pl.BlockSpec(memory_space=pltpu.VMEM)
    return pl.pallas_call(
        functools.partial(gather_kernel, mesh_sizes, shapes),
        out_shape=[jax.ShapeDtypeStruct((*mesh_sizes, *s), d) for s, d in zip(shapes, dtypes)],
        in_specs=[vm] * n,
        out_specs=[pl.BlockSpec(memory_space=pl.ANY)] * n,
        scratch_shapes=[pltpu.VMEM(s, d) for s, d in zip(shapes, dtypes)]
        + [pltpu.SemaphoreType.DMA((n,)), pltpu.SemaphoreType.DMA((total,)), pltpu.SemaphoreType.DMA((total,))],
        compiler_params=pltpu.CompilerParams(collective_id=0, has_side_effects=True, vmem_limit_bytes=48 << 20),
        name="gather_weights",
    )(*masters)


def reduce_sems(order, sizes):
    return 1 + sum(1 if sizes[x] == 2 else 2 * (sizes[x] - 1) for x in order)


def reduce_rounds(place, grad, order, got, bufs, total, sems):
    sizes = place.sizes
    after = []
    e = place.at[3]

    def rdma(src, dst, axis, coord, pair):
        return pltpu.make_async_remote_copy(
            src_ref=src, dst_ref=dst, send_sem=pair[0], recv_sem=pair[1],
            device_id=place.device(axis, coord), device_id_type=MESH)

    def add_into(dst, src):
        dst[...] = (dst[...].astype(F32) + src[...].astype(F32)).astype(dst.dtype)

    def each(dims, f):
        count = 1
        for d in dims:
            count *= d
        if count == 1:
            f(tuple(0 for _ in dims))
            return

        def step(i, _):
            idx = []
            for d in reversed(dims):
                idx.append(i % d)
                i = i // d
            f(tuple(reversed(idx)))
            return 0

        lax.fori_loop(0, count, step, 0)

    cp = rdma(grad.at[:, :, :, 1 - e], got, 3, 1 - e, sems.take())
    cp.start()
    yield
    cp.wait()
    each(sizes[:3], lambda i: add_into(got.at[i], grad.at[(*i, e)]))
    cur, left = got, [0, 1, 2]
    for axis, buf in zip(order, bufs):
        n, me = sizes[axis], place.at[axis]
        pos = left.index(axis)
        rest = [x for x in left if x != axis]
        dims = [sizes[x] for x in rest]

        def part(ref, coord):
            return ref.at[tuple(coord if i == pos else slice(None) for i in range(len(left)))]

        def one(ref, coord, i):
            i = list(i)
            i.insert(pos, coord)
            return ref.at[tuple(i)]

        last = not rest
        if n == 2:
            cp = rdma(part(cur, 1 - me), buf, axis, 1 - me, sems.take())
            cp.start()
            yield
            cp.wait()
            if last:
                total[...] = buf[...].astype(F32) + cur[me].astype(F32)
            else:
                each(dims, lambda i: add_into(buf.at[i], one(cur, me, i)))
        else:
            for t in range(n - 1):
                for way, step in enumerate((1, -1)):
                    j = n - 1 - t if step == 1 else t
                    to, back = me + step, me - step
                    ahead = (j > me) if step == 1 else (j < me)
                    gets = ahead & (back >= 0) & (back < n)
                    pair = sems.take()
                    come = rdma(part(cur, j), buf.at[way, j], axis, to, pair)

                    @pl.when(gets)
                    def _():
                        come.wait_recv()
                        each(dims, lambda i: add_into(one(cur, j, i), buf.at[(way, j, *i)]))

                    pl.when(ahead)(come.start)
                    after.append(lambda come=come, ahead=ahead: pl.when(ahead)(come.wait_send))
                    ends = (j == me) & (back >= 0) & (back < n)
                    after.append(lambda come=come, ends=ends: pl.when(ends)(come.wait_recv))
                yield
            for f in after:
                f()
            after = []
            keep = buf.at[0, me]

            def close(i):
                mine = one(cur, me, i)[...].astype(F32)
                v = mine + jnp.where(me > 0, buf[(0, me, *i)].astype(F32), 0.0)
                v = v + jnp.where(me < n - 1, buf[(1, me, *i)].astype(F32), 0.0)
                if last:
                    total[...] = v
                else:
                    buf[(0, me, *i)] = v.astype(buf.dtype)

            each(dims, close)
            buf = keep
        cur, left = buf, rest
    for f in after:
        f()


def reduce_bufs(order, sizes, shape):
    left, out = [0, 1, 2], [(*sizes[:3], *shape)]
    for axis in order:
        rest = [x for x in left if x != axis]
        dims = tuple(sizes[x] for x in rest)
        out.append((*dims, *shape) if sizes[axis] == 2 else (2, sizes[axis], *dims, *shape))
        left = rest
    return out


BACK = tuple(tuple(reversed(o)) for o in ORDERS)


def adam(mean_old, square_old, grad):
    mean_new = beta_one * mean_old + (1.0 - beta_one) * grad
    square_new = beta_two * square_old + (1.0 - beta_two) * grad * grad
    steps = float(STEP)
    mean_hat = mean_new / (1.0 - beta_one**steps)
    square_hat = square_new / (1.0 - beta_two**steps)
    return -learn_rate * mean_hat / (jnp.sqrt(square_hat) + 1e-08), mean_new


def reduce_kernel(sizes, shapes, counts, *refs):
    n = len(shapes)
    refs = list(refs)

    def take(k):
        out = refs[:k]
        del refs[:k]
        return out

    grads, totals = take(n), take(n)
    bufs = [take(c) for c in counts]
    send, recv = take(2)
    place = Place(sizes)
    place.greet()
    sems = Sems(send, recv)
    interleave([reduce_rounds(place, grads[k], BACK[k], bufs[k][0], bufs[k][1:], totals[k], sems) for k in range(n)])


def reduce_all(mesh_sizes, grads, shapes):
    n = len(shapes)
    lists = [reduce_bufs(BACK[k], mesh_sizes, shapes[k]) for k in range(n)]
    total = sum(reduce_sems(BACK[k], mesh_sizes) for k in range(n))
    vm = pl.BlockSpec(memory_space=pltpu.VMEM)
    scratch = []
    for k in range(n):
        scratch += [pltpu.VMEM(s, grads[k].dtype) for s in lists[k]]
    scratch += [pltpu.SemaphoreType.DMA((total,)), pltpu.SemaphoreType.DMA((total,))]
    return pl.pallas_call(
        functools.partial(reduce_kernel, mesh_sizes, shapes, [len(x) for x in lists]),
        out_shape=[jax.ShapeDtypeStruct(s, F32) for s in shapes],
        in_specs=[vm] * n,
        out_specs=[vm] * n,
        scratch_shapes=scratch,
        compiler_params=pltpu.CompilerParams(collective_id=1, has_side_effects=True, vmem_limit_bytes=60 << 20),
        name="reduce_gradients",
    )(*grads)


def adam_kernel(shapes, count, *refs):
    n = len(shapes)
    refs = list(refs)
    rows_in, grads, means, squares = refs[:count], refs[count:count + n], refs[count + n:count + 2 * n], refs[count + 2 * n:count + 3 * n]
    refs = refs[count + 3 * n:]
    rows_out, outs, held, sem = refs[:count], refs[count:-count - 1], refs[-count - 1:-1], refs[-1]
    copies = [pltpu.make_async_copy(a, b, sem.at[i]) for i, (a, b) in enumerate(zip(rows_in, held))]
    copies += [pltpu.make_async_copy(a, b, sem.at[count + i]) for i, (a, b) in enumerate(zip(held, rows_out))]
    for cp in copies[:count]:
        cp.start()
    for k, (rows, cols) in enumerate(shapes):
        change, mean, summed = outs[3 * k:3 * k + 3]
        if rows == 1:
            summed[...] = grads[k][:, 0:cols]
        else:
            rows_to_flat(grads[k], summed, rows, cols)
        change[...], mean[...] = adam(means[k][...], squares[k][...], summed[...])
        if k < count:
            copies[k].wait()
            copies[count + k].start()
    for cp in copies[count:]:
        cp.wait()


def adam_all(rows, grads, means, squares, shapes):
    vm, hb = pl.BlockSpec(memory_space=pltpu.VMEM), pl.BlockSpec(memory_space=pltpu.HBM)
    flat = [((r * c) // 128, 128) if r > 1 else (1, c) for r, c in shapes]
    count = len(rows)
    return pl.pallas_call(
        functools.partial(adam_kernel, shapes, count),
        out_shape=[jax.ShapeDtypeStruct(r.shape, F32) for r in rows] + [jax.ShapeDtypeStruct(f, F32) for f in flat for _ in range(3)],
        in_specs=[hb] * count + [vm] * (3 * len(shapes)),
        out_specs=[hb] * count + [vm] * (3 * len(shapes)),
        scratch_shapes=[pltpu.VMEM(r.shape, F32) for r in rows] + [pltpu.SemaphoreType.DMA((2 * count,))],
        name="adam",
    )(*rows, *grads, *means, *squares)

D = 512
HEADS = 8
HD = 64
FF = 2048
ROW = 1024
SEGS = 24
MOST = 512
QT = 256
KT = 128
PAIR = 128
NEG = -1000000000.0


def dot(a, b):
    return jnp.dot(a, b, preferred_element_type=F32)


def dot_t(a, b):
    return lax.dot_general(a, b, (((1,), (1,)), ((), ())), preferred_element_type=F32)


def t_dot(a, b):
    return lax.dot_general(a, b, (((0,), (0,)), ((), ())), preferred_element_type=F32)


def for_rows(block, f, rows=ROW):
    def step(i, _):
        f(pl.ds(pl.multiple_of(i * block, block), block))
        return 0

    lax.fori_loop(0, rows // block, step, 0)


def ends_of(lengths):
    out, total = [], jnp.int32(0)
    for i in range(SEGS):
        total = total + lengths[0, i]
        out.append(total)
    return out


def seg_at(ends, place):
    count = jnp.int32(0)
    for e in ends:
        count = count + (e <= place).astype(jnp.int32)
    return count


def pick(values, index):
    out = values[-1]
    for i in range(len(values) - 2, -1, -1):
        out = jnp.where(index <= i, values[i], out)
    return out


def seg_row(ends):
    place = lax.broadcasted_iota(jnp.int32, (1, ROW), 1)
    out = jnp.zeros((1, ROW), jnp.int32)
    for e in ends:
        out = out + (place >= e).astype(jnp.int32)
    return out.astype(F32)


def store_seg(ends, row_ref, col_ref):
    row_ref[...] = jnp.broadcast_to(seg_row(ends), (8, ROW))
    for i in range(ROW // 128):
        block = jnp.broadcast_to(row_ref[0:1, i * 128:(i + 1) * 128], (128, 128))
        col_ref[i * 128:(i + 1) * 128, :] = jnp.transpose(block)


def ranges(query_ends, key_ends, causal, tile, other, by_query):
    out = []
    here, there = (query_ends, key_ends) if by_query else (key_ends, query_ends)
    starts = [jnp.int32(0)] + there[:-1]
    for i in range(ROW // tile):
        first, last = i * tile, (i + 1) * tile - 1
        low = pick(starts, seg_at(here, first)) // other
        high = (pick(there, seg_at(here, last)) + other - 1) // other
        if causal and by_query:
            high = jnp.int32((i + 1) * tile // other)
        if causal and not by_query:
            low = jnp.int32(i * tile // other)
        out.append((low, high))
    return out


def store_ranges(ref, base, pairs):
    for i, (low, high) in enumerate(pairs):
        ref[base + 2 * i] = low
        ref[base + 2 * i + 1] = high


def head_masks():
    lane = lax.broadcasted_iota(jnp.int32, (1, PAIR), 1)
    left = (lane < HD).astype(F32).astype(BF)
    return left, (1.0 - left.astype(F32)).astype(BF)


def stack_heads(block, masks):
    return jnp.concatenate([block * masks[0], block * masks[1]], 0)


def block_diag(pair_t):
    zero = jnp.zeros((HD, pair_t.shape[1]), pair_t.dtype)
    top = jnp.concatenate([pair_t[:HD], zero], 1)
    low = jnp.concatenate([zero, pair_t[HD:]], 1)
    return jnp.concatenate([top, low], 0)


def bias_tile(key_col, query_row, k0, q0, causal):
    keys = key_col[pl.ds(k0, KT), :]
    keys = jnp.concatenate([keys] * (QT // 128), 1)
    ok = keys == query_row[0:1, pl.ds(q0, QT)]
    if causal:
        kpos = k0 + lax.broadcasted_iota(jnp.int32, (KT, QT), 0)
        qpos = q0 + lax.broadcasted_iota(jnp.int32, (KT, QT), 1)
        ok = ok & (kpos <= qpos)
    return jnp.where(ok, 0.0, NEG)


def norm_back(dh, xhat, rstd, gain):
    dx = dh * gain
    mean_dx = jnp.mean(dx, -1, keepdims=True)
    mean_xx = jnp.mean(dx * xhat, -1, keepdims=True)
    return rstd[:, 0:1] * (dx - mean_dx - xhat * mean_xx)


def fold(x):
    return jnp.sum(x.reshape(-1, 8, x.shape[-1]), 0)


def pipeline(count, *stages):
    values = {}
    last = len(stages) - 1
    for tick in range(count + last):
        for i in reversed(range(count)):
            st = tick - i
            if 0 <= st <= last:
                values[i] = stages[st](i) if st == 0 else stages[st](i, values[i])
    return [values[i] for i in range(count)]


def over(first, end, step):
    if isinstance(first, int):
        for i in range(first, end):
            step(i, 0)
    else:
        lax.fori_loop(first, end, step, 0)


def columns(hp):
    return slice(hp * PAIR, (hp + 1) * PAIR)


def score_tile(k0, q0, q, k, key_col, query_row, causal, scores, peak, masks):
    bias = bias_tile(key_col, query_row, k0, q0, causal)

    def meet(hp):
        return dot_t(stack_heads(k[pl.ds(k0, KT), columns(hp)], masks), q[pl.ds(q0, QT), columns(hp)])

    def keep(hp, s):
        for side in range(2):
            h = 2 * hp + side
            sh = s[side * KT:(side + 1) * KT] + bias
            scores[hp][pl.ds(k0, KT), side * QT:(side + 1) * QT] = sh
            peak[h] = jnp.maximum(peak[h], jnp.max(sh.reshape(KT // 8, 8, QT), 0))

    pipeline(HEADS // 2, meet, keep)


def weigh_tile(k0, vt, scores, acc, peak, tally):
    def weigh(hp):
        probs = []
        for side in range(2):
            h = 2 * hp + side
            sh = scores[hp][pl.ds(k0, KT), side * QT:(side + 1) * QT]
            p = jnp.exp(sh.reshape(KT // 8, 8, QT) - peak[h][None])
            tally[h] += jnp.sum(p, 0)
            probs.append(p.reshape(KT, QT).astype(BF))
        return jnp.concatenate(probs, 0)

    def spread(hp, probs):
        return dot(block_diag(vt[columns(hp), pl.ds(k0, KT)]), probs)

    def add(hp, o):
        acc[columns(hp), :] += o

    pipeline(HEADS // 2, weigh, spread, add)


def attend(tile, span, q, k, vt, key_col, query_row, causal, out, lse, scores, acc, peak, tally, pump=None):
    masks = head_masks()
    q0 = pl.multiple_of(tile * QT, QT) if not isinstance(tile, int) else tile * QT

    def place_of(j):
        return j * KT if isinstance(j, int) else pl.multiple_of(j * KT, KT)

    first, end = span
    peak[...] = jnp.full_like(peak, -3e38)

    def score(j, _):
        score_tile(place_of(j), q0, q, k, key_col, query_row, causal, scores, peak, masks)
        return 0

    over(first, end, score)
    if pump:
        pump()
    for h in range(HEADS):
        peak[h] = jnp.broadcast_to(jnp.max(peak[h], 0, keepdims=True), (8, QT))
    acc[...] = jnp.zeros_like(acc)
    tally[...] = jnp.zeros_like(tally)

    def weigh(j, _):
        weigh_tile(place_of(j), vt, scores, acc, peak, tally)
        return 0

    over(first, end, weigh)
    if pump:
        pump()
    for hp in range(HEADS // 2):
        rows = []
        for side in range(2):
            h = 2 * hp + side
            total = jnp.sum(tally[h], 0, keepdims=True)
            lse[h:h + 1, pl.ds(q0, QT)] = peak[h, 0:1, :] + jnp.log(total)
            rows.append(acc[hp * PAIR + side * HD:hp * PAIR + (side + 1) * HD, :] * (1.0 / total))
        out[pl.ds(q0, QT), hp * PAIR:(hp + 1) * PAIR] = jnp.transpose(jnp.concatenate(rows, 0)).astype(BF)


def attend_back(tile, span, k, v, kt, qt, gt, lse, inner, key_col, query_row, causal, dqt, dk, dv, dk_acc, dv_acc):
    masks = head_masks()
    k0 = pl.multiple_of(tile * KT, KT) if not isinstance(tile, int) else tile * KT
    dk_acc[...] = jnp.zeros_like(dk_acc)
    dv_acc[...] = jnp.zeros_like(dv_acc)

    def step(i, _):
        q0 = i * QT if isinstance(i, int) else pl.multiple_of(i * QT, QT)
        bias = bias_tile(key_col, query_row, k0, q0, causal)
        at = pl.ds(q0, QT)

        def meet(hp):
            cols = columns(hp)
            s = dot(stack_heads(k[pl.ds(k0, KT), cols], masks), qt[cols, at])
            return s, dot(stack_heads(v[pl.ds(k0, KT), cols], masks), gt[cols, at])

        def weigh(hp, both):
            s, dp = both
            probs, slopes = [], []
            for side in range(2):
                h = 2 * hp + side
                rows = slice(side * KT, (side + 1) * KT)
                p = jnp.exp(s[rows] + bias - lse[h:h + 1, at])
                slopes.append((p * (dp[rows] - inner[h:h + 1, at])).astype(BF))
                probs.append(p.astype(BF))
            return jnp.concatenate(probs, 0), jnp.concatenate(slopes, 0)

        def spread(hp, both):
            cols = columns(hp)
            probs, slopes = both
            to_q = dot(block_diag(kt[cols, pl.ds(k0, KT)]), slopes)
            return dot_t(gt[cols, at], probs), dot_t(qt[cols, at], slopes), to_q

        def add(hp, terms):
            to_v, to_k, to_q = terms
            for acc, to in ((dv_acc, to_v), (dk_acc, to_k)):
                acc[hp * PAIR:hp * PAIR + HD, :] += to[:HD, :KT]
                acc[hp * PAIR + HD:(hp + 1) * PAIR, :] += to[HD:, KT:]
            dqt[columns(hp), at] += to_q

        pipeline(HEADS // 2, meet, weigh, spread, add)
        return 0

    over(span[0], span[1], step)
    dk[pl.ds(k0, KT), :] = jnp.transpose(dk_acc[...]).astype(BF)
    dv[pl.ds(k0, KT), :] = jnp.transpose(dv_acc[...]).astype(BF)


def flip(src, dst):
    for i in range(ROW // 128):
        dst[:, i * 128:(i + 1) * 128] = jnp.transpose(src[i * 128:(i + 1) * 128, :])


def standard(r):
    centered = r - jnp.mean(r, -1, keepdims=True)
    spread = jnp.mean(centered * centered, -1, keepdims=True)
    scale = lax.rsqrt(spread + 1e-05)
    return centered * scale, scale


def into_attention(g, c, inner, at, heads):
    both = g.astype(F32) * c.astype(F32)
    high = both.astype(BF)
    low = (both - high.astype(F32)).astype(BF)
    inner[:, at] = dot_t(heads, high) + dot_t(heads, low)


def head_rows():
    at = lax.broadcasted_iota(jnp.int32, (HEADS, D), 1) // HD == lax.broadcasted_iota(jnp.int32, (HEADS, D), 0)
    return at.astype(F32).astype(BF)


class Mover:
    def __init__(self, sems):
        self.sems, self.used, self.out = sems, 0, []

    def start(self, src, dst):
        cp = pltpu.make_async_copy(src, dst, self.sems.at[self.used])
        self.used += 1
        cp.start()
        return cp

    def store(self, src, dst):
        self.out.append(self.start(src, dst))

    def finish(self):
        for cp in self.out:
            cp.wait()


def own_spans():
    return [(max(0, (i * QT - MOST + 1) // KT), (i + 1) * QT // KT) for i in range(ROW // QT)]


def own_spans_back():
    return [(j * KT // QT, min(ROW // QT, ((j + 1) * KT - 1 + MOST - 1) // QT + 1)) for j in range(ROW // KT)]


def front_compute(x, mem, win, wout, norms, q1, k1, v1, c1, lse1, xh1, rs1, q2, k2, v2, trow, tcol, vt, scores, acc, peak, tally, ready, pump):
    ready("first")
    for i in range(ROW // 256):
        at = slice(i * 256, (i + 1) * 256)
        for out, w in ((q1, 0), (k1, 1), (v1, 2)):
            y = dot(x[at, :], win[w * D:(w + 1) * D, :]).astype(BF)
            out[at, :] = y * BF(0.125) if w == 0 else y
        pump()
    ready("projected")
    flip(v1, vt)
    for i, span in enumerate(own_spans()):
        attend(i, span, q1, k1, vt, tcol, trow, True, c1, lse1, scores, acc, peak, tally, pump)
    ready("second")
    for i in range(ROW // 256):
        at = slice(i * 256, (i + 1) * 256)
        for out, w in ((k2, 4), (v2, 5)):
            out[at, :] = dot(mem[at, :], win[w * D:(w + 1) * D, :]).astype(BF)
        pump()
    ready("keys")
    for i in range(ROW // 256):
        at = slice(i * 256, (i + 1) * 256)
        xhat, scale = standard(x[at, :].astype(F32) + dot(c1[at, :], wout[0:D, :]))
        xh1[at, :] = xhat
        rs1[at, :] = jnp.broadcast_to(scale, (256, 128))
        h = xhat * norms[0:1, :] + norms[3:4, :]
        q2[at, :] = dot(h.astype(BF), win[3 * D:4 * D, :]).astype(BF) * BF(0.125)
        pump()


FRONT_OUTS = (
    ((ROW, D), BF), ((ROW, D), BF), ((ROW, D), BF), ((ROW, D), BF), ((HEADS, ROW), F32),
    ((ROW, D), F32), ((ROW, 128), F32), ((ROW, D), BF), ((ROW, D), BF), ((ROW, D), BF),
)
KEPT = len(FRONT_OUTS)


def front_scratch():
    return (
        [pltpu.VMEM(s, d) for s, d in FRONT_OUTS]
        + [pltpu.VMEM((8, ROW), F32), pltpu.VMEM((ROW, 128), F32), pltpu.VMEM((D, ROW), BF)]
        + [pltpu.VMEM((ROW, D), F32)] * 4
        + [pltpu.VMEM((D, QT), F32), pltpu.VMEM((HEADS, 8, QT), F32), pltpu.VMEM((HEADS, 8, QT), F32)]
        + [pltpu.VMEM((ROW, D), BF)] * 2
        + [pltpu.VMEM((6 * D, D), BF), pltpu.VMEM((2 * D, D), BF), pltpu.SemaphoreType.DMA((40,))]
    )


def take(refs, k):
    out = refs[:k]
    del refs[:k]
    return out


SEG_OUTS = (((8, ROW), F32), ((ROW, 128), F32), ((ROW, 128), F32))


def segments_of(tlen, slen, trow, tcol, scol, table):
    tends, sends = ends_of(tlen), ends_of(slen)
    store_seg(sends, trow, scol)
    store_seg(tends, trow, tcol)
    store_ranges(table, 0, ranges(tends, sends, False, QT, KT, True))
    store_ranges(table, 8, ranges(tends, sends, False, KT, QT, False))


def front_kernel(tlen, slen, x, mem, win, wout, norms, *refs):
    refs = list(refs)
    outs, segs, table, kept = take(refs, 10), take(refs, 3), refs.pop(0), take(refs, 10)
    trow, tcol, vt = take(refs, 3)
    scores, (acc, peak, tally), (xs, ms, ws, os, sems, scol) = take(refs, 4), take(refs, 3), refs
    mover = Mover(sems)
    coming = [mover.start(x, xs), mover.start(win, ws), mover.start(wout, os), mover.start(mem, ms)]
    segments_of(tlen, slen, trow, tcol, scol, table)
    for k, ref in enumerate((trow, tcol, scol)):
        mover.store(ref, segs[k])

    def ready(stage):
        if stage == "first":
            coming[0].wait()
            coming[1].wait()
        if stage == "second":
            coming[2].wait()
            coming[3].wait()

    front_compute(xs, ms, ws, os, norms, *kept, trow, tcol, vt, scores, acc, peak, tally, ready, lambda: None)
    for k in range(10):
        mover.store(kept[k], outs[k])
    mover.finish()


def middle_kernel(
    tlen, table, mem, cot, q2, k2, v2, xh1, win, wout, up, down, norms, rows_in, cols_in,
    result, dk_out, dv_out, dh1, gin, gout, gup, gdown, gnorm,
    mem_s, cot_s, q_s, k_s, v_s, xh_s, win_s, wout_s, up_s, down_s,
    result_s, dk, dv, dh1_s, gin_s, gout_s, gup_s, gdown_s,
    trow, scol, flipped, qt, gt, c2, lse, inner, acc, peak, tally, spare, other, dr,
    h1b, h2b, act, du, dy, pre, turn, dc, dq, dqt, dk_acc, dv_acc, sems,
):
    mover = Mover(sems)
    pairs = (
        (k2, k_s), (q2, q_s), (v2, v_s), (wout.at[pl.ds(D, D)], wout_s), (xh1, xh_s), (up, up_s), (down, down_s),
        (cot, cot_s), (win.at[pl.ds(3 * D, D)], win_s), (mem, mem_s),
    )
    segs = [mover.start(rows_in, trow), mover.start(cols_in, scol)]
    coming = [mover.start(a, b) for a, b in pairs]
    gnorm[...] = jnp.zeros_like(gnorm)
    heads = head_rows()
    for cp in segs + coming[:3]:
        cp.wait()
    flip(v_s, flipped)

    def forward(i, _):
        span = (table[2 * i], table[2 * i + 1])
        attend(i, span, q_s, k_s, flipped, scol, trow, False, c2, lse, (other, dh1_s, dr, spare), acc, peak, tally)
        return 0

    lax.fori_loop(0, ROW // QT, forward, 0)
    for k in range(3, 8):
        coming[k].wait()
    live_end = ends_of(tlen)[SEGS - 2]
    block = 256

    def rows(i, _):
        at = pl.ds(pl.multiple_of(i * block, block), block)
        h = xh_s[at, :] * norms[0:1, :] + norms[3:4, :]
        h1b[at, :] = h.astype(BF)
        xh2, rs2 = standard(h + dot(c2[at, :], wout_s[...]))
        h = xh2 * norms[1:2, :] + norms[4:5, :]
        hb = h.astype(BF)
        h2b[at, :] = hb

        def cols_of(j):
            return slice(j * D, (j + 1) * D)

        def widen(j):
            u = dot(hb, up_s[:, cols_of(j)])
            pre[:, cols_of(j)] = u
            return u

        def gate(j, u):
            a = (u / (1.0 + jnp.exp(-u))).astype(BF)
            act[at, cols_of(j)] = a
            return a

        def narrow(j, a):
            return dot(a, down_s[cols_of(j), :])

        parts = pipeline(FF // D, widen, gate, narrow)
        r3 = h + ((parts[0] + parts[1]) + (parts[2] + parts[3]))
        xhat, rstd = standard(r3)
        result_s[at, :] = (xhat * norms[2:3, :] + norms[5:6, :]).astype(BF)
        place = i * block + lax.broadcasted_iota(jnp.int32, (block, D), 0)
        seed = jnp.where(place < live_end, cot_s[at, :].astype(F32), 0.0)
        gnorm[0:8, :] += fold(seed * xhat)
        gnorm[8:16, :] += fold(seed)
        dr3 = norm_back(seed, xhat, rstd, norms[2:3, :])
        dyb = dr3.astype(BF)
        dy[at, :] = dyb

        def widen_back(j):
            return dot_t(dyb, down_s[cols_of(j), :])

        def gate_back(j, grad):
            u = pre[:, cols_of(j)]
            sig = 1.0 / (1.0 + jnp.exp(-u))
            d = (grad * (sig * (1.0 + u * (1.0 - sig)))).astype(BF)
            du[at, cols_of(j)] = d
            return d

        def narrow_back(j, d):
            return dot_t(d, up_s[:, cols_of(j)])

        parts = pipeline(FF // D, widen_back, gate_back, narrow_back)
        dh = dr3 + ((parts[0] + parts[1]) + (parts[2] + parts[3]))
        gnorm[16:24, :] += fold(dh * xh2)
        gnorm[24:32, :] += fold(dh)
        r = norm_back(dh, xh2, rs2, norms[1:2, :])
        dr[at, :] = r
        rb = r.astype(BF)
        dy2 = dot_t(rb, wout_s[...]).astype(BF)
        turn[at, :] = rb
        dc[at, :] = dy2
        into_attention(dy2, c2[at, :], inner, at, heads)
        return 0

    lax.fori_loop(0, ROW // block, rows, 0)
    mover.store(result_s, result)
    for j in range(FF // D):
        cols = slice(j * D, (j + 1) * D)
        gdown_s[cols, :] = t_dot(act[:, cols], dy[...]).astype(BF)
    mover.store(gdown_s, gdown)
    for j in range(FF // D):
        cols = slice(j * D, (j + 1) * D)
        gup_s[:, cols] = t_dot(h2b[...], du[:, cols]).astype(BF)
    mover.store(gup_s, gup)
    gout_s[...] = t_dot(c2[...], turn[...]).astype(BF)
    mover.store(gout_s, gout)
    flip(k_s, flipped)
    flip(q_s, qt)
    flip(dc, gt)
    dqt[...] = jnp.zeros_like(dqt)

    def backward(j, _):
        span = (table[8 + 2 * j], table[9 + 2 * j])
        attend_back(j, span, k_s, v_s, flipped, qt, gt, lse, inner, scol, trow, False, dqt, dk, dv, dk_acc, dv_acc)
        return 0

    lax.fori_loop(0, ROW // KT, backward, 0)
    mover.store(dk, dk_out)
    mover.store(dv, dv_out)
    coming[8].wait()
    coming[9].wait()
    gin_s[D:2 * D, :] = t_dot(mem_s[...], dk[...]).astype(BF)
    gin_s[2 * D:3 * D, :] = t_dot(mem_s[...], dv[...]).astype(BF)

    def end(at):
        q = jnp.transpose(dqt[:, at] * 0.125).astype(BF)
        dq[at, :] = q
        dh1_s[at, :] = dr[at, :] + dot_t(q, win_s[...])

    for_rows(256, end)
    mover.store(dh1_s, dh1)
    gin_s[0:D, :] = t_dot(h1b[...], dq[...]).astype(BF)
    mover.store(gin_s, gin)
    mover.finish()


def back_compute(
    x, q1, k1, v1, c1, lse, xh1, rs1, dh1, win, wout, dk2, dv2, win2, norms, tgrad, mgrad, gin, gout, gnorm,
    trow, tcol, kt, qt, gt, inner, dr, dc, dq, dk, dv, dqt, dk_acc, dv_acc, ready, pump,
):
    heads = head_rows()
    ready("first")
    for i in range(ROW // 256):
        at = slice(i * 256, (i + 1) * 256)
        dh, xhat = dh1[at, :], xh1[at, :]
        gain, bias = fold(dh * xhat), fold(dh)
        gnorm[0:8, :] = gain if i == 0 else gnorm[0:8, :] + gain
        gnorm[8:16, :] = bias if i == 0 else gnorm[8:16, :] + bias
        r = norm_back(dh, xhat, rs1[at, :], norms[0:1, :])
        dr[at, :] = r
        rb = r.astype(BF)
        g = dot_t(rb, wout[...]).astype(BF)
        dq[at, :] = rb
        dc[at, :] = g
        into_attention(g, c1[at, :], inner, at, heads)
        pump()
    gout[...] = t_dot(c1[...], dq[...]).astype(BF)
    ready("outward")
    flip(k1, kt)
    flip(q1, qt)
    flip(dc, gt)
    pump()
    dqt[...] = jnp.zeros_like(dqt)
    for j, span in enumerate(own_spans_back()):
        attend_back(j, span, k1, v1, kt, qt, gt, lse, inner, tcol, trow, True, dqt, dk, dv, dk_acc, dv_acc)
        pump()
    gin[D:2 * D, :] = t_dot(x[...], dk[...]).astype(BF)
    gin[2 * D:3 * D, :] = t_dot(x[...], dv[...]).astype(BF)
    for i in range(ROW // 256):
        at = slice(i * 256, (i + 1) * 256)
        dq[at, :] = jnp.transpose(dqt[:, at] * 0.125).astype(BF)
    gin[0:D, :] = t_dot(x[...], dq[...]).astype(BF)
    ready("inward")
    for i in range(ROW // 256):
        at = slice(i * 256, (i + 1) * 256)
        t = dr[at, :]
        for k, g in enumerate((dq, dk, dv)):
            t = t + dot_t(g[at, :], win[k * D:(k + 1) * D, :])
        tgrad[at, :] = t
        pump()
    ready("target")
    for i in range(ROW // 256):
        at = slice(i * 256, (i + 1) * 256)
        mgrad[at, :] = dot_t(dk2[at, :], win2[0:D, :]) + dot_t(dv2[at, :], win2[D:2 * D, :])
        pump()
    ready("memory")


BACK_INS = (
    ((ROW, D), BF), ((ROW, D), BF), ((ROW, D), BF), ((ROW, D), BF), ((ROW, D), BF), ((HEADS, ROW), F32),
    ((ROW, D), F32), ((ROW, 128), F32), ((ROW, D), F32), ((3 * D, D), BF), ((D, D), BF),
    ((ROW, D), BF), ((ROW, D), BF), ((2 * D, D), BF),
)
TAKEN = len(BACK_INS)


def back_scratch():
    return (
        [pltpu.VMEM(s, d) for s, d in BACK_INS]
        + [pltpu.VMEM((ROW, D), F32)] * 2
        + [pltpu.VMEM((8, ROW), F32), pltpu.VMEM((ROW, 128), F32)]
        + [pltpu.VMEM((D, ROW), BF)] * 3
        + [pltpu.VMEM((HEADS, ROW), F32), pltpu.VMEM((ROW, D), F32)]
        + [pltpu.VMEM((ROW, D), BF)] * 4
        + [pltpu.VMEM((D, ROW), F32), pltpu.VMEM((D, KT), F32), pltpu.VMEM((D, KT), F32), pltpu.SemaphoreType.DMA((40,))]
    )


def back_loads(mover, ins, kept):
    win, wout = ins[9], ins[10]
    parts = list(ins[:9]) + [win.at[pl.ds(0, 3 * D)], wout.at[pl.ds(0, D)], ins[11], ins[12], win.at[pl.ds(4 * D, 2 * D)]]
    order = (8, 6, 7, 10, 4, 2, 1, 3, 5, 0, 9, 11, 12, 13)
    return [mover.start(parts[k], kept[k]) for k in order]


def back_kernel(norms, *refs):
    refs = list(refs)
    ins, segs, (tgrad, mgrad, gin, gout, gnorm), kept = take(refs, TAKEN - 1), take(refs, 2), take(refs, 5), take(refs, TAKEN)
    (tgrad_s, mgrad_s), work, sems = refs[:2], refs[2:-1], refs[-1]
    mover = Mover(sems)
    coming = [mover.start(segs[0], work[0]), mover.start(segs[1], work[1])] + back_loads(mover, ins, kept)

    def ready(stage):
        if stage == "first":
            for cp in coming:
                cp.wait()

    back_compute(*kept, norms, tgrad_s, mgrad_s, gin, gout, gnorm, *work, ready, lambda: None)
    mover.store(tgrad_s, tgrad)
    mover.store(mgrad_s, mgrad)
    mover.finish()


VM = pl.BlockSpec(memory_space=pltpu.VMEM)
SM = pl.BlockSpec(memory_space=pltpu.SMEM)
HB = pl.BlockSpec(memory_space=pltpu.HBM)


def call(kernel, name, ins, in_specs, outs, out_specs, scratch, params):
    return pl.pallas_call(
        kernel,
        out_shape=[jax.ShapeDtypeStruct(s, d) for s, d in outs],
        in_specs=in_specs,
        out_specs=out_specs,
        scratch_shapes=scratch,
        compiler_params=pltpu.CompilerParams(vmem_limit_bytes=62 << 20, **params),
        name=name,
    )(*ins)


def middle(tlen, table, mem, cot, q2, k2, v2, xh1, win, wout, up, down, norms, trow, scol):
    tok, tokf, flat = ((ROW, D), BF), ((ROW, D), F32), ((D, ROW), BF)
    outs = [tok, tok, tok, tokf, ((3 * D, D), BF), ((D, D), BF), ((D, FF), BF), ((FF, D), BF)]
    ins = [tok] * 5 + [tokf, ((D, D), BF), ((D, D), BF), ((D, FF), BF), ((FF, D), BF)]
    stat, tile = ((HEADS, ROW), F32), ((D, KT), F32)
    work = [((8, ROW), F32), ((ROW, 128), F32), flat, flat, flat, tok, stat, stat, ((D, QT), F32), ((HEADS, 8, QT), F32),
            ((HEADS, 8, QT), F32), tokf, tokf, tokf, tok, tok, ((ROW, FF), BF), ((ROW, FF), BF), tok, ((256, FF), F32), tok, tok, tok,
            ((D, ROW), F32), tile, tile]
    scratch = [pltpu.VMEM(*s) for s in ins + outs + work]
    return call(
        middle_kernel, "middle", [tlen, table, mem, cot, q2, k2, v2, xh1, win, wout, up, down, norms, trow, scol],
        [SM, SM] + [HB] * 10 + [VM, HB, HB], outs + [((32, D), F32)], [HB] * 8 + [VM],
        scratch + [pltpu.SemaphoreType.DMA((20,))], {},
    )


def layer(tlen, slen, x, mem, cot, win, wout, up, down, norms):
    q1, k1, v1, c1, lse1, xh1, rs1, q2, k2, v2, trow, tcol, scol, table = call(
        front_kernel, "front", [tlen, slen, x, mem, win, wout, norms], [SM, SM] + [HB] * 4 + [VM],
        [*FRONT_OUTS, *SEG_OUTS, ((32,), jnp.int32)], [HB] * 13 + [SM], front_scratch() + [pltpu.VMEM((ROW, 128), F32)], {},
    )
    result, dk2, dv2, dh1, gin_two, gout_two, gup, gdown, gnorm_rest = middle(
        tlen, table, mem, cot, q2, k2, v2, xh1, win, wout, up, down, norms, trow, scol)
    tgrad, mgrad, gin_one, gout_one, gnorm_one = call(
        back_kernel, "back", [norms, x, q1, k1, v1, c1, lse1, xh1, rs1, dh1, win, wout, dk2, dv2, trow, tcol],
        [VM] + [HB] * (TAKEN + 1),
        [((ROW, D), F32), ((ROW, D), F32), ((3 * D, D), BF), ((D, D), BF), ((16, D), F32)], [HB, HB, VM, VM, VM], back_scratch(), {},
    )
    gin, gout = jnp.concatenate([gin_one, gin_two]), jnp.concatenate([gout_one, gout_two])
    one = jnp.sum(gnorm_one.reshape(2, 8, D), 1)
    rest = jnp.sum(gnorm_rest.reshape(4, 8, D), 1)
    gnorm = jnp.stack([one[0], rest[2], rest[0], one[1], rest[3], rest[1]])
    return result, tgrad, mgrad, gin, gout, gup, gdown, gnorm


def every(dims):
    return [(a, b, c, e) for a in range(dims[0]) for b in range(dims[1]) for c in range(dims[2]) for e in range(dims[3])]


def lanes_up_to(n):
    return lax.broadcasted_iota(jnp.int32, (8, 128), 1) < n


def norms_from_shards(shards, lined, flat, out):
    for i, at in enumerate(every(shards.shape[:4])):
        lined[i:i + 1, :] = shards[at]
    n = [lined[pl.ds(k, 8, stride=4), :] for k in range(4)]
    flat[pl.ds(0, 8, stride=3), :] = jnp.where(lanes_up_to(96), n[0], pltpu.roll(n[1], 96, 1))
    flat[pl.ds(1, 8, stride=3), :] = jnp.where(lanes_up_to(64), pltpu.roll(n[1], 96, 1), pltpu.roll(n[2], 64, 1))
    flat[pl.ds(2, 8, stride=3), :] = jnp.where(lanes_up_to(32), pltpu.roll(n[2], 64, 1), pltpu.roll(n[3], 32, 1))
    for i in range(24):
        out[i // 4:i // 4 + 1, (i % 4) * 128:(i % 4 + 1) * 128] = flat[i:i + 1, :]


def norms_to_shards(rows, flat, lined, shards):
    for i in range(24):
        flat[i:i + 1, :] = rows[i // 4][:, (i % 4) * 128:(i % 4 + 1) * 128]
    r = [flat[pl.ds(k, 8, stride=3), :] for k in range(3)]
    lined[pl.ds(0, 8, stride=4), :] = r[0]
    lined[pl.ds(1, 8, stride=4), :] = jnp.where(lanes_up_to(32), pltpu.roll(r[0], 32, 1), pltpu.roll(r[1], 32, 1))
    lined[pl.ds(2, 8, stride=4), :] = jnp.where(lanes_up_to(64), pltpu.roll(r[1], 64, 1), pltpu.roll(r[2], 64, 1))
    lined[pl.ds(3, 8, stride=4), :] = pltpu.roll(r[2], 96, 1)
    for i, at in enumerate(every(shards.shape[:4])):
        shards[at] = lined[i:i + 1, :]


DONE = "done"


def until_done(flow):
    for _ in flow:
        yield None
    while True:
        yield DONE


def around(place, d):
    n = place.sizes[0]
    return lax.rem(place.at[0] + (d + n), n)


def spot(first, p, q, at_p, at_q, e):
    return (first, at_p, at_q, *e) if p < q else (first, at_q, at_p, *e)


def gather_bulk(place, ref, own, p, q, sems, span=None, part=None, before=None):
    n, e = place.sizes[0], place.at[3]
    low, high = span or (0, n)
    whole = (low, high) == (0, n)
    group = slice(None) if whole else pl.ds(low, high - low)
    rows = (pl.ds(*part),) if part else ()
    after = []

    def inside(coord):
        return None if whole else (coord >= low) & (coord < high)

    def view(first, flip_p, flip_q, core=None):
        at_p = 1 - place.at[p] if flip_p else place.at[p]
        at_q = slice(None) if flip_q is None else 1 - place.at[q] if flip_q else place.at[q]
        return ref.at[(*spot(first, p, q, at_p, at_q, (e if core is None else core,)), *rows)]

    def send(src, dst, device, cond=None):
        pair = sems.take()
        go = remote(src, dst, pair, device)
        when(cond, go.start)
        after.append((cond, go.wait_send))
        return lambda view: remote(view, view, pair, device)

    def to_sibling(flip_p, flip_q):
        come = send(view(group, flip_p, flip_q), view(group, flip_p, flip_q), place.device(3, 1 - e))
        after.append((None, come(view(group, flip_p, flip_q, 1 - e)).wait_recv))

    own = own.at[rows] if rows else own
    mine = inside(place.at[0])
    come = {}
    for d in range(1, n):
        come[d] = send(own, view(place.at[0], 0, 0), place.device(0, around(place, d)), mine)
    yield
    for d in range(1, n):
        src = around(place, -d)
        when(inside(src), come[d](view(src, 0, 0)).wait_recv)
    if before:
        before()
    here = view(group, 0, 0)
    to_p, to_q = place.device(p, 1 - place.at[p]), place.device(q, 1 - place.at[q])
    from_p, from_q = send(here, here, to_p), send(here, here, to_q)
    to_sibling(0, 0)
    yield
    there = view(group, 1, 0)
    from_p(there).wait_recv()
    from_pq = send(there, there, to_q)
    to_sibling(1, 0)
    yield
    from_q(view(group, 0, 1)).wait_recv()
    to_sibling(0, 1)
    from_pq(view(group, 1, 1)).wait_recv()
    to_sibling(1, 1)
    yield
    for cond, f in after:
        when(cond, f)


def gather_bulk_sems(sizes):
    return sizes[0] - 1 + 3 + 4


def add_rows(dst, *srcs):
    v = srcs[0][...].astype(F32)
    for s in srcs[1:]:
        v = v + s[...].astype(F32)
    dst[...] = v.astype(dst.dtype)


def reduce_bulk(place, grad, half, from_q, from_p, from_z, total, p, q, sems, low=0, part=None):
    n, e = place.sizes[0], place.at[3]
    count = grad.shape[0]
    whole = count == n
    rows = (pl.ds(*part),) if part else ()
    after = []
    me_p, me_q, all_of = place.at[p], place.at[q], slice(None)

    def inside(coord):
        return None if whole else (coord >= low) & (coord < low + count)

    def g(first, at_p, at_q, core):
        return grad.at[(*spot(first, p, q, at_p, at_q, (core,)), *rows)]

    def h(first, at_p, at_q):
        return half.at[(*spot(first, p, q, at_p, at_q, ()), *rows)]

    def send(src, dst, device, cond=None):
        go = remote(src, dst, sems.take(), device)
        when(cond, go.start)
        after.append((cond, go.wait_send))
        return go

    def each(f, times):
        def step(i, _):
            f(i)
            return 0

        lax.fori_loop(0, times, step, 0)

    sibling = place.device(3, 1 - e)
    core_q, core_p, core = [
        send(g(all_of, at_p, at_q, 1 - e), h(all_of, at_p, at_q), sibling)
        for at_p, at_q in ((all_of, 1 - me_q), (1 - me_p, me_q), (me_p, me_q))]
    yield
    core_q.wait_recv()

    def far(i):
        a, at_p = lax.div(i, 2), lax.rem(i, 2)
        add_rows(h(a, at_p, 1 - me_q), g(a, at_p, 1 - me_q, e), h(a, at_p, 1 - me_q))

    each(far, 2 * count)
    come_q = send(h(all_of, all_of, 1 - me_q), from_q, place.device(q, 1 - me_q))
    yield
    core_p.wait_recv()
    come_q.wait_recv()
    each(lambda a: add_rows(h(a, 1 - me_p, me_q), g(a, 1 - me_p, me_q, e), h(a, 1 - me_p, me_q), from_q.at[a, 1 - me_p]), count)
    come_p = send(h(all_of, 1 - me_p, me_q), from_p, place.device(p, 1 - me_p))
    yield
    core.wait_recv()
    come_p.wait_recv()
    each(lambda a: add_rows(h(a, me_p, me_q), g(a, me_p, me_q, e), h(a, me_p, me_q), from_q.at[a, me_p], from_p.at[a]), count)
    come_z = []
    for d in range(1, n):
        to = around(place, d)
        pair = sems.take()
        go = remote(h(to - low, me_p, me_q), from_z.at[d - 1], pair, place.device(0, to))
        when(inside(to), go.start)
        after.append((inside(to), go.wait_send))
        come_z.append(remote(from_z.at[d - 1], from_z.at[d - 1], pair, place.device(0, to)))
    yield

    def close():
        for come in come_z:
            come.wait_recv()
        add_rows(total.at[rows] if rows else total, h(place.at[0] - low, me_p, me_q), *[from_z.at[d] for d in range(n - 1)])

    when(inside(place.at[0]), close)
    for cond, f in after:
        when(cond, f)


def reduce_bulk_sems(sizes):
    return 5 + sizes[0] - 1


def reduce_bulk_bufs(sizes, count, shape):
    return [(count, 2, *shape), (count, *shape), (sizes[0] - 1, *shape)]


def front_remote_kernel(sizes, shapes, tlen, slen, x, mem, *refs):
    refs = list(refs)
    masters = take(refs, 5)
    outs, segs, (win, wout, up, down, norms, table), kept = take(refs, KEPT), take(refs, 3), take(refs, 6), take(refs, KEPT)
    trow, tcol, vt = take(refs, 3)
    scores, (acc, peak, tally), (xs, ms, ws, os, sems) = take(refs, 4), take(refs, 3), take(refs, 5)
    scol, stage_up, stage_down, shards, lined, flat, send, recv = refs
    place, mover = Place(sizes), Mover(sems)
    coming = [mover.start(x, xs), mover.start(mem, ms)]
    mine = [ws.at[place.at], os.at[place.at], stage_up, stage_down]
    for k in range(4):
        flat_to_rows(masters[k], mine[k], *shapes[k])
    shards[place.at] = jnp.zeros((1, 128), F32)
    width = masters[4].shape[1]
    shards[(*place.at, slice(None), slice(0, width))] = masters[4][...].astype(BF).astype(F32)
    local = [mover.start(stage_up, up.at[place.at]), mover.start(stage_down, down.at[place.at])]
    pool, half, rows = Sems(send, recv), sizes[0] // 2, shapes[0][0] // 2
    low, high, top, low_rows = (0, half), (half, sizes[0]), (0, rows), (rows, rows)

    def flow(ref, own, p, q, *rest):
        return until_done(gather_bulk(place, ref, own, p, q, pool, *rest))

    place.greet(True)
    inward, outward = ws.at[place.at], os.at[place.at]
    flows_by = {
        "a": flow(ws, inward, 2, 1, low, top), "b": flow(ws, inward, 1, 2, low, low_rows),
        "c": flow(ws, inward, 2, 1, high, top), "d": flow(ws, inward, 1, 2, high, low_rows),
        "o": flow(os, outward, 1, 2), "n": flow(shards, shards.at[place.at], 1, 2),
        "u": flow(up, stage_up, 2, 1, None, None, local[0].wait), "v": flow(down, stage_down, 1, 2, None, None, local[1].wait),
    }

    def go_on(names):
        for name in names:
            if name in flows_by and next(flows_by[name]) is DONE:
                del flows_by[name]

    def finish(names):
        while set(names) & set(flows_by):
            go_on(names)

    go_on(BEGIN)
    segments_of(tlen, slen, trow, tcol, scol, table)
    for k, ref in enumerate((trow, tcol, scol)):
        mover.store(ref, segs[k])
    go_on(FIRST)
    finish("ab")
    count = [0]

    def pump():
        count[0] += 1
        go_on(FRONT_PLAN.get(count[0], ""))

    def ready(stage):
        if stage == "first":
            coming[0].wait()
        if stage == "projected":
            for k in range(3):
                mover.store(kept[k], outs[k])
        if stage == "second":
            finish("cdon")
            mover.store(ws, win)
            mover.store(os, wout)
            norms_from_shards(shards, lined, flat, norms)
            coming[1].wait()
        if stage == "keys":
            for k in (3, 4, 8, 9):
                mover.store(kept[k], outs[k])

    front_compute(
        xs, ms, ws.reshape(6 * D, D), os.reshape(2 * D, D), norms, *kept, trow, tcol, vt, scores, acc, peak, tally, ready, pump)
    for k in (5, 6, 7):
        mover.store(kept[k], outs[k])
    finish("uv")
    mover.finish()


BEGIN = "abcdon"
FIRST = "ababcdonuvabab"
FRONT_PLAN = {1: "cdon", 5: "uv", 6: "cdon", 10: "cdon", 11: "uv", 16: "uv"}


def front_remote(sizes, shapes, tlen, slen, x, mem, masters):
    weights = [((*sizes, *s), BF) for s in shapes[:4]]
    count = 8 * gather_bulk_sems(sizes)
    scratch = front_scratch()
    scratch[-3:-1] = [pltpu.VMEM(*w) for w in weights[:2]]
    return call(
        functools.partial(front_remote_kernel, sizes, shapes), "front", [tlen, slen, x, mem, *masters],
        [SM, SM, HB, HB] + [VM] * 5, (*FRONT_OUTS, *SEG_OUTS, *weights, ((6, D), F32), ((32,), jnp.int32)),
        [HB] * (KEPT + 7) + [VM, SM],
        scratch
        + [pltpu.VMEM((ROW, 128), F32), pltpu.VMEM(shapes[2], BF), pltpu.VMEM(shapes[3], BF), pltpu.VMEM((*sizes, 1, 128), F32),
           pltpu.VMEM((32, 128), F32), pltpu.VMEM((24, 128), F32)]
        + [pltpu.SemaphoreType.DMA((count,))] * 2,
        dict(collective_id=0, has_side_effects=True),
    )


def back_remote_kernel(sizes, shapes, norms, rest, *refs):
    refs = list(refs)
    ins, segs, grads, (tgrad, mgrad), totals = take(refs, TAKEN - 1), take(refs, 2), take(refs, 4), take(refs, 2), take(refs, 5)
    kept, (tgrad_s, mgrad_s), work = take(refs, TAKEN), take(refs, 2), take(refs, 14)
    sems, gin, gout, gnorm, lined, flat, shards = take(refs, 7)
    staged, halves = take(refs, 4), take(refs, 7)
    bufs, (send, recv) = [take(refs, 3) for _ in range(8)], refs
    place, mover = Place(sizes), Mover(sems)
    loads = [mover.start(grads[k], staged[k]) for k in (3, 2, 0, 1)]
    coming = [mover.start(segs[0], work[0]), mover.start(segs[1], work[1])] + back_loads(mover, ins, kept)
    place.greet(True)
    pool, half = Sems(send, recv), sizes[0] // 2
    flows_by = {}

    def begin(name, k, grad, into, total, p, q, low=0, part=None):
        flows_by[name] = until_done(reduce_bulk(place, grad, into, *bufs[k], total, p, q, pool, low, part))
        next(flows_by[name])

    def go_on(names):
        for name in names:
            if name in flows_by and next(flows_by[name]) is DONE:
                del flows_by[name]

    for name, cp, k, p, q, low in zip("duio", loads, (3, 2, 0, 1), (2, 1, 2, 1), (1, 2, 1, 2), (0, 0, half, half)):
        cp.wait()
        begin(name, k, staged[k], halves[k], totals[k], p, q, low)
    count = [0]

    def pump():
        count[0] += 1
        go_on(PLAN.get(count[0], ""))

    def ready(stage):
        if stage == "first":
            for cp in coming[:-3]:
                cp.wait()
        if stage == "target":
            mover.store(tgrad_s, tgrad)
            for cp in coming[-3:]:
                cp.wait()
        if stage == "memory":
            mover.store(mgrad_s, mgrad)
        if stage == "outward":
            begin("w", 4, gout, halves[5], totals[1], 1, 2)
            one = [jnp.sum(gnorm[8 * i:8 * i + 8, :], 0, keepdims=True) for i in range(2)]
            more = [jnp.sum(rest[8 * i:8 * i + 8, :], 0, keepdims=True) for i in range(4)]
            norms_to_shards([one[0], more[2], more[0], one[1], more[3], more[1]], flat, lined, shards)
            begin("n", 5, shards, halves[6], totals[4], 1, 2)
        if stage == "inward":
            rows = shapes[0][0] // 2
            begin("a", 6, gin, halves[4], totals[0], 2, 1, 0, (0, rows))
            begin("b", 7, gin, halves[4], totals[0], 1, 2, 0, (rows, rows))

    back_compute(
        *kept, norms, tgrad_s, mgrad_s, gin.reshape(3 * D, D), gout.reshape(D, D), gnorm, *work, ready, pump)
    go_on(REST)
    while flows_by:
        go_on("abiowndu")
    mover.finish()


PLAN = {3: "du", 4: "io", 8: "duwn", 10: "duo", 12: "wni", 13: "wn", 15: "ab", 16: "io"}
REST = "ab"


def back_remote(sizes, shapes, norms, rest, ins, segs, grads):
    half = sizes[0] // 2
    counts = (half, half, sizes[0], sizes[0])
    grads = [g.reshape(n, *sizes[1:], *s) for g, n, s in zip(grads, counts, shapes)]
    halves = [((n, *sizes[1:3], *s), BF) for n, s in zip((*counts, half, half), (*shapes[:4], *shapes[:2]))]
    halves.append(((*sizes[:3], *shapes[4]), F32))
    rows, cols = shapes[0]
    flows_of = [(n, s, BF) for n, s in zip(counts, shapes)] + [
        (half, shapes[1], BF), (sizes[0], shapes[4], F32), (half, (rows // 2, cols), BF), (half, (rows // 2, cols), BF)]
    bufs = [pltpu.VMEM(s, d) for n, shape, d in flows_of for s in reduce_bulk_bufs(sizes, n, shape)]
    return call(
        functools.partial(back_remote_kernel, sizes, shapes), "back", [norms, rest, *ins, *segs, *grads],
        [VM, VM] + [HB] * (TAKEN + 5),
        [((ROW, D), F32)] * 2 + [(s, F32) for s in shapes], [HB] * 2 + [VM] * 5,
        back_scratch()
        + [pltpu.VMEM((half, *sizes[1:], *shapes[0]), BF), pltpu.VMEM((half, *sizes[1:], *shapes[1]), BF),
           pltpu.VMEM((16, D), F32), pltpu.VMEM((32, 128), F32), pltpu.VMEM((24, 128), F32), pltpu.VMEM((*sizes, 1, 128), F32)]
        + [pltpu.VMEM(g.shape, BF) for g in grads] + [pltpu.VMEM(*h) for h in halves]
        + bufs + [pltpu.SemaphoreType.DMA((8 * reduce_bulk_sems(sizes),))] * 2,
        dict(collective_id=1, has_side_effects=True),
    )


def shard_views(inward, outward, expand, shrink, norms):
    arrays, shapes = [], []
    for x, wide in ((inward, D), (outward, D), (expand, FF), (shrink, D)):
        cols = wide if x.shape[0] >= 16 * wide else D
        arrays.append(x.reshape(-1, 128))
        shapes.append((x.shape[0] // cols, cols))
    arrays.append(norms.reshape(1, -1))
    shapes.append((1, -(-norms.shape[0] // 128) * 128))
    return arrays, tuple(shapes)


def body(
    sizes, target, memory, cotangent, target_lengths, source_lengths,
    inward_master, inward_mean, inward_square, outward_master, outward_mean, outward_square,
    expand_master, expand_mean, expand_square, shrink_master, shrink_mean, shrink_square,
    norms_master, norms_mean, norms_square,
):
    flat, shapes = shard_views(inward_master, outward_master, expand_master, shrink_master, norms_master)
    norm_count = norms_master.shape[0]
    means, _ = shard_views(inward_mean, outward_mean, expand_mean, shrink_mean, norms_mean)
    squares, _ = shard_views(inward_square, outward_square, expand_square, shrink_square, norms_square)
    x, mem, cot = target[0], memory[0], cotangent[0]
    if sizes[1:] == (2, 2, 2) and norm_count == 96 and all(s[0] % 16 == 0 for s in shapes[:4]):
        *kept, trow, tcol, scol, win, wout, up, down, norms, table = front_remote(
            sizes, shapes, target_lengths, source_lengths, x, mem, flat)
        win, wout = win.reshape(6 * D, D), wout.reshape(2 * D, D)
        q1, k1, v1, c1, lse1, xh1, rs1, q2, k2, v2 = kept
        result, dk2, dv2, dh1, gin, gout, gup, gdown, rest = middle(
            target_lengths, table, mem, cot, q2, k2, v2, xh1, win, wout, up.reshape(D, FF), down.reshape(FF, D), norms,
            trow, scol)
        tgrad, mgrad, *sums = back_remote(
            sizes, shapes, norms, rest, [x, q1, k1, v1, c1, lse1, xh1, rs1, dh1, win, wout, dk2, dv2], [trow, tcol],
            [gin, gout, gup, gdown])
    else:
        padding = ((0, 0), (0, shapes[4][1] - norm_count))
        win, wout, up, down, norms = gather_all(
            sizes, [*flat[:4], jnp.pad(flat[4], padding)], shapes, [BF, BF, BF, BF, F32])
        norms = norms.reshape(-1, norms.shape[-1])[:, :norm_count].reshape(6, D)
        result, tgrad, mgrad, gin, gout, gup, gdown, gnorm = layer(
            target_lengths, source_lengths, x, mem, cot,
            win.reshape(6 * D, D), wout.reshape(2 * D, D), up.reshape(D, FF), down.reshape(FF, D), norms,
        )
        gnorm = jnp.pad(gnorm.reshape(-1, norm_count), padding)
        grads = [g.reshape(*sizes, *s) for g, s in zip((gin, gout, gup, gdown, gnorm), shapes)]
        sums = reduce_all(sizes, grads, shapes)
    tgrad, mgrad, *outs = adam_all([tgrad, mgrad], sums, means, squares, (*shapes[:4], (1, norm_count)))
    return (result[None], tgrad[None], mgrad[None], *[x.reshape(-1) for x in outs])


def solution(mesh):
    rows, cols = mesh.shape["dp"], mesh.shape["shard"]
    both = ("dp", "shard")
    row, flat = P(both, None, None), P(both)
    return jax.shard_map(
        functools.partial(body, (rows // 2, 2, cols // 2, 2)),
        mesh=mesh,
        in_specs=(row, row, row, P(both, None), P(both, None), *[flat] * 15),
        out_specs=(row, row, row, *[flat] * 15),
        check_vma=False,
    )
```
